32 devices in a mesh: row: 8 (over z, y), col: 2 (over x), fiber: 2 (over core).
Axes of the slice: x: 2, y: 2, z: 4, core: 2. Of those that a mesh axis runs over, the one named last changes fastest.
Arguments:
- a_panels: float32 [3072, 2, 2, 768], P(('row', 'col'), 'fiber'), may hold values from -12 to 12
- b_panels: float32 [2, 2, 768, 2048], P('fiber', None, 'row', 'col'), may hold values from -0.15625 to 0.15625
- a_pattern: int32 [24, 2, 2, 6], P('row', 'fiber'), may hold values 0 or 1
- c_pattern: int32 [24, 16], P('row', 'col'), may hold values 0 or 1
Outputs:
- scaled: float32 [3072, 2048], P(('row', 'fiber'), 'col')
The draws below stay inside these ranges and needn't reach their ends.
All inputs are finite; a program needn't handle non-finite values. No bound on the sum of `a_pattern` or of `c_pattern` on one device may be relied on, other than what follows from the above.
Results may differ from the reference program's by a relative error of at most 0.00013.
Values sent between devices are 32-bit elements; how exact they have to be, the bound alone decides.
No kernel may reach another device: no remote copies, remote signals or barrier semaphores. Data moves between devices by JAX's collectives and lax.ppermute only.
A program may use at most 64 MiB of HBM per device.

```python
import jax
import jax.numpy as jnp
from jax import lax

BLK = 128
RB = 3
CB = 8
WB = 6
SECTIONS = 2
LAYERS = 2
ROWS = 3072
WIDTH = 768
COLS = 2048
N_ROW = 8
N_COL = 2


def draw_a_panels(key, part):
    first_key = jax.random.fold_in(key, 11)
    second_key = jax.random.fold_in(key, 23)
    shape_full = (ROWS, LAYERS, SECTIONS, WIDTH)
    row_index = jnp.arange(ROWS).astype(jnp.float32)
    rising = 1.0 + 2.0 * row_index / max(ROWS - 1, 1)
    values = jax.random.truncated_normal(first_key, -2.5, 2.5, shape_full, jnp.float32)
    jitter = jnp.exp(jax.random.uniform(second_key, (ROWS,), jnp.float32, -0.35, 0.35))
    return values * (rising * jitter)[:, None, None, None]


def plant(array, rng, smallest, high):
    longest = array.shape.index(max(array.shape))
    spots = []
    for shift in (0, 1):
        where = [jax.random.randint(jax.random.fold_in(rng, axis), (), 0, length) for axis, length in enumerate(array.shape)]
        where[longest] = (where[longest] + shift) % array.shape[longest]
        spots.append(tuple(where))
    return array.at[spots[0]].set(smallest).at[spots[1]].set(high)


def levels(stream_key, dims, cuts, low, top_value):
    level, own = 1.0, jax.random.fold_in(stream_key, 6)
    for position, blocks in cuts:
        steps = jnp.exp(jax.random.uniform(jax.random.fold_in(own, position), (blocks,), jnp.float32, low / len(cuts), top_value / len(cuts)))
        level = level * jnp.repeat(steps, dims[position] // blocks).reshape([-1 if axis == position else 1 for axis in range(len(dims))])
    return level


def scatter_about(stream_key, extent, deviation, most, cuts=(), held_as=jnp.bfloat16):
    array = deviation * jax.random.normal(stream_key, extent, jnp.float32)
    if cuts:
        array = array * levels(stream_key, extent, cuts, -0.22, 0.18)
    return jnp.clip(array, -most, most).astype(held_as)


def setup_inputs(seed: int = 0) -> dict:
    seeds = jax.random.split(jax.random.key(seed), 5)
    a_panels = draw_a_panels(jax.random.fold_in(seeds[4], 71), 0)
    b_panels = scatter_about(seeds[1], (LAYERS, SECTIONS, WIDTH, COLS), (LAYERS * SECTIONS * WIDTH // 2) ** -0.5, 0.15625, ((0, 2), (2, 8), (3, 2)), jnp.float32)
    a_pattern = plant((jax.random.randint(seeds[2], (RB * N_ROW, LAYERS, SECTIONS, WB), 0, 2) < 1).astype(jnp.int32), jax.random.fold_in(seeds[2], 1), 0, 1)
    c_pattern = plant((jax.random.randint(seeds[3], (RB * N_ROW, CB * N_COL), 0, 4) < 3).astype(jnp.int32), jax.random.fold_in(seeds[3], 1), 0, 1)
    return {"a_panels": a_panels, "b_panels": b_panels, "a_pattern": a_pattern, "c_pattern": c_pattern}


EPS = 1e-6


def reference(a_panels, b_panels, a_pattern, c_pattern):
    row_total, layer_count, section_count, panel_width = a_panels.shape
    block_size = BLK
    column_total = b_panels.shape[3]
    keep_left = a_pattern.astype(jnp.float32)
    blocked = a_panels.reshape(row_total // block_size, block_size, layer_count, section_count, panel_width // block_size, block_size)
    blocked = blocked * keep_left[:, None, :, :, :, None]
    left_matrix = blocked.reshape(row_total, layer_count * section_count * panel_width)
    right_matrix = b_panels.reshape(layer_count * section_count * panel_width, column_total)
    product = jnp.dot(left_matrix, right_matrix, precision=lax.Precision.HIGHEST, preferred_element_type=jnp.float32)
    keep_product = c_pattern.astype(jnp.float32)
    keep_full = jnp.broadcast_to(keep_product[:, None, :, None], (keep_product.shape[0], block_size, keep_product.shape[1], block_size))
    product = product * keep_full.reshape(row_total, column_total)
    inflated = product * product
    colmean = jnp.sum(inflated, axis=0) / row_total
    return inflated / (colmean + EPS)
```

```python
import jax
import jax.numpy as jnp
from jax import lax
from jax.sharding import PartitionSpec as P

BLK = 128


EPS = 1e-06
PRECISION = lax.Precision.HIGH
HALVES = 2
LONGEST_RING = 16


def ring_order(size):
    return list(range(0, size, 2)) + list(range(size - 1 - size % 2, 0, -2))


def shifted(order, step):
    size = len(order)
    return [(order[i], order[(i + step) % size]) for i in range(size)]


def all_sum(value, axis_name):
    size = lax.axis_size(axis_name)
    stride = 1
    while stride < size:
        rest = size // stride
        radix = next(p for p in range(2, rest + 1) if rest % p == 0)
        total = value
        for turn in range(1, radix):
            pairs = []
            for i in range(size):
                digit = i // stride % radix
                pairs.append((i, i + ((digit + turn) % radix - digit) * stride))
            total = total + lax.ppermute(value, axis_name, pairs)
        value = total
        stride *= radix
    return value


def gathered(a_panels, b_panels, a_pattern, c_pattern):
    rows, _, sections, width = a_panels.shape
    block_rows, width_blocks = a_pattern.shape[0], a_pattern.shape[3]
    columns = b_panels.shape[3]
    local_rows = block_rows * BLK
    n_row, fibers = lax.axis_size("row"), lax.axis_size("fiber")
    share = local_rows // fibers
    total = jnp.zeros((local_rows, columns), jnp.float32)
    for section in range(sections):
        block = lax.all_gather(a_panels[:, 0, section, :], "col", axis=0, tiled=True)
        keep = a_pattern[:, 0, section, :].astype(jnp.float32)
        left = block.reshape(block_rows, BLK, width_blocks, BLK) * keep[:, None, :, None]
        right = lax.all_gather(b_panels[0, section], "row", axis=0, tiled=True)
        total = total + jnp.dot(
            left.reshape(local_rows, width),
            right,
            precision=PRECISION,
            preferred_element_type=jnp.float32,
        )
    keep = jnp.broadcast_to(
        c_pattern.astype(jnp.float32)[:, None, :, None],
        (block_rows, BLK, columns // BLK, BLK),
    ).reshape(local_rows, columns)
    merged = lax.psum_scatter(total, "fiber", scatter_dimension=0, tiled=True)
    product = merged * lax.dynamic_slice_in_dim(keep, lax.axis_index("fiber") * share, share, 0)
    inflated = product * product
    sums = all_sum(all_sum(jnp.sum(inflated, axis=0, keepdims=True), "fiber"), "row")
    return inflated / (sums / (share * fibers * n_row) + EPS)


def local(a_panels, b_panels, a_pattern, c_pattern):
    rows, _, sections, width = a_panels.shape
    block_rows = a_pattern.shape[0]
    blocks = sections * a_pattern.shape[3]
    depth, columns = b_panels.shape[2:]
    n_row, n_col, fibers = (lax.axis_size(name) for name in ("row", "col", "fiber"))
    my_row, my_col, my_fiber = (lax.axis_index(name) for name in ("row", "col", "fiber"))
    local_rows = rows * n_col
    inner = sections * depth
    half = columns // HALVES

    order = ring_order(n_row)
    place = jnp.asarray([order.index(r) for r in range(n_row)], jnp.int32)
    owners = jnp.asarray(order, jnp.int32)
    forward, backward = shifted(order, 1), shifted(order, -1)
    my_place = place[my_row]

    if n_row > LONGEST_RING:
        return gathered(a_panels, b_panels, a_pattern, c_pattern)

    own = [b_panels[0, :, :, h * half : (h + 1) * half].reshape(inner, half) for h in range(HALVES)]
    shards = {(0, h): own[h] for h in range(HALVES)}
    up, down = list(own), list(own)
    far = n_row // 2
    for step in range(1, far):
        for h in range(HALVES):
            up[h] = lax.ppermute(up[h], "row", forward)
            down[h] = lax.ppermute(down[h], "row", backward)
            shards[-step, h] = up[h]
            shards[step, h] = down[h]
    middle = inner // 2
    for h in range(HALVES):
        top = lax.ppermute(up[h][:middle], "row", forward)
        bottom = lax.ppermute(down[h][middle:], "row", backward)
        shards[far, h] = jnp.concatenate([top, bottom], axis=0)

    mine = a_panels.reshape(rows, sections * width)
    left = jnp.zeros((local_rows, sections * width), jnp.float32)
    left = lax.dynamic_update_slice(left, mine, (my_col * rows, 0))
    for step in range(1, n_col):
        piece = lax.ppermute(mine, "col", [(i, (i + step) % n_col) for i in range(n_col)])
        left = lax.dynamic_update_slice(left, piece, ((my_col - step) % n_col * rows, 0))
    keep_left = a_pattern.astype(jnp.float32).reshape(block_rows, 1, blocks, 1)
    left = left.reshape(block_rows, BLK, blocks, BLK) * keep_left
    left = left.reshape(local_rows, sections, n_row, depth).transpose(2, 0, 1, 3)
    left = left.reshape(n_row, local_rows, inner)

    share = local_rows // fibers
    keep_product = lax.dynamic_slice_in_dim(
        jnp.broadcast_to(
            c_pattern.astype(jnp.float32)[:, None, :, None],
            (block_rows, BLK, columns // BLK, BLK),
        ).reshape(local_rows, columns),
        my_fiber * share,
        share,
        0,
    )

    inflated, totals = [], []
    for h in range(HALVES):
        total = jnp.zeros((local_rows, half), jnp.float32)
        for step in sorted(range(1 - far, far + 1), key=abs):
            owner = owners[(my_place + step) % n_row]
            total = total + jnp.dot(
                lax.dynamic_index_in_dim(left, owner, 0, keepdims=False),
                shards[step, h],
                precision=PRECISION,
                preferred_element_type=jnp.float32,
            )
        kept = lax.dynamic_slice_in_dim(total, my_fiber * share, share, 0)
        for step in range(1, fibers):
            target = (my_fiber + step) % fibers
            sent = lax.dynamic_slice_in_dim(total, target * share, share, 0)
            kept = kept + lax.ppermute(sent, "fiber", [(i, (i + step) % fibers) for i in range(fibers)])
        product = kept * keep_product[:, h * half : (h + 1) * half]
        square = product * product
        inflated.append(square)
        totals.append(jnp.sum(square, axis=0, keepdims=True))
    sums = jnp.concatenate(totals, axis=1)
    sums = all_sum(all_sum(sums, "fiber"), "row")
    return jnp.concatenate(inflated, axis=1) / (sums / (share * fibers * n_row) + EPS)


def solution(mesh):
    placed = (
        P(("row", "col"), "fiber", None, None),
        P("fiber", None, "row", "col"),
        P("row", "fiber", None, None),
        P("row", "col"),
    )
    return jax.shard_map(
        local, mesh=mesh, in_specs=placed, out_specs=P(("row", "fiber"), "col"), check_vma=False
    )
```

```python
import jax
import jax.numpy as jnp
from jax import lax
from jax.experimental import pallas as pl
from jax.experimental.pallas import tpu as pltpu
from jax.sharding import PartitionSpec as P

BLK = 128


EPS = 1e-06
LONGEST_RING = 8
TILE = 256


def ring_order(size):
    return list(range(0, size, 2)) + list(range(size - 1, 0, -2))


def owner_at(size, row, step):
    place = jnp.where(row % 2 == 0, row // 2, size - 1 - row // 2)
    place = (place + step + size) % size
    return jnp.where(place < size // 2, 2 * place, 2 * (size - 1 - place) + 1)


def shifted(order, step):
    size = len(order)
    return [(order[i], order[(i + step) % size]) for i in range(size)]


def all_sum(value, axis_name):
    size = lax.axis_size(axis_name)
    stride = 1
    while stride < size:
        rest = size // stride
        radix = next(p for p in range(2, rest + 1) if rest % p == 0)
        total = value
        for turn in range(1, radix):
            pairs = []
            for i in range(size):
                digit = i // stride % radix
                pairs.append((i, i + ((digit + turn) % radix - digit) * stride))
            total = total + lax.ppermute(value, axis_name, pairs)
        value = total
        stride *= radix
    return value


def gathered(a_panels, b_panels, a_pattern, c_pattern):
    rows, _, sections, width = a_panels.shape
    block_rows, width_blocks = a_pattern.shape[0], a_pattern.shape[3]
    columns = b_panels.shape[3]
    local_rows = block_rows * BLK
    n_row, fibers = lax.axis_size("row"), lax.axis_size("fiber")
    share = local_rows // fibers
    total = jnp.zeros((local_rows, columns), jnp.float32)
    for section in range(sections):
        block = lax.all_gather(a_panels[:, 0, section, :], "col", axis=0, tiled=True)
        keep = a_pattern[:, 0, section, :].astype(jnp.float32)
        left = block.reshape(block_rows, BLK, width_blocks, BLK) * keep[:, None, :, None]
        right = lax.all_gather(b_panels[0, section], "row", axis=0, tiled=True)
        total = total + jnp.dot(
            left.reshape(local_rows, width),
            right,
            precision=lax.Precision.HIGH,
            preferred_element_type=jnp.float32,
        )
    keep = jnp.broadcast_to(
        c_pattern.astype(jnp.float32)[:, None, :, None],
        (block_rows, BLK, columns // BLK, BLK),
    ).reshape(local_rows, columns)
    merged = lax.psum_scatter(total, "fiber", scatter_dimension=0, tiled=True)
    product = merged * lax.dynamic_slice_in_dim(keep, lax.axis_index("fiber") * share, share, 0)
    inflated = product * product
    sums = all_sum(all_sum(jnp.sum(inflated, axis=0, keepdims=True), "fiber"), "row")
    return inflated / (sums / (share * fibers * n_row) + EPS)


def split(value):
    high = value.astype(jnp.bfloat16)
    low = (value - high.astype(jnp.float32)).astype(jnp.bfloat16)
    return high, low


def product3(a_high, a_low, b_high, b_low):
    def dot(x, y):
        return jnp.dot(x, y, preferred_element_type=jnp.float32)

    return dot(a_high, b_high) + (dot(a_high, b_low) + dot(a_low, b_high))


def left_kernel(pattern, own, peer, high, low, far_high, far_low):
    rows, _, sections, width = own.shape
    n_row = lax.axis_size("row")
    depth = width // n_row
    far = owner_at(n_row, lax.axis_index("row"), n_row // 2)
    col = lax.axis_index("col")
    group = 64
    for source, position in ((own, col), (peer, 1 - col)):
        for s in range(sections):
            for g in range(rows // group):
                start = pl.multiple_of(position * rows + g * group, group)
                block_row = start // BLK
                kept = []
                for w in range(width // BLK):
                    keep = pattern[(block_row * sections + s) * (width // BLK) + w]
                    piece = source[pl.ds(g * group, group), 0, s, pl.ds(w * BLK, BLK)]
                    kept.append(jnp.where(keep != 0, piece, 0.0))
                h, l = split(jnp.concatenate(kept, axis=1))
                high[s, pl.ds(start, group), :] = h
                low[s, pl.ds(start, group), :] = l
    for r in range(n_row):

        @pl.when(far == r)
        def _():
            for s in range(sections):
                far_high[s] = high[s, :, r * depth : (r + 1) * depth]
                far_low[s] = low[s, :, r * depth : (r + 1) * depth]


def near_kernel(*refs):
    high, low, *shards, out, b_high, b_low = refs
    n_row = lax.axis_size("row")
    row = lax.axis_index("row")
    sections = high.shape[0]
    depth, columns = shards[0].shape[-2:]
    steps = range(1 - n_row // 2, n_row // 2)

    def put(s, step, value):
        start = pl.multiple_of(owner_at(n_row, row, step) * depth, depth)
        h, l = split(value)
        b_high[s, pl.ds(start, depth), :] = h
        b_low[s, pl.ds(start, depth), :] = l

    shards = iter(shards)
    for step in steps:
        for s in range(sections):
            shard = next(shards)
            put(s, step, shard[...])
    for s in range(sections):
        put(s, n_row // 2, jnp.zeros((depth, columns), jnp.float32))
    for t in range(columns // TILE):
        tile = pl.ds(t * TILE, TILE)
        total = product3(high[0], low[0], b_high[0, :, tile], b_low[0, :, tile])
        for s in range(1, sections):
            total += product3(high[s], low[s], b_high[s, :, tile], b_low[s, :, tile])
        out[:, tile] = total


def far_kernel(high, low, near, *refs):
    *shards, kept, sent = refs
    sections = high.shape[0]
    columns = near.shape[1]
    share = near.shape[0] // 2
    fiber = lax.axis_index("fiber")
    for t in range(columns // TILE):
        tile = pl.ds(t * TILE, TILE)
        parts = [split(shard[:, tile]) for shard in shards]
        for out, which in ((sent, 1 - fiber), (kept, fiber)):
            block = pl.ds(pl.multiple_of(which * share, share), share)
            total = near[block, tile]
            for s in range(sections):
                total += product3(high[s, block, :], low[s, block, :], *parts[s])
            out[:, tile] = total


def square_kernel(pattern, kept, received, squares, sums):
    share, columns = kept.shape
    fiber = lax.axis_index("fiber")
    group = 64
    blocks = columns // BLK
    for w in range(blocks):
        tile = pl.ds(w * BLK, BLK)
        total = jnp.zeros((8, BLK), jnp.float32)
        for g in range(share // group):
            block_row = (fiber * share + g * group) // BLK
            keep = pattern[block_row * blocks + w]
            part = pl.ds(g * group, group)
            value = kept[part, tile] + received[part, tile]
            value = jnp.where(keep != 0, value, 0.0)
            value = value * value
            squares[part, tile] = value
            total += jnp.sum(value.reshape(group // 8, 8, BLK), axis=0)
        sums[:, tile] = jnp.sum(total, axis=0, keepdims=True)


VMEM = pl.BlockSpec(memory_space=pltpu.VMEM)
SMEM = pl.BlockSpec(memory_space=pltpu.SMEM)


def call(kernel, out_shapes, specs, scratch=(), flops=0, name=None):
    def run(*args):
        moved = sum(a.size * a.dtype.itemsize for a in (*args, *out_shapes))
        return pl.pallas_call(
            kernel,
            name=name,
            out_shape=out_shapes,
            in_specs=specs,
            out_specs=[VMEM] * len(out_shapes),
            scratch_shapes=scratch,
            cost_estimate=pl.CostEstimate(flops=flops, bytes_accessed=moved, transcendentals=0),
            compiler_params=pltpu.CompilerParams(vmem_limit_bytes=60 * 2**20),
        )(*args)

    return run


def local(a_panels, b_panels, a_pattern, c_pattern):
    rows, _, sections, width = a_panels.shape
    block_rows = a_pattern.shape[0]
    depth, columns = b_panels.shape[2:]
    n_row, n_col, fibers = (lax.axis_size(name) for name in ("row", "col", "fiber"))
    local_rows = rows * n_col
    share = local_rows // fibers
    if n_row > LONGEST_RING or n_row % 2 or (n_col, fibers, sections) != (2, 2, 2):
        return gathered(a_panels, b_panels, a_pattern, c_pattern)

    order = ring_order(n_row)
    forward, backward = shifted(order, 1), shifted(order, -1)
    far = n_row // 2

    own = [b_panels[0, s] for s in range(sections)]
    shards = {(0, s): own[s] for s in range(sections)}
    up, down = list(own), list(own)
    for step in range(1, far):
        for s in range(sections):
            up[s] = shards[-step, s] = lax.ppermute(up[s], "row", forward)
            down[s] = shards[step, s] = lax.ppermute(down[s], "row", backward)
    last = [
        lax.ppermute(up[0], "row", forward),
        lax.ppermute(down[1], "row", backward),
    ]

    peer = lax.ppermute(a_panels, "col", [(0, 1), (1, 0)])
    half = jax.ShapeDtypeStruct((sections, local_rows, width), jnp.bfloat16)
    narrow = jax.ShapeDtypeStruct((sections, local_rows, depth), jnp.bfloat16)
    high, low, far_high, far_low = call(
        left_kernel, [half, half, narrow, narrow], [SMEM, VMEM, VMEM], name="left"
    )(a_pattern.reshape(-1), a_panels, peer)

    near_shards = [shards[step, s] for step in range(1 - far, far) for s in range(sections)]
    right = pltpu.VMEM((sections, width, columns), jnp.bfloat16)
    (near,) = call(
        near_kernel,
        [jax.ShapeDtypeStruct((local_rows, columns), jnp.float32)],
        [VMEM] * (2 + len(near_shards)),
        [right, right],
        6 * local_rows * columns * width * sections,
        name="near",
    )(high, low, *near_shards)
    part = jax.ShapeDtypeStruct((share, columns), jnp.float32)
    kept, sent = call(
        far_kernel,
        [part, part],
        [VMEM] * 5,
        flops=6 * local_rows * columns * depth * sections,
        name="far",
    )(far_high, far_low, near, *last)
    received = lax.ppermute(sent, "fiber", [(0, 1), (1, 0)])
    squares, sums = call(
        square_kernel,
        [part, jax.ShapeDtypeStruct((1, columns), jnp.float32)],
        [SMEM, VMEM, VMEM],
        name="square",
    )(c_pattern.reshape(-1), kept, received)
    sums = all_sum(all_sum(sums, "fiber"), "row")
    return squares / (sums / (share * fibers * n_row) + EPS)


def solution(mesh):
    placed = (
        P(("row", "col"), "fiber", None, None),
        P("fiber", None, "row", "col"),
        P("row", "fiber", None, None),
        P("row", "col"),
    )
    return jax.shard_map(
        local, mesh=mesh, in_specs=placed, out_specs=P(("row", "fiber"), "col"), check_vma=False
    )
```

```python
import functools

import jax
import jax.numpy as jnp
from jax import lax
from jax.experimental import pallas as pl
from jax.experimental.pallas import tpu as pltpu
from jax.sharding import PartitionSpec as P

BLK = 128


EPS = 1e-06
TILE = 256


def ring_order(size):
    return list(range(0, size, 2)) + list(range(size - 1, 0, -2))


def owner_at(size, row, step):
    place = jnp.where(row % 2 == 0, row // 2, size - 1 - row // 2)
    place = (place + step + size) % size
    return jnp.where(place < size // 2, 2 * place, 2 * (size - 1 - place) + 1)


def shifted(order, step):
    size = len(order)
    return [(order[i], order[(i + step) % size]) for i in range(size)]


def all_sum(value, axis_name):
    size = lax.axis_size(axis_name)
    stride = 1
    while stride < size:
        rest = size // stride
        radix = next(p for p in range(2, rest + 1) if rest % p == 0)
        total = value
        for turn in range(1, radix):
            pairs = []
            for i in range(size):
                digit = i // stride % radix
                pairs.append((i, i + ((digit + turn) % radix - digit) * stride))
            total = total + lax.ppermute(value, axis_name, pairs)
        value = total
        stride *= radix
    return value


def gathered(a_panels, b_panels, a_pattern, c_pattern):
    rows, _, sections, width = a_panels.shape
    block_rows, width_blocks = a_pattern.shape[0], a_pattern.shape[3]
    columns = b_panels.shape[3]
    local_rows = block_rows * BLK
    n_row, fibers = lax.axis_size("row"), lax.axis_size("fiber")
    share = local_rows // fibers
    total = jnp.zeros((local_rows, columns), jnp.float32)
    for section in range(sections):
        block = lax.all_gather(a_panels[:, 0, section, :], "col", axis=0, tiled=True)
        keep = a_pattern[:, 0, section, :].astype(jnp.float32)
        left = block.reshape(block_rows, BLK, width_blocks, BLK) * keep[:, None, :, None]
        right = lax.all_gather(b_panels[0, section], "row", axis=0, tiled=True)
        total = total + jnp.dot(
            left.reshape(local_rows, width),
            right,
            precision=lax.Precision.HIGH,
            preferred_element_type=jnp.float32,
        )
    keep = jnp.broadcast_to(
        c_pattern.astype(jnp.float32)[:, None, :, None],
        (block_rows, BLK, columns // BLK, BLK),
    ).reshape(local_rows, columns)
    merged = lax.psum_scatter(total, "fiber", scatter_dimension=0, tiled=True)
    product = merged * lax.dynamic_slice_in_dim(keep, lax.axis_index("fiber") * share, share, 0)
    inflated = product * product
    sums = all_sum(all_sum(jnp.sum(inflated, axis=0, keepdims=True), "fiber"), "row")
    return inflated / (sums / (share * fibers * n_row) + EPS)


def split(value):
    high = value.astype(jnp.bfloat16)
    low = (value - high.astype(jnp.float32)).astype(jnp.bfloat16)
    return high, low


def product3(a_high, a_low, b_high, b_low):
    def dot(x, y):
        return jnp.dot(x, y, preferred_element_type=jnp.float32)

    return dot(a_high, b_high) + (dot(a_high, b_low) + dot(a_low, b_high))


def left_kernel(groups, is_peer, pattern, source, *refs):
    *outs, turned = refs
    rows, _, sections, width = source.shape
    n_row, row = lax.axis_size("row"), lax.axis_index("row")
    depth = width // n_row
    col = lax.axis_index("col")
    position = 1 - col if is_peer else col
    group = 64
    for g in range(rows // group):
        part = pl.ds(g * group, group)
        block_row = (position * rows + g * group) // BLK
        for s in range(sections):
            kept = []
            for w in range(width // BLK):
                keep = pattern[block_row, 0, s, w]
                piece = source[part, 0, s, pl.ds(w * BLK, BLK)]
                kept.append(jnp.where(keep != 0, piece, 0.0))
            value = jnp.concatenate(kept, axis=1)
            for r in range(n_row):
                turned[r, s, part, :] = value[:, r * depth : (r + 1) * depth]
        for i, members in enumerate(groups):
            pieces = [turned[owner_at(n_row, row, step), s, part, :] for step, s in members]
            high, low = split(jnp.concatenate(pieces, axis=1))
            outs[2 * i][part, :] = high
            outs[2 * i + 1][part, :] = low


def group_kernel(count, *refs):
    own_high, own_low, peer_high, peer_low, *rest = refs
    shards, (*near, out, b_high, b_low) = rest[:count], rest[count:]
    depth, columns = shards[0].shape
    rows = own_high.shape[0]
    for i, shard in enumerate(shards):
        part = pl.ds(i * depth, depth)
        b_high[part, :], b_low[part, :] = split(shard[...])
    high = jnp.concatenate([own_high[...], peer_high[...]], axis=0)
    low = jnp.concatenate([own_low[...], peer_low[...]], axis=0)
    for t in range(columns // TILE):
        tile = pl.ds(t * TILE, TILE)
        total = product3(high, low, b_high[:, tile], b_low[:, tile])
        for k in range(2):
            value = total[k * rows : (k + 1) * rows]
            out[k, :, tile] = near[0][k, :, tile] + value if near else value


def far_kernel(is_kept, count, *refs):
    own_high, own_low, peer_high, peer_low, *rest = refs
    shards, (near, out, b_high, b_low) = rest[:count], rest[count:]
    depth, columns = shards[0].shape
    peers = lax.axis_index("col") != lax.axis_index("fiber")
    if not is_kept:
        peers = jnp.logical_not(peers)
    for i, shard in enumerate(shards):
        part = pl.ds(i * depth, depth)
        b_high[part, :], b_low[part, :] = split(shard[...])
    for k, (high, low) in enumerate(((own_high, own_low), (peer_high, peer_low))):

        @pl.when(peers == (k == 1))
        def _():
            for t in range(columns // TILE):
                tile = pl.ds(t * TILE, TILE)
                value = product3(high[...], low[...], b_high[:, tile], b_low[:, tile])
                out[:, tile] = near[k, :, tile] + value


def square_kernel(pattern, kept, received, squares, sums):
    share, columns = kept.shape
    fiber = lax.axis_index("fiber")
    group = 64
    for w in range(columns // BLK):
        tile = pl.ds(w * BLK, BLK)
        total = jnp.zeros((8, BLK), jnp.float32)
        for g in range(share // group):
            keep = pattern[(fiber * share + g * group) // BLK, w]
            part = pl.ds(g * group, group)
            value = kept[part, tile] + received[part, tile]
            value = jnp.where(keep != 0, value, 0.0)
            value = value * value
            squares[part, tile] = value
            total += jnp.sum(value.reshape(group // 8, 8, BLK), axis=0)
        sums[:, tile] = jnp.sum(total, axis=0, keepdims=True)


VMEM = pl.BlockSpec(memory_space=pltpu.VMEM)
SMEM = pl.BlockSpec(memory_space=pltpu.SMEM)


def call(kernel, out_shapes, specs, scratch=(), flops=0, name=None):
    def run(*args):
        moved = sum(a.size * a.dtype.itemsize for a in (*args, *out_shapes))
        return pl.pallas_call(
            kernel,
            name=name,
            out_shape=out_shapes,
            in_specs=specs,
            out_specs=[VMEM] * len(out_shapes),
            scratch_shapes=scratch,
            cost_estimate=pl.CostEstimate(flops=flops, bytes_accessed=moved, transcendentals=0),
            compiler_params=pltpu.CompilerParams(vmem_limit_bytes=16 * 2**20),
        )(*args)

    return run


def local(a_panels, b_panels, a_pattern, c_pattern):
    rows, _, sections, width = a_panels.shape
    block_rows = a_pattern.shape[0]
    depth, columns = b_panels.shape[2:]
    n_row, n_col, fibers = (lax.axis_size(name) for name in ("row", "col", "fiber"))
    local_rows = rows * n_col
    share = local_rows // fibers
    if (n_row, n_col, fibers, sections) != (8, 2, 2, 2):
        return gathered(a_panels, b_panels, a_pattern, c_pattern)

    order = ring_order(n_row)
    forward, backward = shifted(order, 1), shifted(order, -1)
    far = n_row // 2
    groups = [
        [(0, 0), (0, 1), (-1, 0), (1, 1), (-1, 1), (1, 0)],
        [(-2, 0), (2, 1), (-2, 1), (2, 0), (-3, 0), (3, 1)],
        [(-3, 1), (3, 0)],
        [(far, 0), (far, 1)],
    ]
    parts = []
    for members in groups:
        parts += [jax.ShapeDtypeStruct((rows, len(members) * depth), jnp.bfloat16)] * 2

    def left(source, is_peer):
        return call(
            functools.partial(left_kernel, groups, is_peer),
            parts,
            [SMEM, VMEM],
            [pltpu.VMEM((n_row, sections, rows, depth), jnp.float32)],
            name="peer_left" if is_peer else "own_left",
        )(a_pattern, source)

    def multiply(g, *near):
        members = groups[g]
        factor = pltpu.VMEM((len(members) * depth, columns), jnp.bfloat16)
        operands = [*lefts[0][2 * g : 2 * g + 2], *lefts[1][2 * g : 2 * g + 2]]
        operands += [shards[m] for m in members]
        return operands, members, factor, near

    def near_product(g, *near):
        operands, members, factor, near = multiply(g, *near)
        (total,) = call(
            functools.partial(group_kernel, len(members)),
            [jax.ShapeDtypeStruct((n_col, rows, columns), jnp.float32)],
            [VMEM] * (len(operands) + len(near)),
            [factor, factor],
            6 * local_rows * columns * depth * len(members),
            name=f"group{g}",
        )(*operands, *near)
        return total

    def far_product(is_kept, near):
        operands, members, factor, _ = multiply(far_group)
        (total,) = call(
            functools.partial(far_kernel, is_kept, len(members)),
            [jax.ShapeDtypeStruct((share, columns), jnp.float32)],
            [VMEM] * (len(operands) + 1),
            [factor, factor],
            6 * share * columns * depth * len(members),
            name="kept" if is_kept else "sent",
        )(*operands, near)
        return total

    far_group = len(groups) - 1
    peer_rows = lax.ppermute(a_panels, "col", [(0, 1), (1, 0)])
    own = [b_panels[0, s] for s in range(sections)]
    shards = {(0, s): own[s] for s in range(sections)}

    def hop(step, s):
        if step < 0:
            shards[step, s] = lax.ppermute(shards[step + 1, s], "row", forward)
        else:
            shards[step, s] = lax.ppermute(shards[step - 1, s], "row", backward)

    def after(value, *keys):
        held = lax.optimization_barrier((value, [shards[k] for k in keys]))
        shards.update(zip(keys, held[1], strict=True))
        return held[0]

    first, second = ((-1, 0), (1, 1)), ((-1, 1), (1, 0))
    for sign, s in (*first, *second):
        hop(sign, s)
    lefts = [after(left(a_panels, False), (-1, 0), (1, 1))]
    for sign, s in (*first, *second):
        hop(2 * sign, s)
    for sign, s in first:
        hop(3 * sign, s)
    lefts.append(after(left(peer_rows, True), (-2, 1), (2, 0)))
    for sign, s in second:
        hop(3 * sign, s)
    near = after(near_product(0), (-3, 0), (3, 1))
    shards[far, 0] = lax.ppermute(shards[-3, 0], "row", forward)
    shards[far, 1] = lax.ppermute(shards[3, 1], "row", backward)
    near = near_product(1, near)
    near = near_product(2, near)
    sent = far_product(False, near)
    received = lax.ppermute(sent, "fiber", [(0, 1), (1, 0)])
    kept = far_product(True, near)
    squares, sums = call(
        square_kernel,
        [
            jax.ShapeDtypeStruct((share, columns), jnp.float32),
            jax.ShapeDtypeStruct((1, columns), jnp.float32),
        ],
        [SMEM, VMEM, VMEM],
        name="square",
    )(c_pattern, kept, received)
    sums = all_sum(all_sum(sums, "fiber"), "row")
    return squares / (sums / (share * fibers * n_row) + EPS)


def solution(mesh):
    placed = (
        P(("row", "col"), "fiber", None, None),
        P("fiber", None, "row", "col"),
        P("row", "fiber", None, None),
        P("row", "col"),
    )
    return jax.shard_map(
        local, mesh=mesh, in_specs=placed, out_specs=P(("row", "fiber"), "col"), check_vma=False
    )
```

```python
import functools

import jax
import jax.numpy as jnp
from jax import lax
from jax.experimental import pallas as pl
from jax.experimental.pallas import tpu as pltpu
from jax.sharding import PartitionSpec as P


BLK = 128


EPS = 1e-06
TILE = 256
CHUNK = 256


LINE = (0, 1, 3, 2)


def line_pairs(shift):
    size = len(LINE)
    return [
        (LINE[i] * 2 + y, LINE[(i + shift) % size] * 2 + y) for i in range(size) for y in range(2)
    ]


def line_at(z, step):
    place = jnp.where(z < 2, z, 5 - z)
    place = (place + step + len(LINE)) % len(LINE)
    return jnp.where(place < 2, place, 5 - place)


def all_sum(value, axis_name):
    size = lax.axis_size(axis_name)
    stride = 1
    while stride < size:
        rest = size // stride
        radix = next(p for p in range(2, rest + 1) if rest % p == 0)
        total = value
        for turn in range(1, radix):
            pairs = []
            for i in range(size):
                digit = i // stride % radix
                pairs.append((i, i + ((digit + turn) % radix - digit) * stride))
            total = total + lax.ppermute(value, axis_name, pairs)
        value = total
        stride *= radix
    return value


def gathered(a_panels, b_panels, a_pattern, c_pattern):
    _, _, sections, width = a_panels.shape
    block_rows, width_blocks = a_pattern.shape[0], a_pattern.shape[3]
    columns = b_panels.shape[3]
    local_rows = block_rows * BLK
    n_row, fibers = lax.axis_size("row"), lax.axis_size("fiber")
    share = local_rows // fibers
    total = jnp.zeros((local_rows, columns), jnp.float32)
    for section in range(sections):
        block = lax.all_gather(a_panels[:, 0, section, :], "col", axis=0, tiled=True)
        keep = a_pattern[:, 0, section, :].astype(jnp.float32)
        left = block.reshape(block_rows, BLK, width_blocks, BLK) * keep[:, None, :, None]
        right = lax.all_gather(b_panels[0, section], "row", axis=0, tiled=True)
        total = total + jnp.dot(
            left.reshape(local_rows, width),
            right,
            precision=lax.Precision.HIGH,
            preferred_element_type=jnp.float32,
        )
    keep = jnp.broadcast_to(
        c_pattern.astype(jnp.float32)[:, None, :, None],
        (block_rows, BLK, columns // BLK, BLK),
    ).reshape(local_rows, columns)
    merged = lax.psum_scatter(total, "fiber", scatter_dimension=0, tiled=True)
    product = merged * lax.dynamic_slice_in_dim(keep, lax.axis_index("fiber") * share, share, 0)
    inflated = product * product
    sums = all_sum(all_sum(jnp.sum(inflated, axis=0, keepdims=True), "fiber"), "row")
    return inflated / (sums / (share * fibers * n_row) + EPS)


def split(value):
    high = value.astype(jnp.bfloat16)
    low = (value - high.astype(jnp.float32)).astype(jnp.bfloat16)
    return high, low


def product3(a_high, a_low, b_high, b_low):
    def dot(x, y):
        return jnp.dot(x, y, preferred_element_type=jnp.float32)

    return dot(a_high, b_high) + (dot(a_high, b_low) + dot(a_low, b_high))


def left_kernel(steps, pattern, source, mine, other, turned):
    rows, _, sections, width = source.shape
    n_row, row = lax.axis_size("row"), lax.axis_index("row")
    depth = width // n_row
    group = 64
    for g in range(rows // group):
        part = pl.ds(g * group, group)
        block_row = (lax.axis_index("col") * rows + g * group) // BLK
        for s in range(sections):
            kept = []
            for w in range(width // BLK):
                keep = pattern[block_row, 0, s, w]
                piece = source[part, 0, s, pl.ds(w * BLK, BLK)]
                kept.append(jnp.where(keep != 0, piece, 0.0))
            value = jnp.concatenate(kept, axis=1)
            for r in range(n_row):
                turned[r, s, part, :] = value[:, r * depth : (r + 1) * depth]
        for out, parity in ((mine, row % 2), (other, 1 - row % 2)):
            owners = [line_at(row // 2, step) * 2 + parity for step in steps]
            pieces = [turned[r, s, part, :] for r in owners for s in range(sections)]
            out[part, :] = jnp.concatenate(pieces, axis=1)


def order_kernel(cuts, *refs):
    pieces, outs = refs[:4], refs[4:]
    rows = pieces[0].shape[0]
    flip = lax.axis_index("col") ^ lax.axis_index("fiber")
    for p, piece in enumerate(pieces):
        y, x = divmod(p, 2)
        start = pl.multiple_of((y + 2 * (x ^ flip)) * rows, rows)
        for i, (low_end, high_end) in enumerate(cuts):
            high, low = split(piece[:, low_end:high_end])
            outs[2 * i][pl.ds(start, rows), :] = high
            outs[2 * i + 1][pl.ds(start, rows), :] = low


def group_kernel(count, *refs):
    high, low, *rest = refs
    shards, (*near, out, b_high, b_low) = rest[:count], rest[count:]
    _, sections, depth, columns = shards[0].shape
    for i in range(count * sections):
        part = pl.ds(i * depth, depth)
        b_high[part, :], b_low[part, :] = split(shards[i // sections][0, i % sections])
    for t in range(columns // TILE):
        tile = pl.ds(t * TILE, TILE)
        total = product3(high[...], low[...], b_high[:, tile], b_low[:, tile])
        out[:, tile] = near[0][:, tile] + total if near else total


def far_kernel(first, high, low, near, shard, kept, sent, b_high, b_low):
    _, sections, depth, columns = shard.shape
    rows = kept.shape[1]
    for s in range(sections):
        part = pl.ds(s * depth, depth)
        b_high[part, :], b_low[part, :] = split(shard[0, s])
    value = product3(high[...], low[...], b_high[...], b_low[...])
    for q in range(4):
        out = sent if q >= 2 else kept
        block = pl.ds(q * rows, rows)
        out[q % 2] = near[block, first : first + columns] + value[q * rows : (q + 1) * rows]


def fold_kernel(kept, received, mine, other):
    mine[...] = kept[0] + received[0]
    other[...] = kept[1] + received[1]


def square_kernel(first, pattern, mine, received, *refs):
    *before, squares, sums = refs
    share, columns = mine.shape
    fiber = lax.axis_index("fiber")
    group = 64
    for w in range(columns // BLK):
        tile = pl.ds(w * BLK, BLK)
        total = jnp.zeros((8, BLK), jnp.float32)
        for g in range(share // group):
            keep = pattern[(fiber * share + g * group) // BLK, first // BLK + w]
            part = pl.ds(g * group, group)
            value = mine[part, tile] + received[part, tile]
            value = jnp.where(keep != 0, value, 0.0)
            value = value * value
            squares[part, tile] = value
            total += jnp.sum(value.reshape(group // 8, 8, BLK), axis=0)
        sums[:, pl.ds(first + w * BLK, BLK)] = jnp.sum(total, axis=0, keepdims=True)
    for old in before:
        sums[:, pl.ds(0, first)] = old[...]


def scale_kernel(row_total, sums, *refs):
    *chunks, out = refs
    first = 0
    for chunk in chunks:
        tile = pl.ds(first, chunk.shape[1])
        out[:, tile] = chunk[...] / (sums[:, tile] / row_total + EPS)
        first += chunk.shape[1]


def together(*values):
    return lax.optimization_barrier(values)


VMEM = pl.BlockSpec(memory_space=pltpu.VMEM)
SMEM = pl.BlockSpec(memory_space=pltpu.SMEM)


def call(kernel, out_shapes, specs, scratch=(), flops=0):
    def run(*args):
        moved = sum(a.size * a.dtype.itemsize for a in (*args, *out_shapes))
        return pl.pallas_call(
            kernel,
            out_shape=out_shapes,
            in_specs=specs,
            out_specs=[VMEM] * len(out_shapes),
            scratch_shapes=scratch,
            cost_estimate=pl.CostEstimate(flops=flops, bytes_accessed=moved, transcendentals=0),
            compiler_params=pltpu.CompilerParams(vmem_limit_bytes=16 * 2**20),
        )(*args)

    return run


def local(a_panels, b_panels, a_pattern, c_pattern):
    rows, _, sections, width = a_panels.shape
    depth, columns = b_panels.shape[2:]
    n_row, n_col, fibers = (lax.axis_size(name) for name in ("row", "col", "fiber"))
    local_rows = rows * n_col
    share = local_rows // fibers
    if (n_row, n_col, fibers, sections) != (8, 2, 2, 2):
        return gathered(a_panels, b_panels, a_pattern, c_pattern)

    f32, bf16 = jnp.float32, jnp.bfloat16
    shape = jax.ShapeDtypeStruct
    shard_depth = sections * depth
    half = width * sections // 2
    plane_rows = 4 * rows

    down = lax.ppermute(b_panels, "row", line_pairs(1))
    up = lax.ppermute(b_panels, "row", line_pairs(-1))

    steps = (-1, 1, 0, 2)
    mine, other = call(
        functools.partial(left_kernel, steps),
        [shape((rows, half), f32)] * 2,
        [SMEM, VMEM],
        [pltpu.VMEM((n_row, sections, rows, depth), f32)],
    )(a_pattern, a_panels)
    swap = [(0, 1), (1, 0)]
    swap_y = [(r, r ^ 1) for r in range(n_row)]
    swap_both = [(r * 2 + c, (r ^ 1) * 2 + 1 - c) for r in range(n_row) for c in range(2)]
    from_x = lax.ppermute(mine, "col", swap)
    from_y = lax.ppermute(other, "row", swap_y)
    from_both = lax.ppermute(other, ("row", "col"), swap_both)
    cuts = ((0, 2 * shard_depth), (2 * shard_depth, 3 * shard_depth), (3 * shard_depth, half))
    near_high, near_low, own_high, own_low, far_high, far_low = call(
        functools.partial(order_kernel, cuts),
        [shape((plane_rows, b - a), bf16) for a, b in cuts for _ in range(2)],
        [VMEM] * 4,
    )(mine, from_x, from_y, from_both)

    def product(high, low, *shards_and_near):
        depth_here = high.shape[1]
        factor = pltpu.VMEM((depth_here, columns), bf16)
        (total,) = call(
            functools.partial(group_kernel, depth_here // shard_depth),
            [shape((plane_rows, columns), f32)],
            [VMEM] * (2 + len(shards_and_near)),
            [factor, factor],
            6 * plane_rows * columns * depth_here,
        )(high, low, *shards_and_near)
        return total

    far = [
        lax.ppermute(down[..., j * CHUNK : (j + 1) * CHUNK], "row", line_pairs(1))
        for j in range(columns // CHUNK)
    ]
    near = product(own_high, own_low, b_panels)
    near = product(near_high, near_low, down, up, near)

    ends = []
    for j, shard in enumerate(far):
        if ends:
            shard, _ = together(shard, ends[-1])
        factor = pltpu.VMEM((shard_depth, CHUNK), bf16)
        kept, sent = call(
            functools.partial(far_kernel, j * CHUNK),
            [shape((2, rows, CHUNK), f32)] * 2,
            [VMEM] * 4,
            [factor, factor],
            6 * plane_rows * CHUNK * shard_depth,
        )(far_high, far_low, near, shard)
        received = lax.ppermute(sent, "fiber", swap)
        stays, goes = call(fold_kernel, [shape((rows, CHUNK), f32)] * 2, [VMEM] * 2)(kept, received)
        ends.append(goes)
        far[j] = stays, lax.ppermute(goes, "row", swap_y)
    squares, sums = [], []
    for j, (stays, received) in enumerate(far):
        received, _ = together(received, ends[-1])
        square, total = call(
            functools.partial(square_kernel, j * CHUNK),
            [shape((rows, CHUNK), f32), shape((1, (j + 1) * CHUNK), f32)],
            [SMEM] + [VMEM] * (2 + len(sums)),
        )(c_pattern, stays, received, *sums)
        squares.append(square)
        sums = [total]
    total = all_sum(all_sum(sums[0], "fiber"), "row")
    (out,) = call(
        functools.partial(scale_kernel, share * fibers * n_row),
        [shape((share, columns), f32)],
        [VMEM] * (1 + len(squares)),
    )(total, *squares)
    return out


def solution(mesh):
    placed = (
        P(("row", "col"), "fiber", None, None),
        P("fiber", None, "row", "col"),
        P("row", "fiber", None, None),
        P("row", "col"),
    )

    return jax.shard_map(
        local, mesh=mesh, in_specs=placed, out_specs=P(("row", "fiber"), "col"), check_vma=False
    )
```

```python
import functools

import jax
import jax.numpy as jnp
from jax import lax
from jax.experimental import pallas as pl
from jax.experimental.pallas import tpu as pltpu
from jax.sharding import PartitionSpec as P


BLK = 128


EPS = 1e-06
CHUNKS = (128, 256, 256, 256, 128)


LINE = (0, 1, 3, 2)


def line_pairs(shift):
    size = len(LINE)
    return [
        (LINE[i] * 2 + y, LINE[(i + shift) % size] * 2 + y) for i in range(size) for y in range(2)
    ]


def line_at(z, step):
    place = jnp.where(z < 2, z, 5 - z)
    place = (place + step + len(LINE)) % len(LINE)
    return jnp.where(place < 2, place, 5 - place)


def all_sum(value, axis_name):
    size = lax.axis_size(axis_name)
    stride = 1
    while stride < size:
        rest = size // stride
        radix = next(p for p in range(2, rest + 1) if rest % p == 0)
        total = value
        for turn in range(1, radix):
            pairs = []
            for i in range(size):
                digit = i // stride % radix
                pairs.append((i, i + ((digit + turn) % radix - digit) * stride))
            total = total + lax.ppermute(value, axis_name, pairs)
        value = total
        stride *= radix
    return value


def gathered(a_panels, b_panels, a_pattern, c_pattern):
    _, _, sections, width = a_panels.shape
    block_rows, width_blocks = a_pattern.shape[0], a_pattern.shape[3]
    columns = b_panels.shape[3]
    local_rows = block_rows * BLK
    n_row, fibers = lax.axis_size("row"), lax.axis_size("fiber")
    share = local_rows // fibers
    total = jnp.zeros((local_rows, columns), jnp.float32)
    for section in range(sections):
        block = lax.all_gather(a_panels[:, 0, section, :], "col", axis=0, tiled=True)
        keep = a_pattern[:, 0, section, :].astype(jnp.float32)
        left = block.reshape(block_rows, BLK, width_blocks, BLK) * keep[:, None, :, None]
        right = lax.all_gather(b_panels[0, section], "row", axis=0, tiled=True)
        total = total + jnp.dot(
            left.reshape(local_rows, width),
            right,
            precision=lax.Precision.HIGH,
            preferred_element_type=jnp.float32,
        )
    keep = jnp.broadcast_to(
        c_pattern.astype(jnp.float32)[:, None, :, None],
        (block_rows, BLK, columns // BLK, BLK),
    ).reshape(local_rows, columns)
    merged = lax.psum_scatter(total, "fiber", scatter_dimension=0, tiled=True)
    product = merged * lax.dynamic_slice_in_dim(keep, lax.axis_index("fiber") * share, share, 0)
    inflated = product * product
    sums = all_sum(all_sum(jnp.sum(inflated, axis=0, keepdims=True), "fiber"), "row")
    return inflated / (sums / (share * fibers * n_row) + EPS)


def split(value):
    high = value.astype(jnp.bfloat16)
    low = (value - high.astype(jnp.float32)).astype(jnp.bfloat16)
    return high, low


def product3(a_high, a_low, b_high, b_low):
    def dot(x, y):
        return jnp.dot(x, y, preferred_element_type=jnp.float32)

    return dot(a_high, b_high) + (dot(a_high, b_low) + dot(a_low, b_high))


def left_kernel(steps, rows, pattern, source, mine, other, turned):
    group, _, sections, width = source.shape
    n_row, row = lax.axis_size("row"), lax.axis_index("row")
    depth = width // n_row
    block_row = (lax.axis_index("col") * rows + pl.program_id(0) * group) // BLK
    for s in range(sections):
        kept = []
        for w in range(width // BLK):
            keep = pattern[block_row, 0, s, w]
            kept.append(jnp.where(keep != 0, source[:, 0, s, pl.ds(w * BLK, BLK)], 0.0))
        value = jnp.concatenate(kept, axis=1)
        for r in range(n_row):
            turned[r, s] = value[:, r * depth : (r + 1) * depth]
    for out, parity in ((mine, row % 2), (other, 1 - row % 2)):
        owners = [line_at(row // 2, step) * 2 + parity for step in steps]
        pieces = [turned[r, s] for r in owners for s in range(sections)]
        out[...] = jnp.concatenate(pieces, axis=1)


def order_kernel(cuts, *refs):
    pieces, outs = refs[:4], refs[4:]
    rows = pieces[0].shape[0]
    flip = lax.axis_index("col") ^ lax.axis_index("fiber")
    for p, piece in enumerate(pieces):
        y, x = divmod(p, 2)
        start = pl.multiple_of((y + 2 * (x ^ flip)) * rows, rows)
        for i, (low_end, high_end) in enumerate(cuts):
            high, low = split(piece[:, low_end:high_end])
            outs[2 * i][pl.ds(start, rows), :] = high
            outs[2 * i + 1][pl.ds(start, rows), :] = low


def near_kernel(first, own_high, own_low, high, low, own, down, up, out, b_high, b_low):
    _, sections, depth, _ = own.shape
    tile = slice(first, first + out.shape[1])
    for i, shard in enumerate((down, up, own)):
        for s in range(sections):
            part = pl.ds((i * sections + s) * depth, depth)
            b_high[part, :], b_low[part, :] = split(shard[0, s, :, tile])
    cut = 2 * sections * depth
    total = product3(high[...], low[...], b_high[:cut, :], b_low[:cut, :])
    out[...] = total + product3(own_high[...], own_low[...], b_high[cut:, :], b_low[cut:, :])


def far_kernel(high, low, near, shard, kept, sent, b_high, b_low):
    _, sections, depth, _ = shard.shape
    rows = kept.shape[1]
    for s in range(sections):
        part = pl.ds(s * depth, depth)
        b_high[part, :], b_low[part, :] = split(shard[0, s])
    value = product3(high[...], low[...], b_high[...], b_low[...])
    for q in range(4):
        out = sent if q >= 2 else kept
        block = pl.ds(q * rows, rows)
        out[q % 2] = near[block, :] + value[q * rows : (q + 1) * rows]


def fold_kernel(kept, received, mine, other):
    mine[...] = kept[0] + received[0]
    other[...] = kept[1] + received[1]


def square_kernel(first, pattern, mine, received, *refs):
    *before, squares, sums = refs
    share, columns = mine.shape
    fiber = lax.axis_index("fiber")
    group = 64
    for w in range(columns // BLK):
        tile = pl.ds(w * BLK, BLK)
        total = jnp.zeros((8, BLK), jnp.float32)
        for g in range(share // group):
            keep = pattern[(fiber * share + g * group) // BLK, first // BLK + w]
            part = pl.ds(g * group, group)
            value = mine[part, tile] + received[part, tile]
            value = jnp.where(keep != 0, value, 0.0)
            value = value * value
            squares[part, tile] = value
            total += jnp.sum(value.reshape(group // 8, 8, BLK), axis=0)
        sums[:, pl.ds(first + w * BLK, BLK)] = jnp.sum(total, axis=0, keepdims=True)
    for old in before:
        sums[:, :first] = old[...]


def scale_kernel(row_total, sums, *refs):
    *chunks, out = refs
    first = 0
    for chunk in chunks:
        tile = pl.ds(first, chunk.shape[1])
        out[:, tile] = chunk[...] / (sums[:, tile] / row_total + EPS)
        first += chunk.shape[1]


def together(*values):
    return lax.optimization_barrier(values)


VMEM = pl.BlockSpec(memory_space=pltpu.VMEM)
SMEM = pl.BlockSpec(memory_space=pltpu.SMEM)


def call(kernel, out_shapes, specs, scratch=(), flops=0, limit=16, **kwargs):
    def run(*args):
        moved = sum(a.size * a.dtype.itemsize for a in (*args, *out_shapes))
        return pl.pallas_call(
            kernel,
            out_shape=out_shapes,
            in_specs=specs,
            scratch_shapes=scratch,
            cost_estimate=pl.CostEstimate(flops=flops, bytes_accessed=moved, transcendentals=0),
            compiler_params=pltpu.CompilerParams(vmem_limit_bytes=limit * 2**20),
            **{"out_specs": [VMEM] * len(out_shapes), **kwargs},
        )(*args)

    return run


def local(a_panels, b_panels, a_pattern, c_pattern):
    rows, _, sections, width = a_panels.shape
    depth, columns = b_panels.shape[2:]
    n_row, n_col, fibers = (lax.axis_size(name) for name in ("row", "col", "fiber"))
    local_rows = rows * n_col
    share = local_rows // fibers
    if (n_row, n_col, fibers, sections, columns) != (8, 2, 2, 2, sum(CHUNKS)):
        return gathered(a_panels, b_panels, a_pattern, c_pattern)

    f32, bf16 = jnp.float32, jnp.bfloat16
    shape = jax.ShapeDtypeStruct
    shard_depth = sections * depth
    half = width * sections // 2
    plane_rows = 4 * rows

    down = lax.ppermute(b_panels, "row", line_pairs(1))
    up = lax.ppermute(b_panels, "row", line_pairs(-1))

    steps = (-1, 1, 0, 2)
    group = 64
    blocked = pl.BlockSpec((group, half), lambda i: (i, 0))
    mine, other = call(
        functools.partial(left_kernel, steps, rows),
        [shape((rows, half), f32)] * 2,
        [SMEM, pl.BlockSpec((group, 1, sections, width), lambda i: (i, 0, 0, 0))],
        [pltpu.VMEM((n_row, sections, group, depth), f32)],
        limit=56,
        grid=(rows // group,),
        out_specs=[blocked] * 2,
    )(a_pattern, a_panels)
    swap = [(0, 1), (1, 0)]
    swap_y = [(r, r ^ 1) for r in range(n_row)]
    swap_both = [(r * 2 + c, (r ^ 1) * 2 + 1 - c) for r in range(n_row) for c in range(2)]
    from_x = lax.ppermute(mine, "col", swap)
    from_y = lax.ppermute(other, "row", swap_y)
    from_both = lax.ppermute(other, ("row", "col"), swap_both)
    cuts = ((0, 2 * shard_depth), (2 * shard_depth, 3 * shard_depth), (3 * shard_depth, half))
    near_high, near_low, own_high, own_low, far_high, far_low = call(
        functools.partial(order_kernel, cuts),
        [shape((plane_rows, b - a), bf16) for a, b in cuts for _ in range(2)],
        [VMEM] * 4,
    )(mine, from_x, from_y, from_both)

    starts = [sum(CHUNKS[:j]) for j in range(len(CHUNKS))]
    far = [
        lax.ppermute(down[..., first : first + chunk], "row", line_pairs(1))
        for first, chunk in zip(starts, CHUNKS, strict=True)
    ]

    def near_product(j):
        factor = pltpu.VMEM((3 * shard_depth, CHUNKS[j]), bf16)
        (total,) = call(
            functools.partial(near_kernel, starts[j]),
            [shape((plane_rows, CHUNKS[j]), f32)],
            [VMEM] * 7,
            [factor, factor],
            6 * plane_rows * CHUNKS[j] * 3 * shard_depth,
        )(own_high, own_low, near_high, near_low, b_panels, down, up)
        return total

    ends = []
    near = near_product(0)
    for j, (shard, chunk) in enumerate(zip(far, CHUNKS, strict=True)):
        if ends:
            shard, _ = together(shard, ends[-1])
        factor = pltpu.VMEM((shard_depth, chunk), bf16)
        kept, sent = call(
            far_kernel,
            [shape((2, rows, chunk), f32)] * 2,
            [VMEM] * 4,
            [factor, factor],
            6 * plane_rows * chunk * shard_depth,
        )(far_high, far_low, near, shard)
        received = lax.ppermute(sent, "fiber", swap)
        if j + 1 < len(CHUNKS):
            near = near_product(j + 1)
            received, near = together(received, near)
        stays, goes = call(fold_kernel, [shape((rows, chunk), f32)] * 2, [VMEM] * 2)(kept, received)
        ends.append(goes)
        far[j] = stays, lax.ppermute(goes, "row", swap_y)
    squares, sums = [], []
    for j, (stays, received) in enumerate(far):
        received, _ = together(received, ends[-1])
        square, total = call(
            functools.partial(square_kernel, starts[j]),
            [shape((rows, CHUNKS[j]), f32), shape((1, starts[j] + CHUNKS[j]), f32)],
            [SMEM] + [VMEM] * (2 + len(sums)),
        )(c_pattern, stays, received, *sums)
        squares.append(square)
        sums = [total]
    total = all_sum(all_sum(sums[0], "fiber"), "row")
    (out,) = call(
        functools.partial(scale_kernel, share * fibers * n_row),
        [shape((share, columns), f32)],
        [VMEM] * (1 + len(squares)),
    )(total, *squares)
    return out


def solution(mesh):
    placed = (
        P(("row", "col"), "fiber", None, None),
        P("fiber", None, "row", "col"),
        P("row", "fiber", None, None),
        P("row", "col"),
    )

    return jax.shard_map(local, mesh=mesh, in_specs=placed, out_specs=P(("row", "fiber"), "col"), check_vma=False)
```

```python
import functools

import jax
import jax.numpy as jnp
from jax import lax
from jax.experimental import pallas as pl
from jax.experimental.pallas import tpu as pltpu
from jax.sharding import PartitionSpec as P


BLK = 128


EPS = 1e-06
CHUNKS = (128, 256, 256, 256, 128)


LINE = (0, 1, 3, 2)


def line_pairs(shift):
    size = len(LINE)
    return [
        (LINE[i] * 2 + y, LINE[(i + shift) % size] * 2 + y) for i in range(size) for y in range(2)
    ]


def line_at(z, step):
    place = jnp.where(z < 2, z, 5 - z)
    place = (place + step + len(LINE)) % len(LINE)
    return jnp.where(place < 2, place, 5 - place)


def all_sum(value, axis_name):
    size = lax.axis_size(axis_name)
    stride = 1
    while stride < size:
        rest = size // stride
        radix = next(p for p in range(2, rest + 1) if rest % p == 0)
        total = value
        for turn in range(1, radix):
            pairs = []
            for i in range(size):
                digit = i // stride % radix
                pairs.append((i, i + ((digit + turn) % radix - digit) * stride))
            total = total + lax.ppermute(value, axis_name, pairs)
        value = total
        stride *= radix
    return value


def gathered(a_panels, b_panels, a_pattern, c_pattern):
    _, _, sections, width = a_panels.shape
    block_rows, width_blocks = a_pattern.shape[0], a_pattern.shape[3]
    columns = b_panels.shape[3]
    local_rows = block_rows * BLK
    n_row, fibers = lax.axis_size("row"), lax.axis_size("fiber")
    share = local_rows // fibers
    total = jnp.zeros((local_rows, columns), jnp.float32)
    for section in range(sections):
        block = lax.all_gather(a_panels[:, 0, section, :], "col", axis=0, tiled=True)
        keep = a_pattern[:, 0, section, :].astype(jnp.float32)
        left = block.reshape(block_rows, BLK, width_blocks, BLK) * keep[:, None, :, None]
        right = lax.all_gather(b_panels[0, section], "row", axis=0, tiled=True)
        total = total + jnp.dot(
            left.reshape(local_rows, width),
            right,
            precision=lax.Precision.HIGH,
            preferred_element_type=jnp.float32,
        )
    keep = jnp.broadcast_to(
        c_pattern.astype(jnp.float32)[:, None, :, None],
        (block_rows, BLK, columns // BLK, BLK),
    ).reshape(local_rows, columns)
    merged = lax.psum_scatter(total, "fiber", scatter_dimension=0, tiled=True)
    product = merged * lax.dynamic_slice_in_dim(keep, lax.axis_index("fiber") * share, share, 0)
    inflated = product * product
    sums = all_sum(all_sum(jnp.sum(inflated, axis=0, keepdims=True), "fiber"), "row")
    return inflated / (sums / (share * fibers * n_row) + EPS)


def split(value):
    high = value.astype(jnp.bfloat16)
    low = (value - high.astype(jnp.float32)).astype(jnp.bfloat16)
    return high, low


def product3(a_high, a_low, b_high, b_low):
    def dot(x, y):
        return jnp.dot(x, y, preferred_element_type=jnp.float32)

    return dot(a_high, b_high) + (dot(a_high, b_low) + dot(a_low, b_high))


def left_kernel(steps, pattern, source, mine, other, turned):
    rows, _, sections, width = source.shape
    n_row, row = lax.axis_size("row"), lax.axis_index("row")
    depth = width // n_row
    group = 64
    for g in range(rows // group):
        part = pl.ds(g * group, group)
        block_row = (lax.axis_index("col") * rows + g * group) // BLK
        for s in range(sections):
            kept = []
            for w in range(width // BLK):
                keep = pattern[block_row, 0, s, w]
                piece = source[part, 0, s, pl.ds(w * BLK, BLK)]
                kept.append(jnp.where(keep != 0, piece, 0.0))
            value = jnp.concatenate(kept, axis=1)
            for r in range(n_row):
                turned[r, s, part, :] = value[:, r * depth : (r + 1) * depth]
        for out, parity in ((mine, row % 2), (other, 1 - row % 2)):
            owners = [line_at(row // 2, step) * 2 + parity for step in steps]
            pieces = [turned[r, s, part, :] for r in owners for s in range(sections)]
            out[part, :] = jnp.concatenate(pieces, axis=1)


def order_kernel(cuts, own_x, other_x, *outs):
    rows = own_x.shape[0]
    flip = lax.axis_index("col") ^ lax.axis_index("fiber")
    for x, piece in enumerate((own_x, other_x)):
        start = pl.multiple_of((x ^ flip) * rows, rows)
        for i, (first, last) in enumerate(cuts):
            high, low = split(piece[:, first:last])
            outs[2 * i][pl.ds(start, rows), :] = high
            outs[2 * i + 1][pl.ds(start, rows), :] = low


def stacked(early, late):
    return jnp.concatenate([early[...], late[...]], axis=0)


def near_kernel(first, *refs):
    lefts, (down, up, own, out, b_high, b_low) = refs[:8], refs[8:]
    high, low, own_high, own_low = (stacked(*lefts[2 * i : 2 * i + 2]) for i in range(4))
    _, sections, depth, _ = own.shape
    tile = slice(first, first + out.shape[1])
    for i, shard in enumerate((down, up, own)):
        for s in range(sections):
            part = pl.ds((i * sections + s) * depth, depth)
            b_high[part, :], b_low[part, :] = split(shard[0, s, :, tile])
    cut = 2 * sections * depth
    total = product3(high, low, b_high[:cut, :], b_low[:cut, :])
    out[...] = total + product3(own_high, own_low, b_high[cut:, :], b_low[cut:, :])


def far_kernel(*refs):
    lefts, (near, shard, kept, sent, b_high, b_low) = refs[:4], refs[4:]
    high, low = stacked(*lefts[:2]), stacked(*lefts[2:])
    _, sections, depth, _ = shard.shape
    rows = kept.shape[1]
    for s in range(sections):
        part = pl.ds(s * depth, depth)
        b_high[part, :], b_low[part, :] = split(shard[0, s])
    value = product3(high, low, b_high[...], b_low[...])
    for block in range(4):
        y, x = divmod(block, 2)
        out = sent if x else kept
        out[y] = near[pl.ds(block * rows, rows), :] + value[block * rows : (block + 1) * rows]


def fold_kernel(kept, received, mine, other):
    mine[...] = kept[0] + received[0]
    other[...] = kept[1] + received[1]


def square_kernel(count, pattern, *refs):
    mine, received, (squares, sums) = refs[:count], refs[count : 2 * count], refs[2 * count :]
    share = squares.shape[0]
    fiber = lax.axis_index("fiber")
    group = 64
    first = 0
    for ours, theirs in zip(mine, received, strict=True):
        for w in range(ours.shape[1] // BLK):
            tile, place = pl.ds(w * BLK, BLK), pl.ds(first + w * BLK, BLK)
            total = jnp.zeros((8, BLK), jnp.float32)
            for g in range(share // group):
                keep = pattern[(fiber * share + g * group) // BLK, first // BLK + w]
                part = pl.ds(g * group, group)
                value = ours[part, tile] + theirs[part, tile]
                value = jnp.where(keep != 0, value, 0.0)
                value = value * value
                squares[part, place] = value
                total += jnp.sum(value.reshape(group // 8, 8, BLK), axis=0)
            sums[:, place] = jnp.sum(total, axis=0, keepdims=True)
        first += ours.shape[1]


def scale_kernel(row_total, sums, squares, out):
    out[...] = squares[...] / (sums[...] / row_total + EPS)


def together(*values):
    return lax.optimization_barrier(values)


VMEM = pl.BlockSpec(memory_space=pltpu.VMEM)
SMEM = pl.BlockSpec(memory_space=pltpu.SMEM)


def call(kernel, out_shapes, specs, scratch=(), flops=0, limit=16, **kwargs):
    def run(*args):
        moved = sum(a.size * a.dtype.itemsize for a in (*args, *out_shapes))
        return pl.pallas_call(
            kernel,
            out_shape=out_shapes,
            in_specs=specs,
            scratch_shapes=scratch,
            cost_estimate=pl.CostEstimate(flops=flops, bytes_accessed=moved, transcendentals=0),
            compiler_params=pltpu.CompilerParams(vmem_limit_bytes=limit * 2**20),
            **{"out_specs": [VMEM] * len(out_shapes), **kwargs},
        )(*args)

    return run


def local(a_panels, b_panels, a_pattern, c_pattern):
    rows, _, sections, width = a_panels.shape
    depth, columns = b_panels.shape[2:]
    n_row, n_col, fibers = (lax.axis_size(name) for name in ("row", "col", "fiber"))
    local_rows = rows * n_col
    share = local_rows // fibers
    if (n_row, n_col, fibers, sections, columns) != (8, 2, 2, 2, sum(CHUNKS)):
        return gathered(a_panels, b_panels, a_pattern, c_pattern)

    f32, bf16 = jnp.float32, jnp.bfloat16
    shape = jax.ShapeDtypeStruct
    shard_depth = sections * depth
    half = width * sections // 2
    plane_rows = 4 * rows

    down = lax.ppermute(b_panels, "row", line_pairs(1))
    up = lax.ppermute(b_panels, "row", line_pairs(-1))

    steps = (-1, 1, 0, 2)
    mine, other = call(
        functools.partial(left_kernel, steps),
        [shape((rows, half), f32)] * 2,
        [SMEM, VMEM],
        [pltpu.VMEM((n_row, sections, rows, depth), f32)],
    )(a_pattern, a_panels)
    swap = [(0, 1), (1, 0)]
    swap_y = [(r, r ^ 1) for r in range(n_row)]
    swap_both = [(r * 2 + c, (r ^ 1) * 2 + 1 - c) for r in range(n_row) for c in range(2)]
    from_x = lax.ppermute(mine, "col", swap)
    from_y = lax.ppermute(other, "row", swap_y)
    from_both = lax.ppermute(other, ("row", "col"), swap_both)
    cuts = ((0, 2 * shard_depth), (2 * shard_depth, 3 * shard_depth), (3 * shard_depth, half))

    def ordered(*pieces):
        return call(
            functools.partial(order_kernel, cuts),
            [shape((2 * rows, b - a), bf16) for a, b in cuts for _ in range(2)],
            [VMEM] * 2,
        )(*pieces)

    lefts = list(zip(ordered(mine, from_x), ordered(from_y, from_both), strict=True))
    near_lefts = [part for pair in lefts[:4] for part in pair]
    far_lefts = [part for pair in lefts[4:] for part in pair]

    starts = [sum(CHUNKS[:j]) for j in range(len(CHUNKS))]
    far = [
        lax.ppermute(down[..., first : first + chunk], "row", line_pairs(1))
        for first, chunk in zip(starts, CHUNKS, strict=True)
    ]

    def near_product(j):
        factor = pltpu.VMEM((3 * shard_depth, CHUNKS[j]), bf16)
        (total,) = call(
            functools.partial(near_kernel, starts[j]),
            [shape((plane_rows, CHUNKS[j]), f32)],
            [VMEM] * 11,
            [factor, factor],
            6 * plane_rows * CHUNKS[j] * 3 * shard_depth,
        )(*near_lefts, down, up, b_panels)
        return total

    ends = []
    near = near_product(0)
    for j, (shard, chunk) in enumerate(zip(far, CHUNKS, strict=True)):
        if ends:
            shard, _ = together(shard, ends[-1])
        factor = pltpu.VMEM((shard_depth, chunk), bf16)
        kept, sent = call(
            far_kernel,
            [shape((2, rows, chunk), f32)] * 2,
            [VMEM] * 6,
            [factor, factor],
            6 * plane_rows * chunk * shard_depth,
        )(*far_lefts, near, shard)
        received = lax.ppermute(sent, "fiber", swap)
        if j + 1 < len(CHUNKS):
            near = near_product(j + 1)
            received, near = together(received, near)
        stays, goes = call(fold_kernel, [shape((rows, chunk), f32)] * 2, [VMEM] * 2)(kept, received)
        ends.append(goes)
        far[j] = stays, lax.ppermute(goes, "row", swap_y)
    squares, sums = call(
        functools.partial(square_kernel, len(far)),
        [shape((share, columns), f32), shape((1, columns), f32)],
        [SMEM] + [VMEM] * (2 * len(far)),
    )(c_pattern, *(stays for stays, _ in far), *(received for _, received in far))
    total = all_sum(all_sum(sums, "fiber"), "row")
    (out,) = call(
        functools.partial(scale_kernel, share * fibers * n_row),
        [shape((share, columns), f32)],
        [VMEM] * 2,
    )(total, squares)
    return out


def solution(mesh):
    placed = (
        P(("row", "col"), "fiber", None, None),
        P("fiber", None, "row", "col"),
        P("row", "fiber", None, None),
        P("row", "col"),
    )

    return jax.shard_map(
        local, mesh=mesh, in_specs=placed, out_specs=P(("row", "fiber"), "col"), check_vma=False
    )
```

```python
import functools

import jax
import jax.numpy as jnp
from jax import lax
from jax.experimental import pallas as pl
from jax.experimental.pallas import tpu as pltpu
from jax.sharding import PartitionSpec as P


BLK = 128


EPS = 1e-06
TILE = 256
LAST = 256


def ring_order(size):
    return list(range(0, size, 2)) + list(range(size - 1, 0, -2))


def owner_at(size, row, step):
    place = jnp.where(row % 2 == 0, row // 2, size - 1 - row // 2)
    place = (place + step + size) % size
    return jnp.where(place < size // 2, 2 * place, 2 * (size - 1 - place) + 1)


def shifted(order, step):
    size = len(order)
    return [(order[i], order[(i + step) % size]) for i in range(size)]


def all_sum(value, axis_name):
    size = lax.axis_size(axis_name)
    stride = 1
    while stride < size:
        rest = size // stride
        radix = next(p for p in range(2, rest + 1) if rest % p == 0)
        total = value
        for turn in range(1, radix):
            pairs = []
            for i in range(size):
                digit = i // stride % radix
                pairs.append((i, i + ((digit + turn) % radix - digit) * stride))
            total = total + lax.ppermute(value, axis_name, pairs)
        value = total
        stride *= radix
    return value


def gathered(a_panels, b_panels, a_pattern, c_pattern):
    _, _, sections, width = a_panels.shape
    block_rows, width_blocks = a_pattern.shape[0], a_pattern.shape[3]
    columns = b_panels.shape[3]
    local_rows = block_rows * BLK
    n_row, fibers = lax.axis_size("row"), lax.axis_size("fiber")
    share = local_rows // fibers
    total = jnp.zeros((local_rows, columns), jnp.float32)
    for section in range(sections):
        block = lax.all_gather(a_panels[:, 0, section, :], "col", axis=0, tiled=True)
        keep = a_pattern[:, 0, section, :].astype(jnp.float32)
        left = block.reshape(block_rows, BLK, width_blocks, BLK) * keep[:, None, :, None]
        right = lax.all_gather(b_panels[0, section], "row", axis=0, tiled=True)
        total = total + jnp.dot(
            left.reshape(local_rows, width),
            right,
            precision=lax.Precision.HIGH,
            preferred_element_type=jnp.float32,
        )
    keep = jnp.broadcast_to(
        c_pattern.astype(jnp.float32)[:, None, :, None],
        (block_rows, BLK, columns // BLK, BLK),
    ).reshape(local_rows, columns)
    merged = lax.psum_scatter(total, "fiber", scatter_dimension=0, tiled=True)
    product = merged * lax.dynamic_slice_in_dim(keep, lax.axis_index("fiber") * share, share, 0)
    inflated = product * product
    sums = all_sum(all_sum(jnp.sum(inflated, axis=0, keepdims=True), "fiber"), "row")
    return inflated / (sums / (share * fibers * n_row) + EPS)


def split(value):
    high = value.astype(jnp.bfloat16)
    low = (value - high.astype(jnp.float32)).astype(jnp.bfloat16)
    return high, low


def product3(a_high, a_low, b_high, b_low):
    def dot(x, y):
        return jnp.dot(x, y, preferred_element_type=jnp.float32)

    return dot(a_high, b_high) + (dot(a_high, b_low) + dot(a_low, b_high))


def left_kernel(groups, is_peer, pattern, source, *refs):
    *outs, turned = refs
    rows, _, sections, width = source.shape
    n_row, row = lax.axis_size("row"), lax.axis_index("row")
    depth = width // n_row
    col = lax.axis_index("col")
    position = 1 - col if is_peer else col
    group = 64
    for g in range(rows // group):
        part = pl.ds(g * group, group)
        block_row = (position * rows + g * group) // BLK
        for s in range(sections):
            kept = []
            for w in range(width // BLK):
                keep = pattern[block_row, 0, s, w]
                piece = source[part, 0, s, pl.ds(w * BLK, BLK)]
                kept.append(jnp.where(keep != 0, piece, 0.0))
            value = jnp.concatenate(kept, axis=1)
            for r in range(n_row):
                turned[r, s, part, :] = value[:, r * depth : (r + 1) * depth]
        for i, members in enumerate(groups):
            pieces = [turned[owner_at(n_row, row, step), s, part, :] for step, s in members]
            high, low = split(jnp.concatenate(pieces, axis=1))
            outs[2 * i][part, :] = high
            outs[2 * i + 1][part, :] = low


def group_kernel(count, *refs):
    own_high, own_low, peer_high, peer_low, *rest = refs
    shards, (*near, out, b_high, b_low) = rest[:count], rest[count:]
    depth, columns = shards[0].shape
    rows = own_high.shape[0]
    for i, shard in enumerate(shards):
        part = pl.ds(i * depth, depth)
        b_high[part, :], b_low[part, :] = split(shard[...])
    high = jnp.concatenate([own_high[...], peer_high[...]], axis=0)
    low = jnp.concatenate([own_low[...], peer_low[...]], axis=0)
    for t in range(columns // TILE):
        tile = pl.ds(t * TILE, TILE)
        total = product3(high, low, b_high[:, tile], b_low[:, tile])
        for k in range(2):
            value = total[k * rows : (k + 1) * rows]
            out[k, :, tile] = near[0][k, :, tile] + value if near else value


def far_kernel(is_kept, count, first, *refs):
    own_high, own_low, peer_high, peer_low, *rest = refs
    shards, (near, out, b_high, b_low) = rest[:count], rest[count:]
    depth, columns = shards[0].shape
    peers = lax.axis_index("col") != lax.axis_index("fiber")
    if not is_kept:
        peers = jnp.logical_not(peers)
    for i, shard in enumerate(shards):
        part = pl.ds(i * depth, depth)
        b_high[part, :], b_low[part, :] = split(shard[...])
    for k, (high, low) in enumerate(((own_high, own_low), (peer_high, peer_low))):

        @pl.when(peers == (k == 1))
        def _():
            for t in range(columns // TILE):
                tile = pl.ds(t * TILE, TILE)
                value = product3(high[...], low[...], b_high[:, tile], b_low[:, tile])
                out[:, tile] = near[k, :, pl.ds(first + t * TILE, TILE)] + value


def last_kernel(count, first, *refs):
    own_high, own_low, peer_high, peer_low, *rest = refs
    shards, (near, out, b_high, b_low) = rest[:count], rest[count:]
    depth, columns = shards[0].shape
    rows = own_high.shape[0]
    for i, shard in enumerate(shards):
        part = pl.ds(i * depth, depth)
        b_high[part, :], b_low[part, :] = split(shard[...])
    high = jnp.concatenate([own_high[...], peer_high[...]], axis=0)
    low = jnp.concatenate([own_low[...], peer_low[...]], axis=0)
    value = product3(high, low, b_high[...], b_low[...])
    for k in range(2):
        out[k] = near[k, :, first : first + columns] + value[k * rows : (k + 1) * rows]


def square_kernel(pattern, kept, received, squares, sums):
    share, columns = kept.shape
    fiber = lax.axis_index("fiber")
    group = 64
    for w in range(columns // BLK):
        tile = pl.ds(w * BLK, BLK)
        total = jnp.zeros((8, BLK), jnp.float32)
        for g in range(share // group):
            keep = pattern[(fiber * share + g * group) // BLK, w]
            part = pl.ds(g * group, group)
            value = kept[part, tile] + received[part, tile]
            value = jnp.where(keep != 0, value, 0.0)
            value = value * value
            squares[part, tile] = value
            total += jnp.sum(value.reshape(group // 8, 8, BLK), axis=0)
        sums[:, tile] = jnp.sum(total, axis=0, keepdims=True)


def square_last_kernel(first, pattern, mine, received, early, squares, sums):
    _, share, columns = mine.shape
    fiber, col = lax.axis_index("fiber"), lax.axis_index("col")
    group = 64
    for w in range(columns // BLK):
        tile = pl.ds(w * BLK, BLK)
        total = jnp.zeros((8, BLK), jnp.float32)
        for target, block in ((None, 1 - fiber), (squares, fiber)):
            for g in range(share // group):
                keep = pattern[(block * share + g * group) // BLK, first // BLK + w]
                part = pl.ds(g * group, group)
                value = mine[block ^ col, part, tile] + received[block ^ col, part, tile]
                value = jnp.where(keep != 0, value, 0.0)
                value = value * value
                if target is not None:
                    target[part, tile] = value
                total += jnp.sum(value.reshape(group // 8, 8, BLK), axis=0)
        sums[:, pl.ds(first + w * BLK, BLK)] = jnp.sum(total, axis=0, keepdims=True)
    sums[:, :first] = early[...]


def scale_kernel(row_total, sums, early, last, out):
    first = early.shape[1]
    scale = sums[...] / row_total + EPS
    out[:, :first] = early[...] / scale[:, :first]
    out[:, first:] = last[...] / scale[:, first:]


VMEM = pl.BlockSpec(memory_space=pltpu.VMEM)
SMEM = pl.BlockSpec(memory_space=pltpu.SMEM)


def call(kernel, out_shapes, specs, scratch=(), flops=0):
    def run(*args):
        moved = sum(a.size * a.dtype.itemsize for a in (*args, *out_shapes))
        return pl.pallas_call(
            kernel,
            out_shape=out_shapes,
            in_specs=specs,
            out_specs=[VMEM] * len(out_shapes),
            scratch_shapes=scratch,
            cost_estimate=pl.CostEstimate(flops=flops, bytes_accessed=moved, transcendentals=0),
            compiler_params=pltpu.CompilerParams(vmem_limit_bytes=16 * 2**20),
        )(*args)

    return run


def local(a_panels, b_panels, a_pattern, c_pattern):
    rows, _, sections, _ = a_panels.shape
    depth, columns = b_panels.shape[2:]
    n_row, n_col, fibers = (lax.axis_size(name) for name in ("row", "col", "fiber"))
    local_rows = rows * n_col
    share = local_rows // fibers
    if (n_row, n_col, fibers, sections) != (8, 2, 2, 2) or columns <= LAST:
        return gathered(a_panels, b_panels, a_pattern, c_pattern)

    order = ring_order(n_row)
    forward, backward = shifted(order, 1), shifted(order, -1)
    far = n_row // 2
    groups = [
        [(0, 0), (0, 1), (-1, 0), (1, 1), (-1, 1), (1, 0)],
        [(-2, 0), (2, 1), (-2, 1), (2, 0), (-3, 0), (3, 1)],
        [(-3, 1), (3, 0)],
        [(far, 0), (far, 1)],
    ]
    parts = []
    for members in groups:
        parts += [jax.ShapeDtypeStruct((rows, len(members) * depth), jnp.bfloat16)] * 2

    def left(source, is_peer):
        return call(
            functools.partial(left_kernel, groups, is_peer),
            parts,
            [SMEM, VMEM],
            [pltpu.VMEM((n_row, sections, rows, depth), jnp.float32)],
        )(a_pattern, source)

    def multiply(g, *near):
        members = groups[g]
        factor = pltpu.VMEM((len(members) * depth, columns), jnp.bfloat16)
        operands = [*lefts[0][2 * g : 2 * g + 2], *lefts[1][2 * g : 2 * g + 2]]
        operands += [shards[m] for m in members if m in shards]
        return operands, members, factor, near

    def near_product(g, *near):
        operands, members, factor, near = multiply(g, *near)
        (total,) = call(
            functools.partial(group_kernel, len(members)),
            [jax.ShapeDtypeStruct((n_col, rows, columns), jnp.float32)],
            [VMEM] * (len(operands) + len(near)),
            [factor, factor],
            6 * local_rows * columns * depth * len(members),
        )(*operands, *near)
        return total

    def far_product(kernel, out_shape, first, chunks, near):
        operands, members, _, _ = multiply(far_group)
        chunk = chunks[0].shape[1]
        factor = pltpu.VMEM((len(members) * depth, chunk), jnp.bfloat16)
        (total,) = call(
            functools.partial(kernel, len(members), first),
            [jax.ShapeDtypeStruct((*out_shape, chunk), jnp.float32)],
            [VMEM] * (len(operands) + len(chunks) + 1),
            [factor, factor],
            6 * share * columns * depth * len(members),
        )(*operands, *chunks, near)
        return total

    far_group = len(groups) - 1
    swap = [(0, 1), (1, 0)]
    peer_rows = lax.ppermute(a_panels, "col", swap)
    own = [b_panels[0, s] for s in range(sections)]
    shards = {(0, s): own[s] for s in range(sections)}

    def hop(step, s):
        if step < 0:
            shards[step, s] = lax.ppermute(shards[step + 1, s], "row", forward)
        else:
            shards[step, s] = lax.ppermute(shards[step - 1, s], "row", backward)

    def after(value, *keys):
        held = lax.optimization_barrier((value, [shards[k] for k in keys]))
        shards.update(zip(keys, held[1], strict=True))
        return held[0]

    first, second = ((-1, 0), (1, 1)), ((-1, 1), (1, 0))
    for sign, s in (*first, *second):
        hop(sign, s)
    lefts = [after(left(a_panels, False), (-1, 0), (1, 1))]
    for sign, s in (*first, *second):
        hop(2 * sign, s)
    for sign, s in first:
        hop(3 * sign, s)
    lefts.append(after(left(peer_rows, True), (-2, 1), (2, 0)))
    for sign, s in second:
        hop(3 * sign, s)
    near = after(near_product(0), (-3, 0), (3, 1))
    cut = columns - LAST
    ends = []
    for (first, last) in ((0, cut), (cut, columns)):
        ends.append(
            [
                lax.ppermute(shards[-3, 0][:, first:last], "row", forward),
                lax.ppermute(shards[3, 1][:, first:last], "row", backward),
            ]
        )
    near = near_product(1, near)
    near = near_product(2, near)
    sent = far_product(functools.partial(far_kernel, False), (share,), 0, ends[0], near)
    received = lax.ppermute(sent, "fiber", swap)
    kept = far_product(functools.partial(far_kernel, True), (share,), 0, ends[0], near)
    mine = far_product(last_kernel, (n_col, rows), cut, ends[1], near)
    theirs = lax.ppermute(mine, "fiber", swap)
    squares, sums = call(
        square_kernel,
        [
            jax.ShapeDtypeStruct((share, cut), jnp.float32),
            jax.ShapeDtypeStruct((1, cut), jnp.float32),
        ],
        [SMEM, VMEM, VMEM],
    )(c_pattern, kept, received)
    sums = all_sum(sums, "fiber")
    last_squares, sums = call(
        functools.partial(square_last_kernel, cut),
        [
            jax.ShapeDtypeStruct((share, LAST), jnp.float32),
            jax.ShapeDtypeStruct((1, columns), jnp.float32),
        ],
        [SMEM, VMEM, VMEM, VMEM],
    )(c_pattern, mine, theirs, sums)
    (out,) = call(
        functools.partial(scale_kernel, share * fibers * n_row),
        [jax.ShapeDtypeStruct((share, columns), jnp.float32)],
        [VMEM] * 3,
    )(all_sum(sums, "row"), squares, last_squares)
    return out


def solution(mesh):
    placed = (
        P(("row", "col"), "fiber", None, None),
        P("fiber", None, "row", "col"),
        P("row", "fiber", None, None),
        P("row", "col"),
    )

    return jax.shard_map(
        local, mesh=mesh, in_specs=placed, out_specs=P(("row", "fiber"), "col"), check_vma=False
    )
```

```python
import functools

import jax
import jax.numpy as jnp
from jax import lax
from jax.experimental import pallas as pl
from jax.experimental.pallas import tpu as pltpu
from jax.sharding import PartitionSpec as P


BLK = 128


EPS = 1e-06
LAST = 128
UNIT = 64


LINE = (0, 1, 3, 2)


def line_pairs(shift):
    size = len(LINE)
    return [
        (LINE[i] * 2 + y, LINE[(i + shift) % size] * 2 + y) for i in range(size) for y in range(2)
    ]


def line_at(z, step):
    place = jnp.where(z < 2, z, 5 - z)
    place = (place + step + len(LINE)) % len(LINE)
    return jnp.where(place < 2, place, 5 - place)


def all_sum(value, axis_name):
    size = lax.axis_size(axis_name)
    stride = 1
    while stride < size:
        rest = size // stride
        radix = next(p for p in range(2, rest + 1) if rest % p == 0)
        total = value
        for turn in range(1, radix):
            pairs = []
            for i in range(size):
                digit = i // stride % radix
                pairs.append((i, i + ((digit + turn) % radix - digit) * stride))
            total = total + lax.ppermute(value, axis_name, pairs)
        value = total
        stride *= radix
    return value


def gathered(a_panels, b_panels, a_pattern, c_pattern):
    _, _, sections, width = a_panels.shape
    block_rows, width_blocks = a_pattern.shape[0], a_pattern.shape[3]
    columns = b_panels.shape[3]
    local_rows = block_rows * BLK
    n_row, fibers = lax.axis_size("row"), lax.axis_size("fiber")
    share = local_rows // fibers
    total = jnp.zeros((local_rows, columns), jnp.float32)
    for section in range(sections):
        block = lax.all_gather(a_panels[:, 0, section, :], "col", axis=0, tiled=True)
        keep = a_pattern[:, 0, section, :].astype(jnp.float32)
        left = block.reshape(block_rows, BLK, width_blocks, BLK) * keep[:, None, :, None]
        right = lax.all_gather(b_panels[0, section], "row", axis=0, tiled=True)
        total = total + jnp.dot(
            left.reshape(local_rows, width),
            right,
            precision=lax.Precision.HIGH,
            preferred_element_type=jnp.float32,
        )
    keep = jnp.broadcast_to(
        c_pattern.astype(jnp.float32)[:, None, :, None],
        (block_rows, BLK, columns // BLK, BLK),
    ).reshape(local_rows, columns)
    merged = lax.psum_scatter(total, "fiber", scatter_dimension=0, tiled=True)
    product = merged * lax.dynamic_slice_in_dim(keep, lax.axis_index("fiber") * share, share, 0)
    inflated = product * product
    sums = all_sum(all_sum(jnp.sum(inflated, axis=0, keepdims=True), "fiber"), "row")
    return inflated / (sums / (share * fibers * n_row) + EPS)


def split(value):
    high = value.astype(jnp.bfloat16)
    low = (value - high.astype(jnp.float32)).astype(jnp.bfloat16)
    return high, low


def product3(a_high, a_low, b_high, b_low):
    def dot(x, y):
        return jnp.dot(x, y, preferred_element_type=jnp.float32)

    return dot(a_high, b_high) + (dot(a_high, b_low) + dot(a_low, b_high))


def left_kernel(groups, plan, pattern, *refs):
    sources, outs, turned = refs[: len(plan)], refs[len(plan) : -1], refs[-1]
    _, _, sections, width = sources[0].shape
    n_row, row, col = lax.axis_size("row"), lax.axis_index("row"), lax.axis_index("col")
    depth = width // n_row
    done = 0
    for source, (which, is_peer, first) in zip(sources, plan, strict=True):
        position = 1 - col if is_peer else col
        for g in range(source.shape[0] // UNIT):
            part = pl.ds(g * UNIT, UNIT)
            block_row = (position * (3 * UNIT) + first + g * UNIT) // BLK
            for s in range(sections):
                kept = []
                for w in range(width // BLK):
                    keep = pattern[which, block_row, s * (width // BLK) + w]
                    kept.append(jnp.where(keep != 0, source[part, 0, s, pl.ds(w * BLK, BLK)], 0.0))
                value = jnp.concatenate(kept, axis=1)
                for r in range(n_row):
                    turned[r, s] = value[:, r * depth : (r + 1) * depth]
            place = pl.ds(done, UNIT)
            for i, members in enumerate(groups):
                owners = [line_at(row // 2, step) * 2 + (row + turn) % 2 for step, turn in members]
                pieces = [turned[r, s] for r in owners for s in range(sections)]
                high, low = split(jnp.concatenate(pieces, axis=1))
                outs[2 * i][place, :] = high
                outs[2 * i + 1][place, :] = low
            done += UNIT


def put_shards(shards, b_high, b_low):
    _, sections, depth, _ = shards[0].shape
    for i in range(len(shards) * sections):
        part = pl.ds(i * depth, depth)
        b_high[part, :], b_low[part, :] = split(shards[i // sections][0, i % sections])


def stacked(refs):
    return jnp.concatenate([ref[...] for ref in refs], axis=0)


def group_kernel(sets, sizes, *refs):
    lefts = refs[: 2 * sets * len(sizes)]
    rest = refs[len(lefts) :]
    shards, (*near, out, b_high, b_low) = rest[: sum(sizes)], rest[sum(sizes) :]
    put_shards(shards, b_high, b_low)
    total = near[0][...] if near else None
    first = 0
    for i in range(len(sizes)):
        group = lefts[2 * sets * i : 2 * sets * (i + 1)]
        high, low = stacked(group[:sets]), stacked(group[sets:])
        part = pl.ds(first, high.shape[1])
        value = product3(high, low, b_high[part, :], b_low[part, :])
        total = value if total is None else total + value
        first += high.shape[1]
    out[...] = total


def far_value(first, *refs):
    highs, lows, (near, near_late, shard, b_high, b_low) = refs[:4], refs[4:8], refs[8:]
    put_shards([shard], b_high, b_low)
    value = product3(stacked(highs), stacked(lows), b_high[...], b_low[...])
    tile = slice(first, first + shard.shape[3])
    return value + jnp.concatenate([near[:, tile], near_late[:, tile]], axis=0)


def far_kernel(first, *refs):
    *ins, kept, sent, b_high, b_low = refs
    value = far_value(first, *ins, b_high, b_low)
    rows = kept.shape[1]
    flip = lax.axis_index("col") ^ lax.axis_index("fiber")
    for turn in range(2):

        @pl.when(flip == turn)
        def _():
            for p in range(4):
                y, x = divmod(p, 2)
                out = kept if x == turn else sent
                out[y] = value[p * rows : (p + 1) * rows]


def last_kernel(first, *refs):
    *ins, out, b_high, b_low = refs
    value = far_value(first, *ins, b_high, b_low)
    rows = out.shape[1]
    for p in range(4):
        out[p] = value[p * rows : (p + 1) * rows]


def squared(pattern, which, fiber, first, value):
    columns = value.shape[1]
    half = lax.axis_index("row") % 2 * (pattern.shape[2] // 2)
    out = []
    for g in range(value.shape[0] // UNIT):
        block_row = (fiber * value.shape[0] + g * UNIT) // BLK
        kept = []
        for w in range(columns // BLK):
            keep = pattern[which, block_row, half + first // BLK + w]
            piece = value[g * UNIT : (g + 1) * UNIT, w * BLK : (w + 1) * BLK]
            piece = jnp.where(keep != 0, piece, 0.0)
            kept.append(piece * piece)
        out.append(jnp.concatenate(kept, axis=1) if len(kept) > 1 else kept[0])
    return jnp.concatenate(out, axis=0)


def square_kernel(pattern, kept, received, stays, goes, sums):
    fiber = lax.axis_index("fiber")
    mine = squared(pattern, 0, fiber, 0, kept[0] + received[0])
    other = squared(pattern, 1, fiber, 0, kept[1] + received[1])
    stays[...], goes[...] = mine, other
    sums[...] = jnp.sum(mine, axis=0, keepdims=True) + jnp.sum(other, axis=0, keepdims=True)


def square_last_kernel(first, pattern, mine, received, early, stays, goes, sums):
    fiber, col = lax.axis_index("fiber"), lax.axis_index("col")
    total = None
    for y, target in ((0, stays), (1, goes)):
        for block in (1 - fiber, fiber):
            p = 2 * y + (block ^ col)
            value = squared(pattern, y, block, first, mine[p] + received[p])
            part = jnp.sum(value, axis=0, keepdims=True)
            total = part if total is None else total + part
        target[...] = value
    sums[:, :first] = early[...]
    sums[:, first:] = total


def scale_kernel(row_total, sums, other_sums, *refs):
    *parts, out = refs
    half = sums.shape[1]
    y = lax.axis_index("row") % 2
    for side, total, (early, last) in ((y, sums, parts[:2]), (1 - y, other_sums, parts[2:])):
        scale = total[...] / row_total + EPS
        cut = early.shape[1]
        out[:, pl.ds(pl.multiple_of(side * half, BLK), cut)] = early[...] / scale[:, :cut]
        out[:, pl.ds(pl.multiple_of(side * half + cut, BLK), half - cut)] = last[...] / scale[:, cut:]


def together(*values):
    return lax.optimization_barrier(values)


VMEM = pl.BlockSpec(memory_space=pltpu.VMEM)
SMEM = pl.BlockSpec(memory_space=pltpu.SMEM)


def call(kernel, out_shapes, specs, scratch=(), flops=0):
    def run(*args):
        moved = sum(a.size * a.dtype.itemsize for a in (*args, *out_shapes))
        return pl.pallas_call(
            kernel,
            out_shape=out_shapes,
            in_specs=specs,
            out_specs=[VMEM] * len(out_shapes),
            scratch_shapes=scratch,
            cost_estimate=pl.CostEstimate(flops=flops, bytes_accessed=moved, transcendentals=0),
            compiler_params=pltpu.CompilerParams(vmem_limit_bytes=16 * 2**20),
        )(*args)

    return run


def local(a_panels, b_panels, a_pattern, c_pattern):
    rows, _, sections, _ = a_panels.shape
    block_rows = a_pattern.shape[0]
    depth, columns = b_panels.shape[2:]
    n_row, n_col, fibers = (lax.axis_size(name) for name in ("row", "col", "fiber"))
    local_rows = rows * n_col
    share = local_rows // fibers
    if (n_row, n_col, fibers, sections, rows, columns) != (8, 2, 2, 2, 3 * UNIT, 1024):
        return gathered(a_panels, b_panels, a_pattern, c_pattern)

    f32, bf16 = jnp.float32, jnp.bfloat16
    shape = jax.ShapeDtypeStruct
    half = columns // 2
    cut = half - LAST
    my_y = lax.axis_index("row") & 1
    swap = [(0, 1), (1, 0)]
    swap_y = [(r, r ^ 1) for r in range(n_row)]

    def columns_half(side):
        where = (0, 0, 0, side * half)
        sizes = (*b_panels.shape[:3], half)
        return lax.dynamic_slice(b_panels, where, sizes, allow_negative_indices=False)

    own, gives = columns_half(my_y), columns_half(1 - my_y)
    shards = {(0, 0): own}
    shards[0, 1] = lax.ppermute(gives, "row", swap_y)
    for turn in range(2):
        shards[-1, turn] = lax.ppermute(shards[0, turn], "row", line_pairs(1))
        shards[1, turn] = lax.ppermute(shards[0, turn], "row", line_pairs(-1))
    shards[2, 0] = lax.ppermute(shards[-1, 0], "row", line_pairs(1))
    far_early = lax.ppermute(shards[-1, 1][..., :cut], "row", line_pairs(1))
    far_last = lax.ppermute(shards[-1, 1][..., cut:], "row", line_pairs(1))

    units = [a_panels[u * UNIT : (u + 1) * UNIT] for u in range(3)]
    x2 = lax.ppermute(units[2], "col", swap)
    y0 = lax.ppermute(units[0], "row", swap_y)
    y1 = lax.ppermute(units[1], "row", swap_y)
    x01 = lax.ppermute(a_panels[: 2 * UNIT], "col", swap)
    d2 = lax.ppermute(x2, "row", swap_y)
    y2 = lax.ppermute(units[2], "row", swap_y)
    d0 = lax.ppermute(y0, "col", swap)
    d1 = lax.ppermute(y1, "col", swap)
    a_table = a_pattern.reshape(block_rows, -1)
    a_table = jnp.stack([a_table, lax.ppermute(a_table, "row", swap_y)])
    c_table = jnp.stack([c_pattern, lax.ppermute(c_pattern, "row", swap_y)])

    groups = [[(0, 0), (0, 1), (-1, 0), (1, 0)], [(-1, 1), (1, 1), (2, 0)], [(2, 1)]]
    shard_depth = sections * depth

    def left(*sources):
        arrays = [source for source, *_ in sources]
        plan = tuple((y, x, first) for _, y, x, first in sources)
        count = sum(source.shape[0] for source in arrays)
        parts = [shape((count, len(m) * shard_depth), bf16) for m in groups for _ in range(2)]
        return call(
            functools.partial(left_kernel, groups, plan),
            parts,
            [SMEM] + [VMEM] * len(arrays),
            [pltpu.VMEM((n_row, sections, UNIT, depth), f32)],
        )(a_table, *arrays)

    early_sets = [
        left((a_panels, 0, False, 0)),
        left((x01, 0, True, 0), (x2, 0, True, 2 * UNIT)),
        left((y0, 1, False, 0), (y1, 1, False, UNIT)),
    ]

    def picked(sets, g):
        return [s[2 * g] for s in sets] + [s[2 * g + 1] for s in sets]

    def product(sets, which, *near):
        lefts = [part for g in which for part in picked(sets, g)]
        members = [shards[m] for g in which for m in groups[g]]
        count = sum(s[0].shape[0] for s in sets)
        factor = pltpu.VMEM((len(members) * shard_depth, half), bf16)
        (total,) = call(
            functools.partial(group_kernel, len(sets), tuple(len(groups[g]) for g in which)),
            [shape((count, half), f32)],
            [VMEM] * (len(lefts) + len(members) + len(near)),
            [factor, factor],
            6 * count * half * len(members) * shard_depth,
        )(*lefts, *members, *near)
        return total

    near = product(early_sets, [0])
    y2, near = together(y2, near)
    late_set = left((y2, 1, False, 2 * UNIT), (d0, 1, True, 0), (d1, 1, True, UNIT), (d2, 1, True, 2 * UNIT))

    near = product(early_sets, [1], near)
    near_late = product([late_set], [0, 1])

    far_lefts = picked([*early_sets, late_set], 2)

    def far(kernel, first, shard, outs):
        factor = pltpu.VMEM((shard_depth, shard.shape[3]), bf16)
        return call(
            functools.partial(kernel, first),
            outs,
            [VMEM] * (len(far_lefts) + 3),
            [factor, factor],
            6 * 4 * rows * shard.shape[3] * shard_depth,
        )(*far_lefts, near, near_late, shard)

    kept, sent = far(far_kernel, 0, far_early, [shape((2, rows, cut), f32)] * 2)
    received = lax.ppermute(sent, "fiber", swap)
    (mine,) = far(last_kernel, cut, far_last, [shape((4, rows, LAST), f32)])
    theirs = lax.ppermute(mine, "fiber", swap)
    stays, goes, sums = call(
        square_kernel, [shape((rows, cut), f32)] * 2 + [shape((1, cut), f32)], [SMEM, VMEM, VMEM]
    )(c_table, kept, received)
    comes = lax.ppermute(goes, "row", swap_y)
    sums = sums + lax.ppermute(sums, "fiber", swap)
    last_stays, last_goes, sums = call(
        functools.partial(square_last_kernel, cut),
        [shape((rows, LAST), f32)] * 2 + [shape((1, half), f32)],
        [SMEM, VMEM, VMEM, VMEM],
    )(c_table, mine, theirs, sums)
    last_comes = lax.ppermute(last_goes, "row", swap_y)
    for bit in (2, 4):
        sums = sums + lax.ppermute(sums, "row", [(r, r ^ bit) for r in range(n_row)])
    other_sums = lax.ppermute(sums, "row", swap_y)
    (out,) = call(
        functools.partial(scale_kernel, share * fibers * n_row), [shape((share, columns), f32)], [VMEM] * 6
    )(sums, other_sums, stays, last_stays, comes, last_comes)
    return out


def solution(mesh):
    placed = (
        P(("row", "col"), "fiber", None, None),
        P("fiber", None, "row", "col"),
        P("row", "fiber", None, None),
        P("row", "col"),
    )

    return jax.shard_map(local, mesh=mesh, in_specs=placed, out_specs=P(("row", "fiber"), "col"), check_vma=False)
```

```python
import functools

import jax
import jax.numpy as jnp
from jax import lax
from jax.experimental import pallas as pl
from jax.experimental.pallas import tpu as pltpu
from jax.sharding import PartitionSpec as P


BLK = 128


EPS = 1e-06
LAST = 128
UNIT = 64


LINE = (0, 1, 3, 2)


def line_pairs(shift):
    size = len(LINE)
    return [
        (LINE[i] * 2 + y, LINE[(i + shift) % size] * 2 + y) for i in range(size) for y in range(2)
    ]


def line_at(z, step):
    place = jnp.where(z < 2, z, 5 - z)
    place = (place + step + len(LINE)) % len(LINE)
    return jnp.where(place < 2, place, 5 - place)


def all_sum(value, axis_name):
    size = lax.axis_size(axis_name)
    stride = 1
    while stride < size:
        rest = size // stride
        radix = next(p for p in range(2, rest + 1) if rest % p == 0)
        total = value
        for turn in range(1, radix):
            pairs = []
            for i in range(size):
                digit = i // stride % radix
                pairs.append((i, i + ((digit + turn) % radix - digit) * stride))
            total = total + lax.ppermute(value, axis_name, pairs)
        value = total
        stride *= radix
    return value


def gathered(a_panels, b_panels, a_pattern, c_pattern):
    _, _, sections, width = a_panels.shape
    block_rows, width_blocks = a_pattern.shape[0], a_pattern.shape[3]
    columns = b_panels.shape[3]
    local_rows = block_rows * BLK
    n_row, fibers = lax.axis_size("row"), lax.axis_size("fiber")
    share = local_rows // fibers
    total = jnp.zeros((local_rows, columns), jnp.float32)
    for section in range(sections):
        block = lax.all_gather(a_panels[:, 0, section, :], "col", axis=0, tiled=True)
        keep = a_pattern[:, 0, section, :].astype(jnp.float32)
        left = block.reshape(block_rows, BLK, width_blocks, BLK) * keep[:, None, :, None]
        right = lax.all_gather(b_panels[0, section], "row", axis=0, tiled=True)
        total = total + jnp.dot(
            left.reshape(local_rows, width),
            right,
            precision=lax.Precision.HIGH,
            preferred_element_type=jnp.float32,
        )
    keep = jnp.broadcast_to(
        c_pattern.astype(jnp.float32)[:, None, :, None],
        (block_rows, BLK, columns // BLK, BLK),
    ).reshape(local_rows, columns)
    merged = lax.psum_scatter(total, "fiber", scatter_dimension=0, tiled=True)
    product = merged * lax.dynamic_slice_in_dim(keep, lax.axis_index("fiber") * share, share, 0)
    inflated = product * product
    sums = all_sum(all_sum(jnp.sum(inflated, axis=0, keepdims=True), "fiber"), "row")
    return inflated / (sums / (share * fibers * n_row) + EPS)


def split(value):
    high = value.astype(jnp.bfloat16)
    low = (value - high.astype(jnp.float32)).astype(jnp.bfloat16)
    return high, low


def product3(a_high, a_low, b_high, b_low):
    def dot(x, y):
        return jnp.dot(x, y, preferred_element_type=jnp.float32)

    return dot(a_high, b_high) + (dot(a_high, b_low) + dot(a_low, b_high))


def left_kernel(groups, plan, pattern, other_pattern, *refs):
    sources, outs, turned = refs[: len(plan)], refs[len(plan) : -1], refs[-1]
    _, _, sections, width = sources[0].shape
    n_row, row, col = lax.axis_size("row"), lax.axis_index("row"), lax.axis_index("col")
    depth = width // n_row
    done = 0
    for source, (which, is_peer, first) in zip(sources, plan, strict=True):
        position = 1 - col if is_peer else col
        for g in range(source.shape[0] // UNIT):
            part = pl.ds(g * UNIT, UNIT)
            block_row = (position * (3 * UNIT) + first + g * UNIT) // BLK
            for s in range(sections):
                kept = []
                for w in range(width // BLK):
                    keep = (pattern, other_pattern)[which][block_row, 0, s, w]
                    kept.append(jnp.where(keep != 0, source[part, 0, s, pl.ds(w * BLK, BLK)], 0.0))
                value = jnp.concatenate(kept, axis=1)
                for r in range(n_row):
                    turned[r, s] = value[:, r * depth : (r + 1) * depth]
            place = pl.ds(done, UNIT)
            for i, members in enumerate(groups):
                owners = [line_at(row // 2, step) * 2 + (row + turn) % 2 for step, turn in members]
                pieces = [turned[r, s] for r in owners for s in range(sections)]
                high, low = split(jnp.concatenate(pieces, axis=1))
                outs[2 * i][place, :] = high
                outs[2 * i + 1][place, :] = low
            done += UNIT


def put_shards(shards, b_high, b_low):
    _, sections, depth, _ = shards[0].shape
    for i in range(len(shards) * sections):
        part = pl.ds(i * depth, depth)
        b_high[part, :], b_low[part, :] = split(shards[i // sections][0, i % sections])


def stacked(refs):
    return jnp.concatenate([ref[...] for ref in refs], axis=0)


def group_kernel(sets, sizes, *refs):
    lefts = refs[: 2 * sets * len(sizes)]
    rest = refs[len(lefts) :]
    shards, (*near, out, b_high, b_low) = rest[: sum(sizes)], rest[sum(sizes) :]
    put_shards(shards, b_high, b_low)
    total = near[0][...] if near else None
    first = 0
    for i in range(len(sizes)):
        group = lefts[2 * sets * i : 2 * sets * (i + 1)]
        high, low = stacked(group[:sets]), stacked(group[sets:])
        part = pl.ds(first, high.shape[1])
        value = product3(high, low, b_high[part, :], b_low[part, :])
        total = value if total is None else total + value
        first += high.shape[1]
    out[...] = total


def far_value(first, *refs):
    *lefts, near, near_late, shard, b_high, b_low = refs
    highs, lows = lefts[: len(lefts) // 2], lefts[len(lefts) // 2 :]
    put_shards([shard], b_high, b_low)
    value = product3(stacked(highs), stacked(lows), b_high[...], b_low[...])
    tile = slice(first, first + shard.shape[3])
    return value + jnp.concatenate([near[:, tile], near_late[:, tile]], axis=0)


def far_kernel(first, *refs):
    *ins, kept, sent, b_high, b_low = refs
    value = far_value(first, *ins, b_high, b_low)
    rows = kept.shape[1]
    flip = lax.axis_index("col") ^ lax.axis_index("fiber")
    for turn in range(2):

        @pl.when(flip == turn)
        def _():
            for p in range(4):
                y, x = divmod(p, 2)
                out = kept if x == turn else sent
                out[y] = value[p * rows : (p + 1) * rows]


def last_kernel(first, *refs):
    *ins, out, b_high, b_low = refs
    value = far_value(first, *ins, b_high, b_low)
    rows = out.shape[1]
    for p in range(4):
        out[p] = value[p * rows : (p + 1) * rows]


def squared(pattern, fiber, first, value):
    columns = value.shape[1]
    half = lax.axis_index("row") % 2 * (pattern.shape[1] // 2)
    out = []
    for g in range(value.shape[0] // UNIT):
        block_row = (fiber * value.shape[0] + g * UNIT) // BLK
        kept = []
        for w in range(columns // BLK):
            keep = pattern[block_row, half + first // BLK + w]
            piece = value[g * UNIT : (g + 1) * UNIT, w * BLK : (w + 1) * BLK]
            piece = jnp.where(keep != 0, piece, 0.0)
            kept.append(piece * piece)
        out.append(jnp.concatenate(kept, axis=1) if len(kept) > 1 else kept[0])
    return jnp.concatenate(out, axis=0)


def square_kernel(pattern, other_pattern, kept, received, stays, goes, sums):
    fiber = lax.axis_index("fiber")
    mine = squared(pattern, fiber, 0, kept[0] + received[0])
    other = squared(other_pattern, fiber, 0, kept[1] + received[1])
    stays[...], goes[...] = mine, other
    sums[...] = jnp.sum(mine, axis=0, keepdims=True) + jnp.sum(other, axis=0, keepdims=True)


def square_last_kernel(first, pattern, other_pattern, mine, received, early, stays, goes, sums):
    fiber, col = lax.axis_index("fiber"), lax.axis_index("col")
    total = None
    for y, (table, target) in enumerate(((pattern, stays), (other_pattern, goes))):
        for block in (1 - fiber, fiber):
            p = 2 * y + (block ^ col)
            value = squared(table, block, first, mine[p] + received[p])
            part = jnp.sum(value, axis=0, keepdims=True)
            total = part if total is None else total + part
        target[...] = value
    sums[:, :first] = early[...]
    sums[:, first:] = total


def scale_kernel(row_total, sums, other_sums, *refs):
    *parts, out = refs
    half = sums.shape[1]
    y = lax.axis_index("row") % 2
    for side, total, (early, last) in ((y, sums, parts[:2]), (1 - y, other_sums, parts[2:])):
        scale = total[...] / row_total + EPS
        cut = early.shape[1]
        out[:, pl.ds(pl.multiple_of(side * half, BLK), cut)] = early[...] / scale[:, :cut]
        out[:, pl.ds(pl.multiple_of(side * half + cut, BLK), half - cut)] = last[...] / scale[:, cut:]


def together(*values):
    return lax.optimization_barrier(values)


VMEM = pl.BlockSpec(memory_space=pltpu.VMEM)
SMEM = pl.BlockSpec(memory_space=pltpu.SMEM)


def call(kernel, out_shapes, specs, scratch=(), flops=0):
    def run(*args):
        moved = sum(a.size * a.dtype.itemsize for a in (*args, *out_shapes))
        return pl.pallas_call(
            kernel,
            out_shape=out_shapes,
            in_specs=specs,
            out_specs=[VMEM] * len(out_shapes),
            scratch_shapes=scratch,
            cost_estimate=pl.CostEstimate(flops=flops, bytes_accessed=moved, transcendentals=0),
            compiler_params=pltpu.CompilerParams(vmem_limit_bytes=16 * 2**20),
        )(*args)

    return run


def local(a_panels, b_panels, a_pattern, c_pattern):
    rows, _, sections, _ = a_panels.shape
    depth, columns = b_panels.shape[2:]
    n_row, n_col, fibers = (lax.axis_size(name) for name in ("row", "col", "fiber"))
    local_rows = rows * n_col
    share = local_rows // fibers
    if (n_row, n_col, fibers, sections, rows, columns) != (8, 2, 2, 2, 3 * UNIT, 1024):
        return gathered(a_panels, b_panels, a_pattern, c_pattern)

    f32, bf16 = jnp.float32, jnp.bfloat16
    shape = jax.ShapeDtypeStruct
    half = columns // 2
    cut = half - LAST
    my_y = lax.axis_index("row") & 1
    swap = [(0, 1), (1, 0)]
    swap_y = [(r, r ^ 1) for r in range(n_row)]

    def columns_half(side):
        where = (0, 0, 0, side * half)
        sizes = (*b_panels.shape[:3], half)
        return lax.dynamic_slice(b_panels, where, sizes, allow_negative_indices=False)

    own = columns_half(my_y)
    b_panels, own = together(b_panels, own)
    shards = {(0, 0): own}
    shards[0, 1] = lax.ppermute(columns_half(1 - my_y), "row", swap_y)
    for turn in range(2):
        shards[-1, turn] = lax.ppermute(shards[0, turn], "row", line_pairs(1))
        shards[1, turn] = lax.ppermute(shards[0, turn], "row", line_pairs(-1))
    shards[2, 0] = lax.ppermute(shards[-1, 0], "row", line_pairs(1))
    far_early = lax.ppermute(shards[-1, 1][..., :cut], "row", line_pairs(1))
    far_last = lax.ppermute(shards[-1, 1][..., cut:], "row", line_pairs(1))

    from_x = lax.ppermute(a_panels, "col", swap)
    y0, y1, y2 = (
        lax.ppermute(a_panels[u * UNIT : (u + 1) * UNIT], "row", swap_y) for u in range(3)
    )
    d2 = lax.ppermute(from_x[2 * UNIT :], "row", swap_y)
    d0 = lax.ppermute(y0, "col", swap)
    d1 = lax.ppermute(y1, "col", swap)
    a_tables = [a_pattern, lax.ppermute(a_pattern, "row", swap_y)]
    c_tables = [c_pattern, lax.ppermute(c_pattern, "row", swap_y)]

    groups = [[(0, 0), (0, 1), (-1, 0), (1, 0)], [(-1, 1), (1, 1), (2, 0)], [(2, 1)]]
    shard_depth = sections * depth

    def left(*sources):
        arrays = [source for source, *_ in sources]
        plan = tuple((y, x, first) for _, y, x, first in sources)
        count = sum(source.shape[0] for source in arrays)
        parts = [shape((count, len(m) * shard_depth), bf16) for m in groups for _ in range(2)]
        return call(
            functools.partial(left_kernel, groups, plan),
            parts,
            [SMEM] * 2 + [VMEM] * len(arrays),
            [pltpu.VMEM((n_row, sections, UNIT, depth), f32)],
        )(a_pattern, a_tables[max(y for y, *_ in plan)], *arrays)

    early_sets = [
        left((a_panels, 0, False, 0)), left((from_x, 0, True, 0)), left((y0, 1, False, 0), (y1, 1, False, UNIT))
    ]

    def picked(sets, g):
        return [s[2 * g] for s in sets] + [s[2 * g + 1] for s in sets]

    def product(sets, which, *near):
        lefts = [part for g in which for part in picked(sets, g)]
        members = [shards[m] for g in which for m in groups[g]]
        count = sum(s[0].shape[0] for s in sets)
        factor = pltpu.VMEM((len(members) * shard_depth, half), bf16)
        (total,) = call(
            functools.partial(group_kernel, len(sets), tuple(len(groups[g]) for g in which)),
            [shape((count, half), f32)],
            [VMEM] * (len(lefts) + len(members) + len(near)),
            [factor, factor],
            6 * count * half * len(members) * shard_depth,
        )(*lefts, *members, *near)
        return total

    near = product(early_sets, [1], product(early_sets, [0]))
    d2, d1, near = together(d2, d1, near)
    late_sets = [
        left((y2, 1, False, 2 * UNIT)), left((d0, 1, True, 0)), left((d1, 1, True, UNIT)), left((d2, 1, True, 2 * UNIT))
    ]
    near_late = product(late_sets, [0, 1])

    far_lefts = picked([*early_sets, *late_sets], 2)

    def far(kernel, first, shard, outs):
        factor = pltpu.VMEM((shard_depth, shard.shape[3]), bf16)
        return call(
            functools.partial(kernel, first),
            outs,
            [VMEM] * (len(far_lefts) + 3),
            [factor, factor],
            6 * 4 * rows * shard.shape[3] * shard_depth,
        )(*far_lefts, near, near_late, shard)

    kept, sent = far(far_kernel, 0, far_early, [shape((2, rows, cut), f32)] * 2)
    received = lax.ppermute(sent, "fiber", swap)
    (mine,) = far(last_kernel, cut, far_last, [shape((4, rows, LAST), f32)])
    theirs = lax.ppermute(mine, "fiber", swap)
    stays, goes, sums = call(
        square_kernel, [shape((rows, cut), f32)] * 2 + [shape((1, cut), f32)], [SMEM, SMEM, VMEM, VMEM]
    )(*c_tables, kept, received)
    comes = lax.ppermute(goes, "row", swap_y)
    sums = sums + lax.ppermute(sums, "fiber", swap)
    last_stays, last_goes, sums = call(
        functools.partial(square_last_kernel, cut),
        [shape((rows, LAST), f32)] * 2 + [shape((1, half), f32)],
        [SMEM, SMEM, VMEM, VMEM, VMEM],
    )(*c_tables, mine, theirs, sums)
    last_comes = lax.ppermute(last_goes, "row", swap_y)
    for bit in (2, 4):
        sums = sums + lax.ppermute(sums, "row", [(r, r ^ bit) for r in range(n_row)])
    other_sums = lax.ppermute(sums, "row", swap_y)
    (out,) = call(
        functools.partial(scale_kernel, share * fibers * n_row), [shape((share, columns), f32)], [VMEM] * 6
    )(sums, other_sums, stays, last_stays, comes, last_comes)
    return out


def solution(mesh):
    placed = (
        P(("row", "col"), "fiber", None, None),
        P("fiber", None, "row", "col"),
        P("row", "fiber", None, None),
        P("row", "col"),
    )

    return jax.shard_map(local, mesh=mesh, in_specs=placed, out_specs=P(("row", "fiber"), "col"), check_vma=False)
```

```python
import functools

import jax
import jax.numpy as jnp
from jax import lax
from jax.experimental import pallas as pl
from jax.experimental.pallas import tpu as pltpu
from jax.sharding import PartitionSpec as P


BLK = 128


EPS = 1e-06
LAST = 128
UNIT = 64


LINE = (0, 1, 3, 2)


def line_pairs(shift):
    size = len(LINE)
    return [
        (LINE[i] * 2 + y, LINE[(i + shift) % size] * 2 + y) for i in range(size) for y in range(2)
    ]


def line_at(z, step):
    place = jnp.where(z < 2, z, 5 - z)
    place = (place + step + len(LINE)) % len(LINE)
    return jnp.where(place < 2, place, 5 - place)


def all_sum(value, axis_name):
    size = lax.axis_size(axis_name)
    stride = 1
    while stride < size:
        rest = size // stride
        radix = next(p for p in range(2, rest + 1) if rest % p == 0)
        total = value
        for turn in range(1, radix):
            pairs = []
            for i in range(size):
                digit = i // stride % radix
                pairs.append((i, i + ((digit + turn) % radix - digit) * stride))
            total = total + lax.ppermute(value, axis_name, pairs)
        value = total
        stride *= radix
    return value


def gathered(a_panels, b_panels, a_pattern, c_pattern):
    _, _, sections, width = a_panels.shape
    block_rows, width_blocks = a_pattern.shape[0], a_pattern.shape[3]
    columns = b_panels.shape[3]
    local_rows = block_rows * BLK
    n_row, fibers = lax.axis_size("row"), lax.axis_size("fiber")
    share = local_rows // fibers
    total = jnp.zeros((local_rows, columns), jnp.float32)
    for section in range(sections):
        block = lax.all_gather(a_panels[:, 0, section, :], "col", axis=0, tiled=True)
        keep = a_pattern[:, 0, section, :].astype(jnp.float32)
        left = block.reshape(block_rows, BLK, width_blocks, BLK) * keep[:, None, :, None]
        right = lax.all_gather(b_panels[0, section], "row", axis=0, tiled=True)
        total = total + jnp.dot(
            left.reshape(local_rows, width),
            right,
            precision=lax.Precision.HIGH,
            preferred_element_type=jnp.float32,
        )
    keep = jnp.broadcast_to(
        c_pattern.astype(jnp.float32)[:, None, :, None],
        (block_rows, BLK, columns // BLK, BLK),
    ).reshape(local_rows, columns)
    merged = lax.psum_scatter(total, "fiber", scatter_dimension=0, tiled=True)
    product = merged * lax.dynamic_slice_in_dim(keep, lax.axis_index("fiber") * share, share, 0)
    inflated = product * product
    sums = all_sum(all_sum(jnp.sum(inflated, axis=0, keepdims=True), "fiber"), "row")
    return inflated / (sums / (share * fibers * n_row) + EPS)


def split(value):
    high = value.astype(jnp.bfloat16)
    low = (value - high.astype(jnp.float32)).astype(jnp.bfloat16)
    return high, low


def product3(a_high, a_low, b_high, b_low):
    def dot(x, y):
        return jnp.dot(x, y, preferred_element_type=jnp.float32)

    return dot(a_high, b_high) + (dot(a_high, b_low) + dot(a_low, b_high))


def left_kernel(groups, plan, pattern, other_pattern, *refs):
    sources, outs, turned = refs[: len(plan)], refs[len(plan) : -1], refs[-1]
    _, _, sections, width = sources[0].shape
    n_row, row, col = lax.axis_size("row"), lax.axis_index("row"), lax.axis_index("col")
    depth = width // n_row
    done = 0
    for source, (which, is_peer, first) in zip(sources, plan, strict=True):
        position = 1 - col if is_peer else col
        for g in range(source.shape[0] // UNIT):
            part = pl.ds(g * UNIT, UNIT)
            block_row = (position * (3 * UNIT) + first + g * UNIT) // BLK
            for s in range(sections):
                kept = []
                for w in range(width // BLK):
                    keep = (pattern, other_pattern)[which][block_row, 0, s, w]
                    kept.append(jnp.where(keep != 0, source[part, 0, s, pl.ds(w * BLK, BLK)], 0.0))
                value = jnp.concatenate(kept, axis=1)
                for r in range(n_row):
                    turned[r, s] = value[:, r * depth : (r + 1) * depth]
            place = pl.ds(done, UNIT)
            for i, members in enumerate(groups):
                owners = [line_at(row // 2, step) * 2 + (row + turn) % 2 for step, turn in members]
                pieces = [turned[r, s] for r in owners for s in range(sections)]
                high, low = split(jnp.concatenate(pieces, axis=1))
                outs[2 * i][place, :] = high
                outs[2 * i + 1][place, :] = low
            done += UNIT


def put_shards(shards, b_high, b_low):
    _, sections, depth, _ = shards[0].shape
    for i in range(len(shards) * sections):
        part = pl.ds(i * depth, depth)
        b_high[part, :], b_low[part, :] = split(shards[i // sections][0, i % sections])


def stacked(refs):
    return jnp.concatenate([ref[...] for ref in refs], axis=0)


def split_kernel(*refs):
    *shards, high, low = refs
    put_shards(shards, high, low)


def group_kernel(sets, groups, *refs):
    lefts, rights, out = refs[: 2 * sets * groups], refs[2 * sets * groups : -1], refs[-1]
    total = None
    for i in range(groups):
        group = lefts[2 * sets * i : 2 * sets * (i + 1)]
        right = rights[2 * i : 2 * i + 2]
        value = product3(stacked(group[:sets]), stacked(group[sets:]), right[0][...], right[1][...])
        total = value if total is None else total + value
    out[...] = total


def far_value(first, *refs):
    *lefts, near, near_late, shard, b_high, b_low = refs
    highs, lows = lefts[: len(lefts) // 2], lefts[len(lefts) // 2 :]
    put_shards([shard], b_high, b_low)
    value = product3(stacked(highs), stacked(lows), b_high[...], b_low[...])
    tile = slice(first, first + shard.shape[3])
    return value + jnp.concatenate([near[:, tile], near_late[:, tile]], axis=0)


def far_kernel(first, *refs):
    *ins, kept, sent, b_high, b_low = refs
    value = far_value(first, *ins, b_high, b_low)
    rows = kept.shape[1]
    flip = lax.axis_index("col") ^ lax.axis_index("fiber")
    for turn in range(2):

        @pl.when(flip == turn)
        def _():
            for p in range(4):
                y, x = divmod(p, 2)
                out = kept if x == turn else sent
                out[y] = value[p * rows : (p + 1) * rows]


def last_kernel(first, *refs):
    *ins, out, b_high, b_low = refs
    value = far_value(first, *ins, b_high, b_low)
    rows = out.shape[1]
    for p in range(4):
        out[p] = value[p * rows : (p + 1) * rows]


def squared(pattern, fiber, first, value):
    columns = value.shape[1]
    half = lax.axis_index("row") % 2 * (pattern.shape[1] // 2)
    out = []
    for g in range(value.shape[0] // UNIT):
        block_row = (fiber * value.shape[0] + g * UNIT) // BLK
        kept = []
        for w in range(columns // BLK):
            keep = pattern[block_row, half + first // BLK + w]
            piece = value[g * UNIT : (g + 1) * UNIT, w * BLK : (w + 1) * BLK]
            piece = jnp.where(keep != 0, piece, 0.0)
            kept.append(piece * piece)
        out.append(jnp.concatenate(kept, axis=1) if len(kept) > 1 else kept[0])
    return jnp.concatenate(out, axis=0)


def square_kernel(pattern, other_pattern, kept, received, stays, goes, sums):
    fiber = lax.axis_index("fiber")
    mine = squared(pattern, fiber, 0, kept[0] + received[0])
    other = squared(other_pattern, fiber, 0, kept[1] + received[1])
    stays[...], goes[...] = mine, other
    sums[...] = jnp.sum(mine, axis=0, keepdims=True) + jnp.sum(other, axis=0, keepdims=True)


def square_last_kernel(first, pattern, other_pattern, mine, received, early, stays, goes, sums):
    fiber, col = lax.axis_index("fiber"), lax.axis_index("col")
    total = None
    for y, (table, target) in enumerate(((pattern, stays), (other_pattern, goes))):
        for block in (1 - fiber, fiber):
            p = 2 * y + (block ^ col)
            value = squared(table, block, first, mine[p] + received[p])
            part = jnp.sum(value, axis=0, keepdims=True)
            total = part if total is None else total + part
        target[...] = value
    sums[:, :first] = early[...]
    sums[:, first:] = total


def scale_kernel(row_total, sums, other_sums, *refs):
    *parts, out = refs
    half = sums.shape[1]
    y = lax.axis_index("row") % 2
    for side, total, (early, last) in ((y, sums, parts[:2]), (1 - y, other_sums, parts[2:])):
        scale = total[...] / row_total + EPS
        cut = early.shape[1]
        out[:, pl.ds(pl.multiple_of(side * half, BLK), cut)] = early[...] / scale[:, :cut]
        out[:, pl.ds(pl.multiple_of(side * half + cut, BLK), half - cut)] = last[...] / scale[:, cut:]


def together(*values):
    return lax.optimization_barrier(values)


VMEM = pl.BlockSpec(memory_space=pltpu.VMEM)
SMEM = pl.BlockSpec(memory_space=pltpu.SMEM)


def call(kernel, out_shapes, specs, scratch=(), flops=0):
    def run(*args):
        moved = sum(a.size * a.dtype.itemsize for a in (*args, *out_shapes))
        return pl.pallas_call(
            kernel,
            out_shape=out_shapes,
            in_specs=specs,
            out_specs=[VMEM] * len(out_shapes),
            scratch_shapes=scratch,
            cost_estimate=pl.CostEstimate(flops=flops, bytes_accessed=moved, transcendentals=0),
            compiler_params=pltpu.CompilerParams(vmem_limit_bytes=16 * 2**20),
        )(*args)

    return run


def local(a_panels, b_panels, a_pattern, c_pattern):
    rows, _, sections, _ = a_panels.shape
    depth, columns = b_panels.shape[2:]
    n_row, n_col, fibers = (lax.axis_size(name) for name in ("row", "col", "fiber"))
    local_rows = rows * n_col
    share = local_rows // fibers
    if (n_row, n_col, fibers, sections, rows, columns) != (8, 2, 2, 2, 3 * UNIT, 1024):
        return gathered(a_panels, b_panels, a_pattern, c_pattern)

    f32, bf16 = jnp.float32, jnp.bfloat16
    shape = jax.ShapeDtypeStruct
    half = columns // 2
    cut = half - LAST
    my_y = lax.axis_index("row") & 1
    swap = [(0, 1), (1, 0)]
    swap_y = [(r, r ^ 1) for r in range(n_row)]

    def columns_half(side):
        where = (0, 0, 0, side * half)
        sizes = (*b_panels.shape[:3], half)
        return lax.dynamic_slice(b_panels, where, sizes, allow_negative_indices=False)

    own = columns_half(my_y)
    b_panels, own = together(b_panels, own)
    shards = {(0, 0): own}
    shards[0, 1] = lax.ppermute(columns_half(1 - my_y), "row", swap_y)
    for turn in range(2):
        shards[-1, turn] = lax.ppermute(shards[0, turn], "row", line_pairs(1))
        shards[1, turn] = lax.ppermute(shards[0, turn], "row", line_pairs(-1))
    shards[2, 0] = lax.ppermute(shards[-1, 0], "row", line_pairs(1))
    far_early = lax.ppermute(shards[-1, 1][..., :cut], "row", line_pairs(1))
    far_last = lax.ppermute(shards[-1, 1][..., cut:], "row", line_pairs(1))

    from_x = lax.ppermute(a_panels, "col", swap)
    y0, y1, y2 = (
        lax.ppermute(a_panels[u * UNIT : (u + 1) * UNIT], "row", swap_y) for u in range(3)
    )
    d2 = lax.ppermute(from_x[2 * UNIT :], "row", swap_y)
    d0 = lax.ppermute(y0, "col", swap)
    d1 = lax.ppermute(y1, "col", swap)
    a_tables = [a_pattern, lax.ppermute(a_pattern, "row", swap_y)]
    c_tables = [c_pattern, lax.ppermute(c_pattern, "row", swap_y)]

    groups = [[(0, 0), (0, 1), (-1, 0), (1, 0)], [(-1, 1), (1, 1), (2, 0)], [(2, 1)]]
    shard_depth = sections * depth

    def left(*sources):
        arrays = [source for source, *_ in sources]
        plan = tuple((y, x, first) for _, y, x, first in sources)
        count = sum(source.shape[0] for source in arrays)
        parts = [shape((count, len(m) * shard_depth), bf16) for m in groups for _ in range(2)]
        return call(
            functools.partial(left_kernel, groups, plan),
            parts,
            [SMEM] * 2 + [VMEM] * len(arrays),
            [pltpu.VMEM((n_row, sections, UNIT, depth), f32)],
        )(a_pattern, a_tables[max(y for y, *_ in plan)], *arrays)

    early_sets = [
        left((a_panels, 0, False, 0)), left((from_x, 0, True, 0)), left((y0, 1, False, 0), (y1, 1, False, UNIT))
    ]

    def picked(sets, g):
        return [s[2 * g] for s in sets] + [s[2 * g + 1] for s in sets]

    rights = []
    for g in range(2):
        members = [shards[m] for m in groups[g]]
        rights += call(
            split_kernel, [shape((len(members) * shard_depth, half), bf16)] * 2, [VMEM] * len(members)
        )(*members)

    def product(sets):
        lefts = [part for g in range(2) for part in picked(sets, g)]
        count = sum(s[0].shape[0] for s in sets)
        (total,) = call(
            functools.partial(group_kernel, len(sets), 2),
            [shape((count, half), f32)],
            [VMEM] * (len(lefts) + len(rights)),
            flops=6 * count * half * 7 * shard_depth,
        )(*lefts, *rights)
        return total

    early_sets += [left((y2, 1, False, 2 * UNIT)), left((d0, 1, True, 0))]
    near = product(early_sets)
    d2, d1, near = together(d2, d1, near)
    late_sets = [left((d1, 1, True, UNIT)), left((d2, 1, True, 2 * UNIT))]
    near_late = product(late_sets)

    far_lefts = picked([*early_sets, *late_sets], 2)

    def far(kernel, first, shard, outs):
        factor = pltpu.VMEM((shard_depth, shard.shape[3]), bf16)
        return call(
            functools.partial(kernel, first),
            outs,
            [VMEM] * (len(far_lefts) + 3),
            [factor, factor],
            6 * 4 * rows * shard.shape[3] * shard_depth,
        )(*far_lefts, near, near_late, shard)

    kept, sent = far(far_kernel, 0, far_early, [shape((2, rows, cut), f32)] * 2)
    received = lax.ppermute(sent, "fiber", swap)
    (mine,) = far(last_kernel, cut, far_last, [shape((4, rows, LAST), f32)])
    theirs = lax.ppermute(mine, "fiber", swap)
    stays, goes, sums = call(
        square_kernel, [shape((rows, cut), f32)] * 2 + [shape((1, cut), f32)], [SMEM, SMEM, VMEM, VMEM]
    )(*c_tables, kept, received)
    comes = lax.ppermute(goes, "row", swap_y)
    sums = sums + lax.ppermute(sums, "fiber", swap)
    last_stays, last_goes, sums = call(
        functools.partial(square_last_kernel, cut),
        [shape((rows, LAST), f32)] * 2 + [shape((1, half), f32)],
        [SMEM, SMEM, VMEM, VMEM, VMEM],
    )(*c_tables, mine, theirs, sums)
    last_comes = lax.ppermute(last_goes, "row", swap_y)
    for bit in (2, 4):
        sums = sums + lax.ppermute(sums, "row", [(r, r ^ bit) for r in range(n_row)])
    other_sums = lax.ppermute(sums, "row", swap_y)
    (out,) = call(
        functools.partial(scale_kernel, share * fibers * n_row), [shape((share, columns), f32)], [VMEM] * 6
    )(sums, other_sums, stays, last_stays, comes, last_comes)
    return out


def solution(mesh):
    placed = (
        P(("row", "col"), "fiber", None, None),
        P("fiber", None, "row", "col"),
        P("row", "fiber", None, None),
        P("row", "col"),
    )

    return jax.shard_map(local, mesh=mesh, in_specs=placed, out_specs=P(("row", "fiber"), "col"), check_vma=False)
```

```python
import functools

import jax
import jax.numpy as jnp
from jax import lax
from jax.experimental import pallas as pl
from jax.experimental.pallas import tpu as pltpu
from jax.sharding import PartitionSpec as P


BLK = 128


EPS = 1e-06
LAST = 128
UNIT = 64


LINE = (0, 1, 3, 2)


def line_pairs(shift):
    size = len(LINE)
    return [
        (LINE[i] * 2 + y, LINE[(i + shift) % size] * 2 + y) for i in range(size) for y in range(2)
    ]


def line_at(z, step):
    place = jnp.where(z < 2, z, 5 - z)
    place = (place + step + len(LINE)) % len(LINE)
    return jnp.where(place < 2, place, 5 - place)


def all_sum(value, axis_name):
    size = lax.axis_size(axis_name)
    stride = 1
    while stride < size:
        rest = size // stride
        radix = next(p for p in range(2, rest + 1) if rest % p == 0)
        total = value
        for turn in range(1, radix):
            pairs = []
            for i in range(size):
                digit = i // stride % radix
                pairs.append((i, i + ((digit + turn) % radix - digit) * stride))
            total = total + lax.ppermute(value, axis_name, pairs)
        value = total
        stride *= radix
    return value


def gathered(a_panels, b_panels, a_pattern, c_pattern):
    _, _, sections, width = a_panels.shape
    block_rows, width_blocks = a_pattern.shape[0], a_pattern.shape[3]
    columns = b_panels.shape[3]
    local_rows = block_rows * BLK
    n_row, fibers = lax.axis_size("row"), lax.axis_size("fiber")
    share = local_rows // fibers
    total = jnp.zeros((local_rows, columns), jnp.float32)
    for section in range(sections):
        block = lax.all_gather(a_panels[:, 0, section, :], "col", axis=0, tiled=True)
        keep = a_pattern[:, 0, section, :].astype(jnp.float32)
        left = block.reshape(block_rows, BLK, width_blocks, BLK) * keep[:, None, :, None]
        right = lax.all_gather(b_panels[0, section], "row", axis=0, tiled=True)
        total = total + jnp.dot(
            left.reshape(local_rows, width),
            right,
            precision=lax.Precision.HIGH,
            preferred_element_type=jnp.float32,
        )
    keep = jnp.broadcast_to(
        c_pattern.astype(jnp.float32)[:, None, :, None],
        (block_rows, BLK, columns // BLK, BLK),
    ).reshape(local_rows, columns)
    merged = lax.psum_scatter(total, "fiber", scatter_dimension=0, tiled=True)
    product = merged * lax.dynamic_slice_in_dim(keep, lax.axis_index("fiber") * share, share, 0)
    inflated = product * product
    sums = all_sum(all_sum(jnp.sum(inflated, axis=0, keepdims=True), "fiber"), "row")
    return inflated / (sums / (share * fibers * n_row) + EPS)


def split(value):
    high = value.astype(jnp.bfloat16)
    low = (value - high.astype(jnp.float32)).astype(jnp.bfloat16)
    return high, low


def product3(a_high, a_low, b_high, b_low):
    def dot(x, y):
        return jnp.dot(x, y, preferred_element_type=jnp.float32)

    return dot(a_high, b_high) + (dot(a_high, b_low) + dot(a_low, b_high))


def left_kernel(groups, plan, pattern, other_pattern, *refs):
    sources, outs, turned = refs[: len(plan)], refs[len(plan) : -1], refs[-1]
    _, _, sections, width = sources[0].shape
    n_row, row, col = lax.axis_size("row"), lax.axis_index("row"), lax.axis_index("col")
    depth = width // n_row
    done = 0
    for source, (which, is_peer, first) in zip(sources, plan, strict=True):
        position = 1 - col if is_peer else col
        for g in range(source.shape[0] // UNIT):
            part = pl.ds(g * UNIT, UNIT)
            block_row = (position * (3 * UNIT) + first + g * UNIT) // BLK
            for s in range(sections):
                kept = []
                for w in range(width // BLK):
                    keep = (pattern, other_pattern)[which][block_row, 0, s, w]
                    kept.append(jnp.where(keep != 0, source[part, 0, s, pl.ds(w * BLK, BLK)], 0.0))
                value = jnp.concatenate(kept, axis=1)
                for r in range(n_row):
                    turned[r, s] = value[:, r * depth : (r + 1) * depth]
            place = pl.ds(done, UNIT)
            for i, members in enumerate(groups):
                owners = [line_at(row // 2, step) * 2 + (row + turn) % 2 for step, turn in members]
                pieces = [turned[r, s] for r in owners for s in range(sections)]
                high, low = split(jnp.concatenate(pieces, axis=1))
                outs[2 * i][place, :] = high
                outs[2 * i + 1][place, :] = low
            done += UNIT


def put_shards(shards, b_high, b_low, tiles=None):
    _, sections, depth, _ = shards[0].shape
    for i in range(len(shards) * sections):
        part = pl.ds(i * depth, depth)
        tile = tiles[i // sections] if tiles else slice(None)
        b_high[part, :], b_low[part, :] = split(shards[i // sections][0, i % sections, :, tile])


def stacked(refs):
    return jnp.concatenate([ref[...] for ref in refs], axis=0)


def split_kernel(*refs):
    *shards, high, low = refs
    put_shards(shards, high, low)


def group_kernel(sets, groups, *refs):
    lefts, rights, out = refs[: 2 * sets * groups], refs[2 * sets * groups : -1], refs[-1]
    total = None
    for i in range(groups):
        group = lefts[2 * sets * i : 2 * sets * (i + 1)]
        right = rights[2 * i : 2 * i + 2]
        value = product3(stacked(group[:sets]), stacked(group[sets:]), right[0][...], right[1][...])
        total = value if total is None else total + value
    out[...] = total


def far_value(first, *refs):
    *lefts, near, near_late, hop, shard, b_high, b_low = refs
    highs, lows = lefts[: len(lefts) // 2], lefts[len(lefts) // 2 :]
    tile = slice(first, first + shard.shape[3])
    put_shards([hop, shard], b_high, b_low, [tile, slice(None)])
    value = product3(stacked(highs), stacked(lows), b_high[...], b_low[...])
    return value + jnp.concatenate([near[:, tile], near_late[:, tile]], axis=0)


def far_kernel(first, *refs):
    *ins, kept, sent, b_high, b_low = refs
    value = far_value(first, *ins, b_high, b_low)
    rows = kept.shape[1]
    flip = lax.axis_index("col") ^ lax.axis_index("fiber")
    for turn in range(2):

        @pl.when(flip == turn)
        def _():
            for p in range(4):
                y, x = divmod(p, 2)
                out = kept if x == turn else sent
                out[y] = value[p * rows : (p + 1) * rows]


def last_kernel(first, *refs):
    *ins, out, b_high, b_low = refs
    value = far_value(first, *ins, b_high, b_low)
    rows = out.shape[1]
    for p in range(4):
        out[p] = value[p * rows : (p + 1) * rows]


def squared(pattern, fiber, first, value):
    columns = value.shape[1]
    half = lax.axis_index("row") % 2 * (pattern.shape[1] // 2)
    out = []
    for g in range(value.shape[0] // UNIT):
        block_row = (fiber * value.shape[0] + g * UNIT) // BLK
        kept = []
        for w in range(columns // BLK):
            keep = pattern[block_row, half + first // BLK + w]
            piece = value[g * UNIT : (g + 1) * UNIT, w * BLK : (w + 1) * BLK]
            piece = jnp.where(keep != 0, piece, 0.0)
            kept.append(piece * piece)
        out.append(jnp.concatenate(kept, axis=1) if len(kept) > 1 else kept[0])
    return jnp.concatenate(out, axis=0)


def square_kernel(pattern, other_pattern, kept, received, stays, goes, sums):
    fiber = lax.axis_index("fiber")
    mine = squared(pattern, fiber, 0, kept[0] + received[0])
    other = squared(other_pattern, fiber, 0, kept[1] + received[1])
    stays[...], goes[...] = mine, other
    sums[...] = jnp.sum(mine, axis=0, keepdims=True) + jnp.sum(other, axis=0, keepdims=True)


def square_last_kernel(first, pattern, other_pattern, mine, received, early, stays, goes, sums):
    fiber, col = lax.axis_index("fiber"), lax.axis_index("col")
    total = None
    for y, (table, target) in enumerate(((pattern, stays), (other_pattern, goes))):
        for block in (1 - fiber, fiber):
            p = 2 * y + (block ^ col)
            value = squared(table, block, first, mine[p] + received[p])
            part = jnp.sum(value, axis=0, keepdims=True)
            total = part if total is None else total + part
        target[...] = value
    sums[:, :first] = early[...]
    sums[:, first:] = total


def scale_kernel(row_total, sums, other_sums, *refs):
    *parts, out = refs
    half = sums.shape[1]
    y = lax.axis_index("row") % 2
    for side, total, (early, last) in ((y, sums, parts[:2]), (1 - y, other_sums, parts[2:])):
        scale = total[...] / row_total + EPS
        cut = early.shape[1]
        out[:, pl.ds(pl.multiple_of(side * half, BLK), cut)] = early[...] / scale[:, :cut]
        out[:, pl.ds(pl.multiple_of(side * half + cut, BLK), half - cut)] = last[...] / scale[:, cut:]


def together(*values):
    return lax.optimization_barrier(values)


VMEM = pl.BlockSpec(memory_space=pltpu.VMEM)
SMEM = pl.BlockSpec(memory_space=pltpu.SMEM)


def call(kernel, out_shapes, specs, scratch=(), flops=0):
    def run(*args):
        moved = sum(a.size * a.dtype.itemsize for a in (*args, *out_shapes))
        return pl.pallas_call(
            kernel,
            out_shape=out_shapes,
            in_specs=specs,
            out_specs=[VMEM] * len(out_shapes),
            scratch_shapes=scratch,
            cost_estimate=pl.CostEstimate(flops=flops, bytes_accessed=moved, transcendentals=0),
            compiler_params=pltpu.CompilerParams(vmem_limit_bytes=16 * 2**20),
        )(*args)

    return run


def local(a_panels, b_panels, a_pattern, c_pattern):
    rows, _, sections, _ = a_panels.shape
    depth, columns = b_panels.shape[2:]
    n_row, n_col, fibers = (lax.axis_size(name) for name in ("row", "col", "fiber"))
    local_rows = rows * n_col
    share = local_rows // fibers
    if (n_row, n_col, fibers, sections, rows, columns) != (8, 2, 2, 2, 3 * UNIT, 1024):
        return gathered(a_panels, b_panels, a_pattern, c_pattern)

    f32, bf16 = jnp.float32, jnp.bfloat16
    shape = jax.ShapeDtypeStruct
    half = columns // 2
    cut = half - LAST
    my_y = lax.axis_index("row") & 1
    swap = [(0, 1), (1, 0)]
    swap_y = [(r, r ^ 1) for r in range(n_row)]

    def columns_half(side):
        where = (0, 0, 0, side * half)
        sizes = (*b_panels.shape[:3], half)
        return lax.dynamic_slice(b_panels, where, sizes, allow_negative_indices=False)

    own = columns_half(my_y)
    b_panels, own = together(b_panels, own)
    shards = {(0, 0): own}
    shards[0, 1] = lax.ppermute(columns_half(1 - my_y), "row", swap_y)
    for turn in range(2):
        shards[-1, turn] = lax.ppermute(shards[0, turn], "row", line_pairs(1))
        shards[1, turn] = lax.ppermute(shards[0, turn], "row", line_pairs(-1))
    shards[2, 0] = lax.ppermute(shards[-1, 0], "row", line_pairs(1))
    far_early = lax.ppermute(shards[-1, 1][..., :cut], "row", line_pairs(1))
    far_last = lax.ppermute(shards[-1, 1][..., cut:], "row", line_pairs(1))

    from_x = lax.ppermute(a_panels, "col", swap)
    y0, y1, y2 = (
        lax.ppermute(a_panels[u * UNIT : (u + 1) * UNIT], "row", swap_y) for u in range(3)
    )
    d2 = lax.ppermute(from_x[2 * UNIT :], "row", swap_y)
    d0 = lax.ppermute(y0, "col", swap)
    d1 = lax.ppermute(y1, "col", swap)
    a_tables = [a_pattern, lax.ppermute(a_pattern, "row", swap_y)]
    c_tables = [c_pattern, lax.ppermute(c_pattern, "row", swap_y)]

    groups = [[(0, 0), (0, 1), (-1, 0), (1, 0)], [(-1, 1), (1, 1)], [(2, 0), (2, 1)]]
    shard_depth = sections * depth

    def left(*sources):
        arrays = [source for source, *_ in sources]
        plan = tuple((y, x, first) for _, y, x, first in sources)
        count = sum(source.shape[0] for source in arrays)
        parts = [shape((count, len(m) * shard_depth), bf16) for m in groups for _ in range(2)]
        return call(
            functools.partial(left_kernel, groups, plan),
            parts,
            [SMEM] * 2 + [VMEM] * len(arrays),
            [pltpu.VMEM((n_row, sections, UNIT, depth), f32)],
        )(a_pattern, a_tables[max(y for y, *_ in plan)], *arrays)

    early_sets = [
        left((a_panels, 0, False, 0)), left((from_x, 0, True, 0)), left((y0, 1, False, 0)), left((y1, 1, False, UNIT))
    ]

    def picked(sets, g):
        return [s[2 * g] for s in sets] + [s[2 * g + 1] for s in sets]

    rights = []
    for g in range(2):
        members = [shards[m] for m in groups[g]]
        rights += call(
            split_kernel, [shape((len(members) * shard_depth, half), bf16)] * 2, [VMEM] * len(members)
        )(*members)

    def product(sets):
        lefts = [part for g in range(2) for part in picked(sets, g)]
        count = sum(s[0].shape[0] for s in sets)
        (total,) = call(
            functools.partial(group_kernel, len(sets), 2),
            [shape((count, half), f32)],
            [VMEM] * (len(lefts) + len(rights)),
            flops=6 * count * half * 6 * shard_depth,
        )(*lefts, *rights)
        return total

    early_sets += [left((y2, 1, False, 2 * UNIT)), left((d0, 1, True, 0))]
    near = product(early_sets)
    d2, d1, near = together(d2, d1, near)
    late_sets = [left((d1, 1, True, UNIT))]
    d2, late_sets[0] = together(d2, late_sets[0])
    late_sets.append(left((d2, 1, True, 2 * UNIT)))
    near_late = product(late_sets)

    far_lefts = picked([*early_sets, *late_sets], 2)

    def far(kernel, first, shard, outs):
        factor = pltpu.VMEM((2 * shard_depth, shard.shape[3]), bf16)
        return call(
            functools.partial(kernel, first),
            outs,
            [VMEM] * (len(far_lefts) + 4),
            [factor, factor],
            6 * 4 * rows * shard.shape[3] * 2 * shard_depth,
        )(*far_lefts, near, near_late, shards[2, 0], shard)

    kept, sent = far(far_kernel, 0, far_early, [shape((2, rows, cut), f32)] * 2)
    received = lax.ppermute(sent, "fiber", swap)
    (mine,) = far(last_kernel, cut, far_last, [shape((4, rows, LAST), f32)])
    theirs = lax.ppermute(mine, "fiber", swap)
    stays, goes, sums = call(
        square_kernel, [shape((rows, cut), f32)] * 2 + [shape((1, cut), f32)], [SMEM, SMEM, VMEM, VMEM]
    )(*c_tables, kept, received)
    comes = lax.ppermute(goes, "row", swap_y)
    sums = sums + lax.ppermute(sums, "fiber", swap)
    last_stays, last_goes, sums = call(
        functools.partial(square_last_kernel, cut),
        [shape((rows, LAST), f32)] * 2 + [shape((1, half), f32)],
        [SMEM, SMEM, VMEM, VMEM, VMEM],
    )(*c_tables, mine, theirs, sums)
    last_comes = lax.ppermute(last_goes, "row", swap_y)
    for bit in (2, 4):
        sums = sums + lax.ppermute(sums, "row", [(r, r ^ bit) for r in range(n_row)])
    other_sums = lax.ppermute(sums, "row", swap_y)
    (out,) = call(
        functools.partial(scale_kernel, share * fibers * n_row), [shape((share, columns), f32)], [VMEM] * 6
    )(sums, other_sums, stays, last_stays, comes, last_comes)
    return out


def solution(mesh):
    placed = (
        P(("row", "col"), "fiber", None, None),
        P("fiber", None, "row", "col"),
        P("row", "fiber", None, None),
        P("row", "col"),
    )

    return jax.shard_map(local, mesh=mesh, in_specs=placed, out_specs=P(("row", "fiber"), "col"), check_vma=False)
```

```python
import functools

import jax
import jax.numpy as jnp
from jax import lax
from jax.experimental import pallas as pl
from jax.experimental.pallas import tpu as pltpu
from jax.sharding import PartitionSpec as P


BLK = 128


EPS = 1e-06
LAST = 128
UNIT = 64


LINE = (0, 1, 3, 2)


def line_pairs(shift):
    size = len(LINE)
    return [
        (LINE[i] * 2 + y, LINE[(i + shift) % size] * 2 + y) for i in range(size) for y in range(2)
    ]


def line_at(z, step):
    place = jnp.where(z < 2, z, 5 - z)
    place = (place + step + len(LINE)) % len(LINE)
    return jnp.where(place < 2, place, 5 - place)


def all_sum(value, axis_name):
    size = lax.axis_size(axis_name)
    stride = 1
    while stride < size:
        rest = size // stride
        radix = next(p for p in range(2, rest + 1) if rest % p == 0)
        total = value
        for turn in range(1, radix):
            pairs = []
            for i in range(size):
                digit = i // stride % radix
                pairs.append((i, i + ((digit + turn) % radix - digit) * stride))
            total = total + lax.ppermute(value, axis_name, pairs)
        value = total
        stride *= radix
    return value


def gathered(a_panels, b_panels, a_pattern, c_pattern):
    _, _, sections, width = a_panels.shape
    block_rows, width_blocks = a_pattern.shape[0], a_pattern.shape[3]
    columns = b_panels.shape[3]
    local_rows = block_rows * BLK
    n_row, fibers = lax.axis_size("row"), lax.axis_size("fiber")
    share = local_rows // fibers
    total = jnp.zeros((local_rows, columns), jnp.float32)
    for section in range(sections):
        block = lax.all_gather(a_panels[:, 0, section, :], "col", axis=0, tiled=True)
        keep = a_pattern[:, 0, section, :].astype(jnp.float32)
        left = block.reshape(block_rows, BLK, width_blocks, BLK) * keep[:, None, :, None]
        right = lax.all_gather(b_panels[0, section], "row", axis=0, tiled=True)
        total = total + jnp.dot(
            left.reshape(local_rows, width),
            right,
            precision=lax.Precision.HIGH,
            preferred_element_type=jnp.float32,
        )
    keep = jnp.broadcast_to(
        c_pattern.astype(jnp.float32)[:, None, :, None],
        (block_rows, BLK, columns // BLK, BLK),
    ).reshape(local_rows, columns)
    merged = lax.psum_scatter(total, "fiber", scatter_dimension=0, tiled=True)
    product = merged * lax.dynamic_slice_in_dim(keep, lax.axis_index("fiber") * share, share, 0)
    inflated = product * product
    sums = all_sum(all_sum(jnp.sum(inflated, axis=0, keepdims=True), "fiber"), "row")
    return inflated / (sums / (share * fibers * n_row) + EPS)


def split(value):
    high = value.astype(jnp.bfloat16)
    low = (value - high.astype(jnp.float32)).astype(jnp.bfloat16)
    return high, low


def product3(a_high, a_low, b_high, b_low):
    def dot(x, y):
        return jnp.dot(x, y, preferred_element_type=jnp.float32)

    return dot(a_high, b_high) + (dot(a_high, b_low) + dot(a_low, b_high))


def left_kernel(groups, plan, pattern, other_pattern, *refs):
    sources, outs, turned = refs[: len(plan)], refs[len(plan) : -1], refs[-1]
    _, _, sections, width = sources[0].shape
    n_row, row, col = lax.axis_size("row"), lax.axis_index("row"), lax.axis_index("col")
    depth = width // n_row
    done = 0
    for source, (which, is_peer, first) in zip(sources, plan, strict=True):
        position = 1 - col if is_peer else col
        for g in range(source.shape[0] // UNIT):
            part = pl.ds(g * UNIT, UNIT)
            block_row = (position * (3 * UNIT) + first + g * UNIT) // BLK
            for s in range(sections):
                kept = []
                for w in range(width // BLK):
                    keep = (pattern, other_pattern)[which][block_row, 0, s, w]
                    kept.append(jnp.where(keep != 0, source[part, 0, s, pl.ds(w * BLK, BLK)], 0.0))
                value = jnp.concatenate(kept, axis=1)
                for r in range(n_row):
                    turned[r, s] = value[:, r * depth : (r + 1) * depth]
            place = pl.ds(done, UNIT)
            for i, members in enumerate(groups):
                owners = [line_at(row // 2, step) * 2 + (row + turn) % 2 for step, turn in members]
                pieces = [turned[r, s] for r in owners for s in range(sections)]
                high, low = split(jnp.concatenate(pieces, axis=1))
                outs[2 * i][place, :] = high
                outs[2 * i + 1][place, :] = low
            done += UNIT


def put_shards(shards, b_high, b_low):
    _, sections, depth, _ = shards[0].shape
    for i in range(len(shards) * sections):
        part = pl.ds(i * depth, depth)
        b_high[part, :], b_low[part, :] = split(shards[i // sections][0, i % sections])


def stacked(refs):
    return jnp.concatenate([ref[...] for ref in refs], axis=0)


def split_kernel(*refs):
    *shards, high, low = refs
    put_shards(shards, high, low)


def group_kernel(sets, groups, *refs):
    lefts, rights, out = refs[: 2 * sets * groups], refs[2 * sets * groups : -1], refs[-1]
    total = None
    for i in range(groups):
        group = lefts[2 * sets * i : 2 * sets * (i + 1)]
        right = rights[2 * i : 2 * i + 2]
        value = product3(stacked(group[:sets]), stacked(group[sets:]), right[0][...], right[1][...])
        total = value if total is None else total + value
    out[...] = total


def hop_kernel(sets, *refs):
    lefts, (*nears, shard, out, b_high, b_low) = refs[: 2 * sets], refs[2 * sets :]
    put_shards([shard], b_high, b_low)
    value = product3(stacked(lefts[:sets]), stacked(lefts[sets:]), b_high[...], b_low[...])
    out[...] = value + stacked(nears)


def far_value(first, *refs):
    *lefts, near, shard, b_high, b_low = refs
    highs, lows = lefts[: len(lefts) // 2], lefts[len(lefts) // 2 :]
    put_shards([shard], b_high, b_low)
    value = product3(stacked(highs), stacked(lows), b_high[...], b_low[...])
    return value + near[:, first : first + shard.shape[3]]


def far_kernel(first, *refs):
    *ins, kept, sent, b_high, b_low = refs
    value = far_value(first, *ins, b_high, b_low)
    rows = kept.shape[1]
    flip = lax.axis_index("col") ^ lax.axis_index("fiber")
    for turn in range(2):

        @pl.when(flip == turn)
        def _():
            for p in range(4):
                y, x = divmod(p, 2)
                out = kept if x == turn else sent
                out[y] = value[p * rows : (p + 1) * rows]


def last_kernel(first, *refs):
    *ins, out, b_high, b_low = refs
    value = far_value(first, *ins, b_high, b_low)
    rows = out.shape[1]
    for p in range(4):
        out[p] = value[p * rows : (p + 1) * rows]


def squared(pattern, fiber, first, value):
    columns = value.shape[1]
    half = lax.axis_index("row") % 2 * (pattern.shape[1] // 2)
    out = []
    for g in range(value.shape[0] // UNIT):
        block_row = (fiber * value.shape[0] + g * UNIT) // BLK
        kept = []
        for w in range(columns // BLK):
            keep = pattern[block_row, half + first // BLK + w]
            piece = value[g * UNIT : (g + 1) * UNIT, w * BLK : (w + 1) * BLK]
            piece = jnp.where(keep != 0, piece, 0.0)
            kept.append(piece * piece)
        out.append(jnp.concatenate(kept, axis=1) if len(kept) > 1 else kept[0])
    return jnp.concatenate(out, axis=0)


def square_kernel(pattern, other_pattern, kept, received, stays, goes, sums):
    fiber = lax.axis_index("fiber")
    mine = squared(pattern, fiber, 0, kept[0] + received[0])
    other = squared(other_pattern, fiber, 0, kept[1] + received[1])
    stays[...], goes[...] = mine, other
    sums[...] = jnp.sum(mine, axis=0, keepdims=True) + jnp.sum(other, axis=0, keepdims=True)


def square_last_kernel(first, pattern, other_pattern, mine, received, early, stays, goes, sums):
    fiber, col = lax.axis_index("fiber"), lax.axis_index("col")
    total = None
    for y, (table, target) in enumerate(((pattern, stays), (other_pattern, goes))):
        for block in (1 - fiber, fiber):
            p = 2 * y + (block ^ col)
            value = squared(table, block, first, mine[p] + received[p])
            part = jnp.sum(value, axis=0, keepdims=True)
            total = part if total is None else total + part
        target[...] = value
    sums[:, :first] = early[...]
    sums[:, first:] = total


def scale_kernel(row_total, sums, other_sums, *refs):
    *parts, out = refs
    half = sums.shape[1]
    y = lax.axis_index("row") % 2
    for side, total, (early, last) in ((y, sums, parts[:2]), (1 - y, other_sums, parts[2:])):
        scale = total[...] / row_total + EPS
        cut = early.shape[1]
        out[:, pl.ds(pl.multiple_of(side * half, BLK), cut)] = early[...] / scale[:, :cut]
        out[:, pl.ds(pl.multiple_of(side * half + cut, BLK), half - cut)] = last[...] / scale[:, cut:]


def together(*values):
    return lax.optimization_barrier(values)


VMEM = pl.BlockSpec(memory_space=pltpu.VMEM)
SMEM = pl.BlockSpec(memory_space=pltpu.SMEM)


def call(kernel, out_shapes, specs, scratch=(), flops=0):
    def run(*args):
        moved = sum(a.size * a.dtype.itemsize for a in (*args, *out_shapes))
        return pl.pallas_call(
            kernel,
            out_shape=out_shapes,
            in_specs=specs,
            out_specs=[VMEM] * len(out_shapes),
            scratch_shapes=scratch,
            cost_estimate=pl.CostEstimate(flops=flops, bytes_accessed=moved, transcendentals=0),
            compiler_params=pltpu.CompilerParams(vmem_limit_bytes=16 * 2**20),
        )(*args)

    return run


def local(a_panels, b_panels, a_pattern, c_pattern):
    rows, _, sections, _ = a_panels.shape
    depth, columns = b_panels.shape[2:]
    n_row, n_col, fibers = (lax.axis_size(name) for name in ("row", "col", "fiber"))
    local_rows = rows * n_col
    share = local_rows // fibers
    if (n_row, n_col, fibers, sections, rows, columns) != (8, 2, 2, 2, 3 * UNIT, 1024):
        return gathered(a_panels, b_panels, a_pattern, c_pattern)

    f32, bf16 = jnp.float32, jnp.bfloat16
    shape = jax.ShapeDtypeStruct
    half = columns // 2
    cut = half - LAST
    my_y = lax.axis_index("row") & 1
    swap = [(0, 1), (1, 0)]
    swap_y = [(r, r ^ 1) for r in range(n_row)]

    def columns_half(side):
        where = (0, 0, 0, side * half)
        sizes = (*b_panels.shape[:3], half)
        return lax.dynamic_slice(b_panels, where, sizes, allow_negative_indices=False)

    own = columns_half(my_y)
    b_panels, own = together(b_panels, own)
    shards = {(0, 0): own}
    shards[0, 1] = lax.ppermute(columns_half(1 - my_y), "row", swap_y)
    for turn in range(2):
        shards[-1, turn] = lax.ppermute(shards[0, turn], "row", line_pairs(1))
        shards[1, turn] = lax.ppermute(shards[0, turn], "row", line_pairs(-1))
    shards[2, 0] = lax.ppermute(shards[-1, 0], "row", line_pairs(1))
    far_early = lax.ppermute(shards[-1, 1][..., :cut], "row", line_pairs(1))
    far_last = lax.ppermute(shards[-1, 1][..., cut:], "row", line_pairs(1))

    from_x = lax.ppermute(a_panels, "col", swap)
    y0, y1, y2 = (
        lax.ppermute(a_panels[u * UNIT : (u + 1) * UNIT], "row", swap_y) for u in range(3)
    )
    d2 = lax.ppermute(from_x[2 * UNIT :], "row", swap_y)
    d0 = lax.ppermute(y0, "col", swap)
    d1 = lax.ppermute(y1, "col", swap)
    a_tables = [a_pattern, lax.ppermute(a_pattern, "row", swap_y)]
    c_tables = [c_pattern, lax.ppermute(c_pattern, "row", swap_y)]

    groups = [[(0, 0), (0, 1), (-1, 0), (1, 0)], [(-1, 1), (1, 1)], [(2, 0)], [(2, 1)]]
    shard_depth = sections * depth

    def left(*sources):
        arrays = [source for source, *_ in sources]
        plan = tuple((y, x, first) for _, y, x, first in sources)
        count = sum(source.shape[0] for source in arrays)
        parts = [shape((count, len(m) * shard_depth), bf16) for m in groups for _ in range(2)]
        return call(
            functools.partial(left_kernel, groups, plan),
            parts,
            [SMEM] * 2 + [VMEM] * len(arrays),
            [pltpu.VMEM((n_row, sections, UNIT, depth), f32)],
        )(a_pattern, a_tables[max(y for y, *_ in plan)], *arrays)

    early_sets = [
        left((a_panels, 0, False, 0)),
        left((from_x, 0, True, 0)),
        left((y0, 1, False, 0)),
        left((y1, 1, False, UNIT)),
    ]

    def picked(sets, g):
        return [s[2 * g] for s in sets] + [s[2 * g + 1] for s in sets]

    rights = []
    for g in range(2):
        members = [shards[m] for m in groups[g]]
        rights += call(
            split_kernel,
            [shape((len(members) * shard_depth, half), bf16)] * 2,
            [VMEM] * len(members),
        )(*members)

    def product(sets):
        lefts = [part for g in range(2) for part in picked(sets, g)]
        count = sum(s[0].shape[0] for s in sets)
        (total,) = call(
            functools.partial(group_kernel, len(sets), 2),
            [shape((count, half), f32)],
            [VMEM] * (len(lefts) + len(rights)),
            flops=6 * count * half * 6 * shard_depth,
        )(*lefts, *rights)
        return total

    early_sets += [left((y2, 1, False, 2 * UNIT)), left((d0, 1, True, 0))]
    near = product(early_sets)
    d2, d1, near = together(d2, d1, near)
    late_sets = [left((d1, 1, True, UNIT))]
    d2, late_sets[0] = together(d2, late_sets[0])
    late_sets.append(left((d2, 1, True, 2 * UNIT)))
    near_late = product(late_sets)

    all_sets = [*early_sets, *late_sets]
    hop_lefts = picked(all_sets, 2)
    factor = pltpu.VMEM((shard_depth, half), bf16)
    (near,) = call(
        functools.partial(hop_kernel, len(all_sets)),
        [shape((4 * rows, half), f32)],
        [VMEM] * (len(hop_lefts) + 3),
        [factor, factor],
        6 * 4 * rows * half * shard_depth,
    )(*hop_lefts, near, near_late, shards[2, 0])

    far_lefts = picked(all_sets, 3)

    def far(kernel, first, shard, outs):
        factor = pltpu.VMEM((shard_depth, shard.shape[3]), bf16)
        return call(
            functools.partial(kernel, first),
            outs,
            [VMEM] * (len(far_lefts) + 2),
            [factor, factor],
            6 * 4 * rows * shard.shape[3] * shard_depth,
        )(*far_lefts, near, shard)

    kept, sent = far(far_kernel, 0, far_early, [shape((2, rows, cut), f32)] * 2)
    received = lax.ppermute(sent, "fiber", swap)
    (mine,) = far(last_kernel, cut, far_last, [shape((4, rows, LAST), f32)])
    theirs = lax.ppermute(mine, "fiber", swap)
    stays, goes, sums = call(
        square_kernel,
        [shape((rows, cut), f32)] * 2 + [shape((1, cut), f32)],
        [SMEM, SMEM, VMEM, VMEM],
    )(*c_tables, kept, received)
    comes = lax.ppermute(goes, "row", swap_y)
    sums = sums + lax.ppermute(sums, "fiber", swap)
    last_stays, last_goes, sums = call(
        functools.partial(square_last_kernel, cut),
        [shape((rows, LAST), f32)] * 2 + [shape((1, half), f32)],
        [SMEM, SMEM, VMEM, VMEM, VMEM],
    )(*c_tables, mine, theirs, sums)
    last_comes = lax.ppermute(last_goes, "row", swap_y)
    for bit in (2, 4):
        sums = sums + lax.ppermute(sums, "row", [(r, r ^ bit) for r in range(n_row)])
    other_sums = lax.ppermute(sums, "row", swap_y)
    (out,) = call(
        functools.partial(scale_kernel, share * fibers * n_row),
        [shape((share, columns), f32)],
        [VMEM] * 6,
    )(sums, other_sums, stays, last_stays, comes, last_comes)
    return out


def solution(mesh):
    placed = (
        P(("row", "col"), "fiber", None, None),
        P("fiber", None, "row", "col"),
        P("row", "fiber", None, None),
        P("row", "col"),
    )

    return jax.shard_map(
        local, mesh=mesh, in_specs=placed, out_specs=P(("row", "fiber"), "col"), check_vma=False
    )
```

```python
import functools

import jax
import jax.numpy as jnp
from jax import lax
from jax.experimental import pallas as pl
from jax.experimental.pallas import tpu as pltpu
from jax.sharding import PartitionSpec as P


BLK = 128


EPS = 1e-06
LAST = 128
UNIT = 64


LINE = (0, 1, 3, 2)


def line_pairs(shift):
    size = len(LINE)
    return [
        (LINE[i] * 2 + y, LINE[(i + shift) % size] * 2 + y) for i in range(size) for y in range(2)
    ]


def line_at(z, step):
    place = jnp.where(z < 2, z, 5 - z)
    place = (place + step + len(LINE)) % len(LINE)
    return jnp.where(place < 2, place, 5 - place)


def all_sum(value, axis_name):
    size = lax.axis_size(axis_name)
    stride = 1
    while stride < size:
        rest = size // stride
        radix = next(p for p in range(2, rest + 1) if rest % p == 0)
        total = value
        for turn in range(1, radix):
            pairs = []
            for i in range(size):
                digit = i // stride % radix
                pairs.append((i, i + ((digit + turn) % radix - digit) * stride))
            total = total + lax.ppermute(value, axis_name, pairs)
        value = total
        stride *= radix
    return value


def gathered(a_panels, b_panels, a_pattern, c_pattern):
    _, _, sections, width = a_panels.shape
    block_rows, width_blocks = a_pattern.shape[0], a_pattern.shape[3]
    columns = b_panels.shape[3]
    local_rows = block_rows * BLK
    n_row, fibers = lax.axis_size("row"), lax.axis_size("fiber")
    share = local_rows // fibers
    total = jnp.zeros((local_rows, columns), jnp.float32)
    for section in range(sections):
        block = lax.all_gather(a_panels[:, 0, section, :], "col", axis=0, tiled=True)
        keep = a_pattern[:, 0, section, :].astype(jnp.float32)
        left = block.reshape(block_rows, BLK, width_blocks, BLK) * keep[:, None, :, None]
        right = lax.all_gather(b_panels[0, section], "row", axis=0, tiled=True)
        total = total + jnp.dot(
            left.reshape(local_rows, width),
            right,
            precision=lax.Precision.HIGH,
            preferred_element_type=jnp.float32,
        )
    keep = jnp.broadcast_to(
        c_pattern.astype(jnp.float32)[:, None, :, None],
        (block_rows, BLK, columns // BLK, BLK),
    ).reshape(local_rows, columns)
    merged = lax.psum_scatter(total, "fiber", scatter_dimension=0, tiled=True)
    product = merged * lax.dynamic_slice_in_dim(keep, lax.axis_index("fiber") * share, share, 0)
    inflated = product * product
    sums = all_sum(all_sum(jnp.sum(inflated, axis=0, keepdims=True), "fiber"), "row")
    return inflated / (sums / (share * fibers * n_row) + EPS)


def split(value):
    high = value.astype(jnp.bfloat16)
    low = (value - high.astype(jnp.float32)).astype(jnp.bfloat16)
    return high, low


def product3(a_high, a_low, b_high, b_low):
    def dot(x, y):
        return jnp.dot(x, y, preferred_element_type=jnp.float32)

    return dot(a_high, b_high) + (dot(a_high, b_low) + dot(a_low, b_high))


def left_kernel(groups, plan, pattern, other_pattern, *refs):
    sources, outs, turned = refs[: len(plan)], refs[len(plan) : -1], refs[-1]
    _, _, sections, width = sources[0].shape
    n_row, row, col = lax.axis_size("row"), lax.axis_index("row"), lax.axis_index("col")
    depth = width // n_row
    done = 0
    for source, (which, is_peer, first) in zip(sources, plan, strict=True):
        position = 1 - col if is_peer else col
        for g in range(source.shape[0] // UNIT):
            part = pl.ds(g * UNIT, UNIT)
            block_row = (position * (3 * UNIT) + first + g * UNIT) // BLK
            for s in range(sections):
                kept = []
                for w in range(width // BLK):
                    keep = (pattern, other_pattern)[which][block_row, 0, s, w]
                    kept.append(jnp.where(keep != 0, source[part, 0, s, pl.ds(w * BLK, BLK)], 0.0))
                value = jnp.concatenate(kept, axis=1)
                for r in range(n_row):
                    turned[r, s] = value[:, r * depth : (r + 1) * depth]
            place = pl.ds(done, UNIT)
            for i, members in enumerate(groups):
                owners = [line_at(row // 2, step) * 2 + (row + turn) % 2 for step, turn in members]
                pieces = [turned[r, s] for r in owners for s in range(sections)]
                high, low = split(jnp.concatenate(pieces, axis=1))
                outs[2 * i][place, :] = high
                outs[2 * i + 1][place, :] = low
            done += UNIT


def put_shards(shards, b_high, b_low):
    _, sections, depth, _ = shards[0].shape
    for i in range(len(shards) * sections):
        part = pl.ds(i * depth, depth)
        b_high[part, :], b_low[part, :] = split(shards[i // sections][0, i % sections])


def stacked(refs):
    return jnp.concatenate([ref[...] for ref in refs], axis=0)


def split_kernel(*refs):
    *shards, high, low = refs
    put_shards(shards, high, low)


def group_kernel(sets, groups, *refs):
    lefts, rights, out = refs[: 2 * sets * groups], refs[2 * sets * groups : -1], refs[-1]
    total = None
    for i in range(groups):
        group = lefts[2 * sets * i : 2 * sets * (i + 1)]
        right = rights[2 * i : 2 * i + 2]
        value = product3(stacked(group[:sets]), stacked(group[sets:]), right[0][...], right[1][...])
        total = value if total is None else total + value
    out[...] = total


def hop_kernel(sets, *refs):
    lefts, (*nears, shard, out, b_high, b_low) = refs[: 2 * sets], refs[2 * sets :]
    put_shards([shard], b_high, b_low)
    value = product3(stacked(lefts[:sets]), stacked(lefts[sets:]), b_high[...], b_low[...])
    out[...] = value + stacked(nears)


def far_value(first, *refs):
    *lefts, near, shard, b_high, b_low = refs
    highs, lows = lefts[: len(lefts) // 2], lefts[len(lefts) // 2 :]
    put_shards([shard], b_high, b_low)
    value = product3(stacked(highs), stacked(lows), b_high[...], b_low[...])
    return value + near[:, first : first + shard.shape[3]]


def far_kernel(first, *refs):
    *ins, kept, sent, b_high, b_low = refs
    value = far_value(first, *ins, b_high, b_low)
    rows = kept.shape[1]
    flip = lax.axis_index("col") ^ lax.axis_index("fiber")
    for turn in range(2):

        @pl.when(flip == turn)
        def _():
            for p in range(4):
                y, x = divmod(p, 2)
                out = kept if x == turn else sent
                out[y] = value[p * rows : (p + 1) * rows]


def last_kernel(first, *refs):
    *ins, out, b_high, b_low = refs
    value = far_value(first, *ins, b_high, b_low)
    rows = out.shape[1]
    for p in range(4):
        out[p] = value[p * rows : (p + 1) * rows]


def squared(pattern, fiber, first, value):
    columns = value.shape[1]
    half = lax.axis_index("row") % 2 * (pattern.shape[1] // 2)
    out = []
    for g in range(value.shape[0] // UNIT):
        block_row = (fiber * value.shape[0] + g * UNIT) // BLK
        kept = []
        for w in range(columns // BLK):
            keep = pattern[block_row, half + first // BLK + w]
            piece = value[g * UNIT : (g + 1) * UNIT, w * BLK : (w + 1) * BLK]
            piece = jnp.where(keep != 0, piece, 0.0)
            kept.append(piece * piece)
        out.append(jnp.concatenate(kept, axis=1) if len(kept) > 1 else kept[0])
    return jnp.concatenate(out, axis=0)


def square_kernel(pattern, other_pattern, kept, received, stays, goes, sums):
    fiber = lax.axis_index("fiber")
    mine = squared(pattern, fiber, 0, kept[0] + received[0])
    other = squared(other_pattern, fiber, 0, kept[1] + received[1])
    stays[...], goes[...] = mine, other
    sums[...] = jnp.sum(mine, axis=0, keepdims=True) + jnp.sum(other, axis=0, keepdims=True)


def square_last_kernel(first, pattern, other_pattern, mine, received, early, stays, goes, sums):
    fiber, col = lax.axis_index("fiber"), lax.axis_index("col")
    total = None
    for y, (table, target) in enumerate(((pattern, stays), (other_pattern, goes))):
        for block in (1 - fiber, fiber):
            p = 2 * y + (block ^ col)
            value = squared(table, block, first, mine[p] + received[p])
            part = jnp.sum(value, axis=0, keepdims=True)
            total = part if total is None else total + part
        target[...] = value
    sums[:, :first] = early[...]
    sums[:, first:] = total


def scale_kernel(row_total, sums, other_sums, *refs):
    *parts, out = refs
    half = sums.shape[1]
    y = lax.axis_index("row") % 2
    for side, total, (early, last) in ((y, sums, parts[:2]), (1 - y, other_sums, parts[2:])):
        scale = total[...] / row_total + EPS
        cut = early.shape[1]
        out[:, pl.ds(pl.multiple_of(side * half, BLK), cut)] = early[...] / scale[:, :cut]
        out[:, pl.ds(pl.multiple_of(side * half + cut, BLK), half - cut)] = last[...] / scale[:, cut:]


def together(*values):
    return lax.optimization_barrier(values)


VMEM = pl.BlockSpec(memory_space=pltpu.VMEM)
SMEM = pl.BlockSpec(memory_space=pltpu.SMEM)


def call(kernel, out_shapes, specs, scratch=(), flops=0):
    def run(*args):
        moved = sum(a.size * a.dtype.itemsize for a in (*args, *out_shapes))
        return pl.pallas_call(
            kernel,
            out_shape=out_shapes,
            in_specs=specs,
            out_specs=[VMEM] * len(out_shapes),
            scratch_shapes=scratch,
            cost_estimate=pl.CostEstimate(flops=flops, bytes_accessed=moved, transcendentals=0),
            compiler_params=pltpu.CompilerParams(vmem_limit_bytes=16 * 2**20),
        )(*args)

    return run


def local(a_panels, b_panels, a_pattern, c_pattern):
    rows, _, sections, _ = a_panels.shape
    depth, columns = b_panels.shape[2:]
    n_row, n_col, fibers = (lax.axis_size(name) for name in ("row", "col", "fiber"))
    local_rows = rows * n_col
    share = local_rows // fibers
    if (n_row, n_col, fibers, sections, rows, columns) != (8, 2, 2, 2, 3 * UNIT, 1024):
        return gathered(a_panels, b_panels, a_pattern, c_pattern)

    f32, bf16 = jnp.float32, jnp.bfloat16
    shape = jax.ShapeDtypeStruct
    half = columns // 2
    cut = half - LAST
    my_y = lax.axis_index("row") & 1
    swap = [(0, 1), (1, 0)]
    swap_y = [(r, r ^ 1) for r in range(n_row)]

    def columns_half(side):
        where = (0, 0, 0, side * half)
        sizes = (*b_panels.shape[:3], half)
        return lax.dynamic_slice(b_panels, where, sizes, allow_negative_indices=False)

    own = columns_half(my_y)
    b_panels, own = together(b_panels, own)
    shards = {(0, 0): own}
    shards[0, 1] = lax.ppermute(columns_half(1 - my_y), "row", swap_y)
    for turn in range(2):
        shards[-1, turn] = lax.ppermute(shards[0, turn], "row", line_pairs(1))
        shards[1, turn] = lax.ppermute(shards[0, turn], "row", line_pairs(-1))
    shards[2, 0] = lax.ppermute(shards[-1, 0], "row", line_pairs(1))
    far_early = lax.ppermute(shards[-1, 1][..., :cut], "row", line_pairs(1))
    far_last = lax.ppermute(shards[-1, 1][..., cut:], "row", line_pairs(1))

    from_x = lax.ppermute(a_panels, "col", swap)
    y0, y1, y2 = (
        lax.ppermute(a_panels[u * UNIT : (u + 1) * UNIT], "row", swap_y) for u in range(3)
    )
    d2 = lax.ppermute(from_x[2 * UNIT :], "row", swap_y)
    d0 = lax.ppermute(y0, "col", swap)
    d1 = lax.ppermute(y1, "col", swap)
    a_tables = [a_pattern, lax.ppermute(a_pattern, "row", swap_y)]
    c_tables = [c_pattern, lax.ppermute(c_pattern, "row", swap_y)]

    groups = [[(0, 0), (0, 1), (-1, 0), (1, 0)], [(-1, 1), (1, 1)], [(2, 0)], [(2, 1)]]
    shard_depth = sections * depth

    def left(*sources):
        arrays = [source for source, *_ in sources]
        plan = tuple((y, x, first) for _, y, x, first in sources)
        count = sum(source.shape[0] for source in arrays)
        parts = [shape((count, len(m) * shard_depth), bf16) for m in groups for _ in range(2)]
        return call(
            functools.partial(left_kernel, groups, plan),
            parts,
            [SMEM] * 2 + [VMEM] * len(arrays),
            [pltpu.VMEM((n_row, sections, UNIT, depth), f32)],
        )(a_pattern, a_tables[max(y for y, *_ in plan)], *arrays)

    early_sets = [
        left((a_panels, 0, False, 0)),
        left((from_x, 0, True, 0)),
        left((y0, 1, False, 0)),
        left((y1, 1, False, UNIT)),
    ]

    def picked(sets, g):
        return [s[2 * g] for s in sets] + [s[2 * g + 1] for s in sets]

    rights = []
    for g in range(2):
        members = [shards[m] for m in groups[g]]
        rights += call(
            split_kernel,
            [shape((len(members) * shard_depth, half), bf16)] * 2,
            [VMEM] * len(members),
        )(*members)

    def product(sets):
        lefts = [part for g in range(2) for part in picked(sets, g)]
        count = sum(s[0].shape[0] for s in sets)
        (total,) = call(
            functools.partial(group_kernel, len(sets), 2),
            [shape((count, half), f32)],
            [VMEM] * (len(lefts) + len(rights)),
            flops=6 * count * half * 6 * shard_depth,
        )(*lefts, *rights)
        return total

    early_sets.append(left((y2, 1, False, 2 * UNIT), (d0, 1, True, 0)))
    near = product(early_sets)
    d2, d1, near = together(d2, d1, near)
    late_sets = [left((d1, 1, True, UNIT), (d2, 1, True, 2 * UNIT))]
    near_late = product(late_sets)

    all_sets = [*early_sets, *late_sets]
    hop_lefts = picked(all_sets, 2)
    factor = pltpu.VMEM((shard_depth, half), bf16)
    (near,) = call(
        functools.partial(hop_kernel, len(all_sets)),
        [shape((4 * rows, half), f32)],
        [VMEM] * (len(hop_lefts) + 3),
        [factor, factor],
        6 * 4 * rows * half * shard_depth,
    )(*hop_lefts, near, near_late, shards[2, 0])

    far_lefts = picked(all_sets, 3)

    def far(kernel, first, shard, outs):
        factor = pltpu.VMEM((shard_depth, shard.shape[3]), bf16)
        return call(
            functools.partial(kernel, first),
            outs,
            [VMEM] * (len(far_lefts) + 2),
            [factor, factor],
            6 * 4 * rows * shard.shape[3] * shard_depth,
        )(*far_lefts, near, shard)

    kept, sent = far(far_kernel, 0, far_early, [shape((2, rows, cut), f32)] * 2)
    received = lax.ppermute(sent, "fiber", swap)
    (mine,) = far(last_kernel, cut, far_last, [shape((4, rows, LAST), f32)])
    theirs = lax.ppermute(mine, "fiber", swap)
    stays, goes, sums = call(
        square_kernel,
        [shape((rows, cut), f32)] * 2 + [shape((1, cut), f32)],
        [SMEM, SMEM, VMEM, VMEM],
    )(*c_tables, kept, received)
    comes = lax.ppermute(goes, "row", swap_y)
    sums = sums + lax.ppermute(sums, "fiber", swap)
    last_stays, last_goes, sums = call(
        functools.partial(square_last_kernel, cut),
        [shape((rows, LAST), f32)] * 2 + [shape((1, half), f32)],
        [SMEM, SMEM, VMEM, VMEM, VMEM],
    )(*c_tables, mine, theirs, sums)
    last_comes = lax.ppermute(last_goes, "row", swap_y)
    for bit in (2, 4):
        sums = sums + lax.ppermute(sums, "row", [(r, r ^ bit) for r in range(n_row)])
    other_sums = lax.ppermute(sums, "row", swap_y)
    (out,) = call(
        functools.partial(scale_kernel, share * fibers * n_row),
        [shape((share, columns), f32)],
        [VMEM] * 6,
    )(sums, other_sums, stays, last_stays, comes, last_comes)
    return out


def solution(mesh):
    placed = (
        P(("row", "col"), "fiber", None, None),
        P("fiber", None, "row", "col"),
        P("row", "fiber", None, None),
        P("row", "col"),
    )

    return jax.shard_map(
        local, mesh=mesh, in_specs=placed, out_specs=P(("row", "fiber"), "col"), check_vma=False
    )
```

```python
import functools

import jax
import jax.numpy as jnp
from jax import lax
from jax.experimental import pallas as pl
from jax.experimental.pallas import tpu as pltpu
from jax.sharding import PartitionSpec as P


BLK = 128


EPS = 1e-06
LAST = 128
UNIT = 64


def z_pairs(bits):
    return [(row, row ^ (2 * bits)) for row in range(8)]


def all_sum(value, axis_name):
    size = lax.axis_size(axis_name)
    stride = 1
    while stride < size:
        rest = size // stride
        radix = next(p for p in range(2, rest + 1) if rest % p == 0)
        total = value
        for turn in range(1, radix):
            pairs = []
            for i in range(size):
                digit = i // stride % radix
                pairs.append((i, i + ((digit + turn) % radix - digit) * stride))
            total = total + lax.ppermute(value, axis_name, pairs)
        value = total
        stride *= radix
    return value


def gathered(a_panels, b_panels, a_pattern, c_pattern):
    _, _, sections, width = a_panels.shape
    block_rows, width_blocks = a_pattern.shape[0], a_pattern.shape[3]
    columns = b_panels.shape[3]
    local_rows = block_rows * BLK
    n_row, fibers = lax.axis_size("row"), lax.axis_size("fiber")
    share = local_rows // fibers
    total = jnp.zeros((local_rows, columns), jnp.float32)
    for section in range(sections):
        block = lax.all_gather(a_panels[:, 0, section, :], "col", axis=0, tiled=True)
        keep = a_pattern[:, 0, section, :].astype(jnp.float32)
        left = block.reshape(block_rows, BLK, width_blocks, BLK) * keep[:, None, :, None]
        right = lax.all_gather(b_panels[0, section], "row", axis=0, tiled=True)
        total = total + jnp.dot(
            left.reshape(local_rows, width),
            right,
            precision=lax.Precision.HIGH,
            preferred_element_type=jnp.float32,
        )
    keep = jnp.broadcast_to(
        c_pattern.astype(jnp.float32)[:, None, :, None],
        (block_rows, BLK, columns // BLK, BLK),
    ).reshape(local_rows, columns)
    merged = lax.psum_scatter(total, "fiber", scatter_dimension=0, tiled=True)
    product = merged * lax.dynamic_slice_in_dim(keep, lax.axis_index("fiber") * share, share, 0)
    inflated = product * product
    sums = all_sum(all_sum(jnp.sum(inflated, axis=0, keepdims=True), "fiber"), "row")
    return inflated / (sums / (share * fibers * n_row) + EPS)


def split(value):
    high = value.astype(jnp.bfloat16)
    low = (value - high.astype(jnp.float32)).astype(jnp.bfloat16)
    return high, low


def product3(a_high, a_low, b_high, b_low):
    def dot(x, y):
        return jnp.dot(x, y, preferred_element_type=jnp.float32)

    return dot(a_high, b_high) + (dot(a_high, b_low) + dot(a_low, b_high))


def left_kernel(groups, plan, pattern, other_pattern, *refs):
    sources, outs, turned = refs[: len(plan)], refs[len(plan) : -1], refs[-1]
    _, _, sections, width = sources[0].shape
    n_row, row, col = lax.axis_size("row"), lax.axis_index("row"), lax.axis_index("col")
    depth = width // n_row
    done = 0
    for source, (which, is_peer, first) in zip(sources, plan, strict=True):
        position = 1 - col if is_peer else col
        for g in range(source.shape[0] // UNIT):
            part = pl.ds(g * UNIT, UNIT)
            block_row = (position * (3 * UNIT) + first + g * UNIT) // BLK
            for s in range(sections):
                kept = []
                for w in range(width // BLK):
                    keep = (pattern, other_pattern)[which][block_row, 0, s, w]
                    kept.append(jnp.where(keep != 0, source[part, 0, s, pl.ds(w * BLK, BLK)], 0.0))
                value = jnp.concatenate(kept, axis=1)
                for r in range(n_row):
                    turned[r, s] = value[:, r * depth : (r + 1) * depth]
            place = pl.ds(done, UNIT)
            for i, members in enumerate(groups):
                owners = [row ^ (2 * bits + turn) for bits, turn in members]
                pieces = [turned[r, s] for r in owners for s in range(sections)]
                high, low = split(jnp.concatenate(pieces, axis=1))
                outs[2 * i][place, :] = high
                outs[2 * i + 1][place, :] = low
            done += UNIT


def put_shards(shards, b_high, b_low):
    _, sections, depth, _ = shards[0].shape
    for i in range(len(shards) * sections):
        part = pl.ds(i * depth, depth)
        b_high[part, :], b_low[part, :] = split(shards[i // sections][0, i % sections])


def stacked(refs):
    return jnp.concatenate([ref[...] for ref in refs], axis=0)


def split_kernel(*refs):
    *shards, high, low = refs
    put_shards(shards, high, low)


def group_kernel(sets, groups, *refs):
    lefts, rights, out = refs[: 2 * sets * groups], refs[2 * sets * groups : -1], refs[-1]
    total = None
    for i in range(groups):
        group = lefts[2 * sets * i : 2 * sets * (i + 1)]
        right = rights[2 * i : 2 * i + 2]
        value = product3(stacked(group[:sets]), stacked(group[sets:]), right[0][...], right[1][...])
        total = value if total is None else total + value
    out[...] = total


def hop_kernel(sets, *refs):
    lefts, (*nears, shard, out, b_high, b_low) = refs[: 2 * sets], refs[2 * sets :]
    put_shards([shard], b_high, b_low)
    value = product3(stacked(lefts[:sets]), stacked(lefts[sets:]), b_high[...], b_low[...])
    out[...] = value + stacked(nears)


def far_value(first, *refs):
    *lefts, near, shard, b_high, b_low = refs
    highs, lows = lefts[: len(lefts) // 2], lefts[len(lefts) // 2 :]
    put_shards([shard], b_high, b_low)
    value = product3(stacked(highs), stacked(lows), b_high[...], b_low[...])
    return value + near[:, first : first + shard.shape[3]]


def far_kernel(first, *refs):
    *ins, kept, sent, b_high, b_low = refs
    value = far_value(first, *ins, b_high, b_low)
    rows = kept.shape[1]
    flip = lax.axis_index("col") ^ lax.axis_index("fiber")
    for turn in range(2):

        @pl.when(flip == turn)
        def _():
            for p in range(4):
                y, x = divmod(p, 2)
                out = kept if x == turn else sent
                out[y] = value[p * rows : (p + 1) * rows]


def last_kernel(first, *refs):
    *ins, out, b_high, b_low = refs
    value = far_value(first, *ins, b_high, b_low)
    rows = out.shape[1]
    for p in range(4):
        out[p] = value[p * rows : (p + 1) * rows]


def squared(pattern, fiber, first, value):
    columns = value.shape[1]
    half = lax.axis_index("row") % 2 * (pattern.shape[1] // 2)
    out = []
    for g in range(value.shape[0] // UNIT):
        block_row = (fiber * value.shape[0] + g * UNIT) // BLK
        kept = []
        for w in range(columns // BLK):
            keep = pattern[block_row, half + first // BLK + w]
            piece = value[g * UNIT : (g + 1) * UNIT, w * BLK : (w + 1) * BLK]
            piece = jnp.where(keep != 0, piece, 0.0)
            kept.append(piece * piece)
        out.append(jnp.concatenate(kept, axis=1) if len(kept) > 1 else kept[0])
    return jnp.concatenate(out, axis=0)


def square_kernel(pattern, other_pattern, kept, received, stays, goes, sums):
    fiber = lax.axis_index("fiber")
    mine = squared(pattern, fiber, 0, kept[0] + received[0])
    other = squared(other_pattern, fiber, 0, kept[1] + received[1])
    stays[...], goes[...] = mine, other
    sums[...] = jnp.sum(mine, axis=0, keepdims=True) + jnp.sum(other, axis=0, keepdims=True)


def square_last_kernel(first, pattern, other_pattern, mine, received, early, stays, goes, sums):
    fiber, col = lax.axis_index("fiber"), lax.axis_index("col")
    total = None
    for y, (table, target) in enumerate(((pattern, stays), (other_pattern, goes))):
        for block in (1 - fiber, fiber):
            p = 2 * y + (block ^ col)
            value = squared(table, block, first, mine[p] + received[p])
            part = jnp.sum(value, axis=0, keepdims=True)
            total = part if total is None else total + part
        target[...] = value
    sums[:, :first] = early[...]
    sums[:, first:] = total


def scale_kernel(row_total, sums, other_sums, *refs):
    *parts, out = refs
    half = sums.shape[1]
    y = lax.axis_index("row") % 2
    for side, total, (early, last) in ((y, sums, parts[:2]), (1 - y, other_sums, parts[2:])):
        scale = total[...] / row_total + EPS
        cut = early.shape[1]
        out[:, pl.ds(pl.multiple_of(side * half, BLK), cut)] = early[...] / scale[:, :cut]
        out[:, pl.ds(pl.multiple_of(side * half + cut, BLK), half - cut)] = last[...] / scale[:, cut:]


def together(*values):
    return lax.optimization_barrier(values)


VMEM = pl.BlockSpec(memory_space=pltpu.VMEM)
SMEM = pl.BlockSpec(memory_space=pltpu.SMEM)


def call(kernel, out_shapes, specs, scratch=(), flops=0):
    def run(*args):
        moved = sum(a.size * a.dtype.itemsize for a in (*args, *out_shapes))
        return pl.pallas_call(
            kernel,
            out_shape=out_shapes,
            in_specs=specs,
            out_specs=[VMEM] * len(out_shapes),
            scratch_shapes=scratch,
            cost_estimate=pl.CostEstimate(flops=flops, bytes_accessed=moved, transcendentals=0),
            compiler_params=pltpu.CompilerParams(vmem_limit_bytes=16 * 2**20),
        )(*args)

    return run


def local(a_panels, b_panels, a_pattern, c_pattern):
    rows, _, sections, _ = a_panels.shape
    depth, columns = b_panels.shape[2:]
    n_row, n_col, fibers = (lax.axis_size(name) for name in ("row", "col", "fiber"))
    local_rows = rows * n_col
    share = local_rows // fibers
    if (n_row, n_col, fibers, sections, rows, columns) != (8, 2, 2, 2, 3 * UNIT, 1024):
        return gathered(a_panels, b_panels, a_pattern, c_pattern)

    f32, bf16 = jnp.float32, jnp.bfloat16
    shape = jax.ShapeDtypeStruct
    half = columns // 2
    cut = half - LAST
    my_y = lax.axis_index("row") & 1
    swap = [(0, 1), (1, 0)]
    swap_y = [(r, r ^ 1) for r in range(n_row)]

    def columns_half(side):
        where = (0, 0, 0, side * half)
        sizes = (*b_panels.shape[:3], half)
        return lax.dynamic_slice(b_panels, where, sizes, allow_negative_indices=False)

    own = columns_half(my_y)
    b_panels, own = together(b_panels, own)
    shards = {(0, 0): own}
    shards[0, 1] = lax.ppermute(columns_half(1 - my_y), "row", swap_y)
    for turn in range(2):
        shards[1, turn] = lax.ppermute(shards[0, turn], "row", z_pairs(1))
        shards[2, turn] = lax.ppermute(shards[0, turn], "row", z_pairs(2))
    shards[3, 0] = lax.ppermute(shards[2, 0], "row", z_pairs(1))
    far_early = lax.ppermute(shards[2, 1][..., :cut], "row", z_pairs(1))
    far_last = lax.ppermute(shards[2, 1][..., cut:], "row", z_pairs(1))

    from_x = lax.ppermute(a_panels, "col", swap)
    y0, y1, y2 = (
        lax.ppermute(a_panels[u * UNIT : (u + 1) * UNIT], "row", swap_y) for u in range(3)
    )
    d2 = lax.ppermute(from_x[2 * UNIT :], "row", swap_y)
    d0 = lax.ppermute(y0, "col", swap)
    d1 = lax.ppermute(y1, "col", swap)
    a_tables = [a_pattern, lax.ppermute(a_pattern, "row", swap_y)]
    c_tables = [c_pattern, lax.ppermute(c_pattern, "row", swap_y)]

    groups = [[(0, 0), (0, 1), (1, 0), (2, 0)], [(1, 1), (2, 1)], [(3, 0)], [(3, 1)]]
    shard_depth = sections * depth

    def left(*sources):
        arrays = [source for source, *_ in sources]
        plan = tuple((y, x, first) for _, y, x, first in sources)
        count = sum(source.shape[0] for source in arrays)
        parts = [shape((count, len(m) * shard_depth), bf16) for m in groups for _ in range(2)]
        return call(
            functools.partial(left_kernel, groups, plan),
            parts,
            [SMEM] * 2 + [VMEM] * len(arrays),
            [pltpu.VMEM((n_row, sections, UNIT, depth), f32)],
        )(a_pattern, a_tables[max(y for y, *_ in plan)], *arrays)

    early_sets = [
        left((a_panels, 0, False, 0)),
        left((from_x, 0, True, 0)),
        left((y0, 1, False, 0)),
        left((y1, 1, False, UNIT)),
    ]

    def picked(sets, g):
        return [s[2 * g] for s in sets] + [s[2 * g + 1] for s in sets]

    rights = []
    for g in range(2):
        members = [shards[m] for m in groups[g]]
        rights += call(
            split_kernel,
            [shape((len(members) * shard_depth, half), bf16)] * 2,
            [VMEM] * len(members),
        )(*members)

    def product(sets):
        lefts = [part for g in range(2) for part in picked(sets, g)]
        count = sum(s[0].shape[0] for s in sets)
        (total,) = call(
            functools.partial(group_kernel, len(sets), 2),
            [shape((count, half), f32)],
            [VMEM] * (len(lefts) + len(rights)),
            flops=6 * count * half * 6 * shard_depth,
        )(*lefts, *rights)
        return total

    early_sets.append(left((y2, 1, False, 2 * UNIT), (d0, 1, True, 0)))
    near = product(early_sets)
    d2, d1, near = together(d2, d1, near)
    late_sets = [left((d1, 1, True, UNIT), (d2, 1, True, 2 * UNIT))]
    near_late = product(late_sets)

    all_sets = [*early_sets, *late_sets]
    hop_lefts = picked(all_sets, 2)
    factor = pltpu.VMEM((shard_depth, half), bf16)
    (near,) = call(
        functools.partial(hop_kernel, len(all_sets)),
        [shape((4 * rows, half), f32)],
        [VMEM] * (len(hop_lefts) + 3),
        [factor, factor],
        6 * 4 * rows * half * shard_depth,
    )(*hop_lefts, near, near_late, shards[3, 0])

    far_lefts = picked(all_sets, 3)

    def far(kernel, first, shard, outs):
        factor = pltpu.VMEM((shard_depth, shard.shape[3]), bf16)
        return call(
            functools.partial(kernel, first),
            outs,
            [VMEM] * (len(far_lefts) + 2),
            [factor, factor],
            6 * 4 * rows * shard.shape[3] * shard_depth,
        )(*far_lefts, near, shard)

    kept, sent = far(far_kernel, 0, far_early, [shape((2, rows, cut), f32)] * 2)
    received = lax.ppermute(sent, "fiber", swap)
    (mine,) = far(last_kernel, cut, far_last, [shape((4, rows, LAST), f32)])
    theirs = lax.ppermute(mine, "fiber", swap)
    stays, goes, sums = call(
        square_kernel,
        [shape((rows, cut), f32)] * 2 + [shape((1, cut), f32)],
        [SMEM, SMEM, VMEM, VMEM],
    )(*c_tables, kept, received)
    comes = lax.ppermute(goes, "row", swap_y)
    sums = sums + lax.ppermute(sums, "fiber", swap)
    last_stays, last_goes, sums = call(
        functools.partial(square_last_kernel, cut),
        [shape((rows, LAST), f32)] * 2 + [shape((1, half), f32)],
        [SMEM, SMEM, VMEM, VMEM, VMEM],
    )(*c_tables, mine, theirs, sums)
    last_comes = lax.ppermute(last_goes, "row", swap_y)
    for bit in (2, 4):
        sums = sums + lax.ppermute(sums, "row", [(r, r ^ bit) for r in range(n_row)])
    other_sums = lax.ppermute(sums, "row", swap_y)
    (out,) = call(
        functools.partial(scale_kernel, share * fibers * n_row),
        [shape((share, columns), f32)],
        [VMEM] * 6,
    )(sums, other_sums, stays, last_stays, comes, last_comes)
    return out


def solution(mesh):
    placed = (
        P(("row", "col"), "fiber", None, None),
        P("fiber", None, "row", "col"),
        P("row", "fiber", None, None),
        P("row", "col"),
    )

    return jax.shard_map(
        local, mesh=mesh, in_specs=placed, out_specs=P(("row", "fiber"), "col"), check_vma=False
    )
```

```python
import functools

import jax
import jax.numpy as jnp
from jax import lax
from jax.experimental import pallas as pl
from jax.experimental.pallas import tpu as pltpu
from jax.sharding import PartitionSpec as P


BLK = 128


EPS = 1e-06
LAST = 128
UNIT = 64


def z_pairs(bits):
    return [(row, row ^ (2 * bits)) for row in range(8)]


def all_sum(value, axis_name):
    size = lax.axis_size(axis_name)
    stride = 1
    while stride < size:
        rest = size // stride
        radix = next(p for p in range(2, rest + 1) if rest % p == 0)
        total = value
        for turn in range(1, radix):
            pairs = []
            for i in range(size):
                digit = i // stride % radix
                pairs.append((i, i + ((digit + turn) % radix - digit) * stride))
            total = total + lax.ppermute(value, axis_name, pairs)
        value = total
        stride *= radix
    return value


def gathered(a_panels, b_panels, a_pattern, c_pattern):
    _, _, sections, width = a_panels.shape
    block_rows, width_blocks = a_pattern.shape[0], a_pattern.shape[3]
    columns = b_panels.shape[3]
    local_rows = block_rows * BLK
    n_row, fibers = lax.axis_size("row"), lax.axis_size("fiber")
    share = local_rows // fibers
    total = jnp.zeros((local_rows, columns), jnp.float32)
    for section in range(sections):
        block = lax.all_gather(a_panels[:, 0, section, :], "col", axis=0, tiled=True)
        keep = a_pattern[:, 0, section, :].astype(jnp.float32)
        left = block.reshape(block_rows, BLK, width_blocks, BLK) * keep[:, None, :, None]
        right = lax.all_gather(b_panels[0, section], "row", axis=0, tiled=True)
        total = total + jnp.dot(
            left.reshape(local_rows, width),
            right,
            precision=lax.Precision.HIGH,
            preferred_element_type=jnp.float32,
        )
    keep = jnp.broadcast_to(
        c_pattern.astype(jnp.float32)[:, None, :, None],
        (block_rows, BLK, columns // BLK, BLK),
    ).reshape(local_rows, columns)
    merged = lax.psum_scatter(total, "fiber", scatter_dimension=0, tiled=True)
    product = merged * lax.dynamic_slice_in_dim(keep, lax.axis_index("fiber") * share, share, 0)
    inflated = product * product
    sums = all_sum(all_sum(jnp.sum(inflated, axis=0, keepdims=True), "fiber"), "row")
    return inflated / (sums / (share * fibers * n_row) + EPS)


def split(value):
    high = value.astype(jnp.bfloat16)
    low = (value - high.astype(jnp.float32)).astype(jnp.bfloat16)
    return high, low


def product3(a_high, a_low, b_high, b_low):
    def dot(x, y):
        return jnp.dot(x, y, preferred_element_type=jnp.float32)

    return dot(a_high, b_high) + (dot(a_high, b_low) + dot(a_low, b_high))


def left_kernel(groups, plan, pattern, other_pattern, *refs):
    sources, outs, turned = refs[: len(plan)], refs[len(plan) : -1], refs[-1]
    _, _, sections, width = sources[0].shape
    n_row, row, col = lax.axis_size("row"), lax.axis_index("row"), lax.axis_index("col")
    depth = width // n_row
    done = 0
    for source, (which, is_peer, first) in zip(sources, plan, strict=True):
        position = 1 - col if is_peer else col
        for g in range(source.shape[0] // UNIT):
            part = pl.ds(g * UNIT, UNIT)
            block_row = (position * (3 * UNIT) + first + g * UNIT) // BLK
            for s in range(sections):
                kept = []
                for w in range(width // BLK):
                    keep = (pattern, other_pattern)[which][block_row, 0, s, w]
                    kept.append(jnp.where(keep != 0, source[part, 0, s, pl.ds(w * BLK, BLK)], 0.0))
                value = jnp.concatenate(kept, axis=1)
                for r in range(n_row):
                    turned[r, s] = value[:, r * depth : (r + 1) * depth]
            place = pl.ds(done, UNIT)
            for i, members in enumerate(groups):
                owners = [row ^ (2 * bits + turn) for bits, turn in members]
                pieces = [turned[r, s] for r in owners for s in range(sections)]
                high, low = split(jnp.concatenate(pieces, axis=1))
                outs[2 * i][place, :] = high
                outs[2 * i + 1][place, :] = low
            done += UNIT


def put_shards(shards, b_high, b_low):
    _, sections, depth, _ = shards[0].shape
    for i in range(len(shards) * sections):
        part = pl.ds(i * depth, depth)
        b_high[part, :], b_low[part, :] = split(shards[i // sections][0, i % sections])


def stacked(refs):
    return jnp.concatenate([ref[...] for ref in refs], axis=0)


def split_kernel(*refs):
    *shards, high, low = refs
    put_shards(shards, high, low)


def group_kernel(sets, groups, *refs):
    lefts, rights, out = refs[: 2 * sets * groups], refs[2 * sets * groups : -1], refs[-1]
    total = None
    for i in range(groups):
        group = lefts[2 * sets * i : 2 * sets * (i + 1)]
        right = rights[2 * i : 2 * i + 2]
        value = product3(stacked(group[:sets]), stacked(group[sets:]), right[0][...], right[1][...])
        total = value if total is None else total + value
    out[...] = total


def hop_kernel(sets, *refs):
    lefts, (*nears, shard, out, b_high, b_low) = refs[: 2 * sets], refs[2 * sets :]
    put_shards([shard], b_high, b_low)
    value = product3(stacked(lefts[:sets]), stacked(lefts[sets:]), b_high[...], b_low[...])
    out[...] = value + stacked(nears)


def far_value(first, *refs):
    *lefts, near, shard, b_high, b_low = refs
    highs, lows = lefts[: len(lefts) // 2], lefts[len(lefts) // 2 :]
    put_shards([shard], b_high, b_low)
    value = product3(stacked(highs), stacked(lows), b_high[...], b_low[...])
    return value + near[:, first : first + shard.shape[3]]


def far_kernel(first, *refs):
    *ins, kept, sent, b_high, b_low = refs
    value = far_value(first, *ins, b_high, b_low)
    rows = kept.shape[1]
    flip = lax.axis_index("col") ^ lax.axis_index("fiber")
    for turn in range(2):

        @pl.when(flip == turn)
        def _():
            for p in range(4):
                y, x = divmod(p, 2)
                out = kept if x == turn else sent
                out[y] = value[p * rows : (p + 1) * rows]


def last_kernel(first, *refs):
    *ins, out, b_high, b_low = refs
    value = far_value(first, *ins, b_high, b_low)
    rows = out.shape[1]
    for p in range(4):
        out[p] = value[p * rows : (p + 1) * rows]


def squared(pattern, fiber, first, value):
    columns = value.shape[1]
    half = lax.axis_index("row") % 2 * (pattern.shape[1] // 2)
    out = []
    for g in range(value.shape[0] // UNIT):
        block_row = (fiber * value.shape[0] + g * UNIT) // BLK
        kept = []
        for w in range(columns // BLK):
            keep = pattern[block_row, half + first // BLK + w]
            piece = value[g * UNIT : (g + 1) * UNIT, w * BLK : (w + 1) * BLK]
            piece = jnp.where(keep != 0, piece, 0.0)
            kept.append(piece * piece)
        out.append(jnp.concatenate(kept, axis=1) if len(kept) > 1 else kept[0])
    return jnp.concatenate(out, axis=0)


def square_kernel(pattern, other_pattern, kept, received, stays, goes, sums):
    fiber = lax.axis_index("fiber")
    mine = squared(pattern, fiber, 0, kept[0] + received[0])
    other = squared(other_pattern, fiber, 0, kept[1] + received[1])
    stays[...], goes[...] = mine, other
    sums[...] = jnp.sum(mine, axis=0, keepdims=True) + jnp.sum(other, axis=0, keepdims=True)


def square_last_kernel(first, pattern, other_pattern, mine, received, early, stays, goes, sums):
    fiber, col = lax.axis_index("fiber"), lax.axis_index("col")
    total = None
    for y, (table, target) in enumerate(((pattern, stays), (other_pattern, goes))):
        for block in (1 - fiber, fiber):
            p = 2 * y + (block ^ col)
            value = squared(table, block, first, mine[p] + received[p])
            part = jnp.sum(value, axis=0, keepdims=True)
            total = part if total is None else total + part
        target[...] = value
    sums[:, :first] = early[...]
    sums[:, first:] = total


def scaled(row_total, sums, early, last):
    factor = 1.0 / (sums[...] / row_total + EPS)
    cut = early.shape[1]
    return early[...] * factor[:, :cut], last[...] * factor[:, cut:]


def scale_own_kernel(row_total, sums, early, last, out):
    cut = early.shape[1]
    out[:, :cut], out[:, cut:] = scaled(row_total, sums, early, last)


def scale_kernel(row_total, sums, early, last, own, out):
    half, cut = own.shape[1], early.shape[1]
    y = lax.axis_index("row") % 2
    first = (1 - y) * half
    out[:, pl.ds(pl.multiple_of(y * half, BLK), half)] = own[...]
    left, right = scaled(row_total, sums, early, last)
    out[:, pl.ds(pl.multiple_of(first, BLK), cut)] = left
    out[:, pl.ds(pl.multiple_of(first + cut, BLK), half - cut)] = right


def together(*values):
    return lax.optimization_barrier(values)


VMEM = pl.BlockSpec(memory_space=pltpu.VMEM)
SMEM = pl.BlockSpec(memory_space=pltpu.SMEM)


def call(kernel, out_shapes, specs, scratch=(), flops=0):
    def run(*args):
        moved = sum(a.size * a.dtype.itemsize for a in (*args, *out_shapes))
        return pl.pallas_call(
            kernel,
            out_shape=out_shapes,
            in_specs=specs,
            out_specs=[VMEM] * len(out_shapes),
            scratch_shapes=scratch,
            cost_estimate=pl.CostEstimate(flops=flops, bytes_accessed=moved, transcendentals=0),
            compiler_params=pltpu.CompilerParams(vmem_limit_bytes=16 * 2**20),
        )(*args)

    return run


def local(a_panels, b_panels, a_pattern, c_pattern):
    rows, _, sections, _ = a_panels.shape
    depth, columns = b_panels.shape[2:]
    n_row, n_col, fibers = (lax.axis_size(name) for name in ("row", "col", "fiber"))
    local_rows = rows * n_col
    share = local_rows // fibers
    if (n_row, n_col, fibers, sections, rows, columns) != (8, 2, 2, 2, 3 * UNIT, 1024):
        return gathered(a_panels, b_panels, a_pattern, c_pattern)

    f32, bf16 = jnp.float32, jnp.bfloat16
    shape = jax.ShapeDtypeStruct
    half = columns // 2
    cut = half - LAST
    my_y = lax.axis_index("row") & 1
    swap = [(0, 1), (1, 0)]
    swap_y = [(r, r ^ 1) for r in range(n_row)]

    def columns_half(side):
        where = (0, 0, 0, side * half)
        sizes = (*b_panels.shape[:3], half)
        return lax.dynamic_slice(b_panels, where, sizes, allow_negative_indices=False)

    own = columns_half(my_y)
    b_panels, own = together(b_panels, own)
    shards = {(0, 0): own}
    shards[0, 1] = lax.ppermute(columns_half(1 - my_y), "row", swap_y)
    for turn in range(2):
        shards[1, turn] = lax.ppermute(shards[0, turn], "row", z_pairs(1))
        shards[2, turn] = lax.ppermute(shards[0, turn], "row", z_pairs(2))
    shards[3, 0] = lax.ppermute(shards[2, 0], "row", z_pairs(1))
    far_early = lax.ppermute(shards[2, 1][..., :cut], "row", z_pairs(1))
    far_last = lax.ppermute(shards[2, 1][..., cut:], "row", z_pairs(1))

    from_x = lax.ppermute(a_panels, "col", swap)
    y0, y1, y2 = (
        lax.ppermute(a_panels[u * UNIT : (u + 1) * UNIT], "row", swap_y) for u in range(3)
    )
    d2 = lax.ppermute(from_x[2 * UNIT :], "row", swap_y)
    d0 = lax.ppermute(y0, "col", swap)
    d1 = lax.ppermute(y1, "col", swap)
    a_tables = [a_pattern, lax.ppermute(a_pattern, "row", swap_y)]
    c_tables = [c_pattern, lax.ppermute(c_pattern, "row", swap_y)]

    groups = [[(0, 0), (0, 1), (1, 0), (2, 0)], [(1, 1), (2, 1)], [(3, 0)], [(3, 1)]]
    shard_depth = sections * depth

    def left(*sources):
        arrays = [source for source, *_ in sources]
        plan = tuple((y, x, first) for _, y, x, first in sources)
        count = sum(source.shape[0] for source in arrays)
        parts = [shape((count, len(m) * shard_depth), bf16) for m in groups for _ in range(2)]
        return call(
            functools.partial(left_kernel, groups, plan),
            parts,
            [SMEM] * 2 + [VMEM] * len(arrays),
            [pltpu.VMEM((n_row, sections, UNIT, depth), f32)],
        )(a_pattern, a_tables[max(y for y, *_ in plan)], *arrays)

    early_sets = [
        left((a_panels, 0, False, 0)),
        left((from_x, 0, True, 0)),
        left((y0, 1, False, 0)),
        left((y1, 1, False, UNIT)),
    ]

    def picked(sets, g):
        return [s[2 * g] for s in sets] + [s[2 * g + 1] for s in sets]

    rights = []
    for g in range(2):
        members = [shards[m] for m in groups[g]]
        rights += call(
            split_kernel,
            [shape((len(members) * shard_depth, half), bf16)] * 2,
            [VMEM] * len(members),
        )(*members)

    def product(sets):
        lefts = [part for g in range(2) for part in picked(sets, g)]
        count = sum(s[0].shape[0] for s in sets)
        (total,) = call(
            functools.partial(group_kernel, len(sets), 2),
            [shape((count, half), f32)],
            [VMEM] * (len(lefts) + len(rights)),
            flops=6 * count * half * 6 * shard_depth,
        )(*lefts, *rights)
        return total

    early_sets.append(left((y2, 1, False, 2 * UNIT), (d0, 1, True, 0)))
    near = product(early_sets)
    d2, d1, near = together(d2, d1, near)
    late_sets = [left((d1, 1, True, UNIT), (d2, 1, True, 2 * UNIT))]
    near_late = product(late_sets)

    all_sets = [*early_sets, *late_sets]
    hop_lefts = picked(all_sets, 2)
    factor = pltpu.VMEM((shard_depth, half), bf16)
    (near,) = call(
        functools.partial(hop_kernel, len(all_sets)),
        [shape((4 * rows, half), f32)],
        [VMEM] * (len(hop_lefts) + 3),
        [factor, factor],
        6 * 4 * rows * half * shard_depth,
    )(*hop_lefts, near, near_late, shards[3, 0])

    far_lefts = picked(all_sets, 3)

    def far(kernel, first, shard, outs):
        factor = pltpu.VMEM((shard_depth, shard.shape[3]), bf16)
        return call(
            functools.partial(kernel, first),
            outs,
            [VMEM] * (len(far_lefts) + 2),
            [factor, factor],
            6 * 4 * rows * shard.shape[3] * shard_depth,
        )(*far_lefts, near, shard)

    kept, sent = far(far_kernel, 0, far_early, [shape((2, rows, cut), f32)] * 2)
    received = lax.ppermute(sent, "fiber", swap)
    (mine,) = far(last_kernel, cut, far_last, [shape((4, rows, LAST), f32)])
    theirs = lax.ppermute(mine, "fiber", swap)
    stays, goes, sums = call(
        square_kernel,
        [shape((rows, cut), f32)] * 2 + [shape((1, cut), f32)],
        [SMEM, SMEM, VMEM, VMEM],
    )(*c_tables, kept, received)
    comes = lax.ppermute(goes, "row", swap_y)
    sums = sums + lax.ppermute(sums, "fiber", swap)
    last_stays, last_goes, sums = call(
        functools.partial(square_last_kernel, cut),
        [shape((rows, LAST), f32)] * 2 + [shape((1, half), f32)],
        [SMEM, SMEM, VMEM, VMEM, VMEM],
    )(*c_tables, mine, theirs, sums)
    last_comes = lax.ppermute(last_goes, "row", swap_y)
    for bit in (2, 4):
        sums = sums + lax.ppermute(sums, "row", [(r, r ^ bit) for r in range(n_row)])
    other_sums = lax.ppermute(sums, "row", swap_y)
    row_total = share * fibers * n_row
    (own_scaled,) = call(
        functools.partial(scale_own_kernel, row_total), [shape((share, half), f32)], [VMEM] * 3
    )(sums, stays, last_stays)
    (out,) = call(
        functools.partial(scale_kernel, row_total), [shape((share, columns), f32)], [VMEM] * 4
    )(other_sums, comes, last_comes, own_scaled)
    return out


def solution(mesh):
    placed = (
        P(("row", "col"), "fiber", None, None),
        P("fiber", None, "row", "col"),
        P("row", "fiber", None, None),
        P("row", "col"),
    )

    return jax.shard_map(
        local, mesh=mesh, in_specs=placed, out_specs=P(("row", "fiber"), "col"), check_vma=False
    )
```
